32 devices in a mesh: batch: 8 (over z, y), head: 4 (over x, core).
Axes of the slice: x: 2, y: 2, z: 4, core: 2. Of those that a mesh axis runs over, the one named last changes fastest.
Arguments:
- inputs: bfloat16 [16384, 768], P(('batch', 'head')), may hold values from -6 to 6
- lengths: int32 [8, 8], P('batch'), may hold values from 1 to 1024, 2048 in all within a row
- cotangent: bfloat16 [16384, 768], P(('batch', 'head')), may hold values from -6 to 6
- gain_attn: float32 [768], replicated, may hold values from 0.1 to 1.9
- shift_attn: float32 [768], replicated, may hold values from -2 to 2
- weight_qkv: bfloat16 [768, 12, 192], P(None, 'head'), may hold values from -0.21875 to 0.21875
- bias_qkv: float32 [12, 192], P('head'), may hold values from -3 to 3
- weight_proj: bfloat16 [12, 64, 768], P('head'), may hold values from -1.75 to 1.75
- bias_proj: float32 [768], replicated, may hold values from -2 to 2
- gain_mlp: float32 [768], replicated, may hold values from 0.1 to 1.9
- shift_mlp: float32 [768], replicated, may hold values from -2 to 2
- weight_up: bfloat16 [768, 3072], P(None, 'head'), may hold values from -0.21875 to 0.21875
- bias_up: float32 [3072], P('head'), may hold values from -2 to 2
- weight_down: bfloat16 [3072, 768], P('head'), may hold values from -0.109375 to 0.109375
- bias_down: float32 [768], replicated, may hold values from -2 to 2
Outputs:
- output: bfloat16 [16384, 768], P(('batch', 'head'))
- grad_inputs: bfloat16 [16384, 768], P(('batch', 'head'))
- grad_gain_attn: float32 [768], replicated
- grad_shift_attn: float32 [768], replicated
- grad_weight_qkv: float32 [768, 12, 192], P(None, 'head')
- grad_bias_qkv: float32 [12, 192], P('head')
- grad_weight_proj: float32 [12, 64, 768], P('head')
- grad_bias_proj: float32 [768], replicated
- grad_gain_mlp: float32 [768], replicated
- grad_shift_mlp: float32 [768], replicated
- grad_weight_up: float32 [768, 3072], P(None, 'head')
- grad_bias_up: float32 [3072], P('head')
- grad_weight_down: float32 [3072, 768], P('head')
- grad_bias_down: float32 [768], replicated
The draws below stay inside these ranges and needn't reach their ends.
Inputs may be any that keep to these rules, and one draw needn't show every extreme that they name: `lengths`: in each row the 8 entries sum to 2048; the last one counts the pad rows at the group's end; the largest entry of every row is exactly 1024.
All inputs are finite; a program needn't handle non-finite values.
Results may differ from the reference program's by a relative error of at most 0.013.
The reference program's roundings to bfloat16 on the way count: a program that leaves them out, or rounds other values in their place, can miss the bound.
Values may be sent and summed in bfloat16 or wider, within the bound.
No kernel may reach another device: no remote copies, remote signals or barrier semaphores. Data moves between devices by JAX's collectives and lax.ppermute only.
A program may use at most 192 MiB of HBM per device.

```python
import math
import jax
import jax.numpy as jnp
import numpy as np
from jax import lax

D = 768
H = 12
HD = 64
FF = 3072
TOK_DEV = 2048
SEQS = 7
MAXLEN = 1024
GROUPS = 8
TOKENS = 16384


def block_levels(own_key, shape, split, smallest, high):
    level, own = 1.0, jax.random.fold_in(own_key, 6)
    for position, parts in split:
        draws = jnp.exp(jax.random.uniform(jax.random.fold_in(own, position), (parts,), jnp.float32, smallest / len(split), high / len(split)))
        level = level * jnp.repeat(draws, shape[position] // parts).reshape([-1 if axis == position else 1 for axis in range(len(shape))])
    return level


def profile(amount, total, most, skew):
    weights = [(1 << 20) // math.isqrt(grade ** skew) + 1 for grade in range(2, amount + 1)]
    rest, holding = total - most - (amount - 1), [1] * (amount - 1)
    while rest > 0:
        candidates = [i for i in range(amount - 1) if holding[i] < most]
        whole, left = sum([weights[i] for i in candidates]), rest
        for i in candidates:
            addition = min(most - holding[i], max(1, left * weights[i] // whole), rest)
            holding[i] = holding[i] + addition
            rest = rest - addition
    return np.array([most] + holding)


def ragged(key, amount, total, limit, slope):
    if amount == 2:
        one = jax.random.randint(key, (), max(1, total - limit), min(limit, total - 1) + 1)
        return jnp.stack([one, total - one])
    sizes = jnp.asarray(profile(amount, total, limit, slope), jnp.int32)
    pairs = (amount - 1) // 2
    donor, taker = sizes[1:1 + 2 * pairs:2], sizes[2:2 + 2 * pairs:2]
    slack = jnp.minimum(donor - 1, limit - taker)
    passed = jax.random.randint(jax.random.fold_in(key, 1), (pairs,), 0, 1 << 20) % (slack + 1)
    sizes = sizes.at[1:1 + 2 * pairs:2].set(donor - passed).at[2:2 + 2 * pairs:2].set(taker + passed)
    return sizes[jax.random.permutation(jax.random.fold_in(key, 2), amount)]


def centred(rng, dims, scale, bound, split=(), kind=jnp.bfloat16):
    factor_of = block_levels(rng, dims, split, -0.22, 0.18) if split else 1.0
    values = jax.random.normal(rng, dims, jnp.float32) * scale * factor_of
    return jnp.minimum(jnp.maximum(values, -bound), bound).astype(kind)


def setup_inputs(seed: int = 0) -> dict:
    streams_of = jax.random.split(jax.random.key(seed), 16)
    return {
        "inputs": centred(streams_of[0], (TOKENS, D), 1.0, 6.0, ((0, 32),)),
        "lengths": jax.vmap(lambda own: ragged(own, SEQS + 1, TOK_DEV, MAXLEN, 2))(jax.random.split(streams_of[1], GROUPS)).reshape((GROUPS, SEQS + 1)).astype(jnp.int32),
        "cotangent": centred(streams_of[2], (TOKENS, D), 1.0, 6.0, ((0, 32),)),
        "gain_attn": jnp.clip(1.0 + 0.18 * jax.random.normal(streams_of[3], (D,), jnp.float32), 0.1, 1.9),
        "shift_attn": centred(streams_of[4], (D,), 0.3, 2.0, (), jnp.float32),
        "weight_qkv": centred(streams_of[5], (D, H, 3 * HD), D ** -0.5, 0.21875, ((1, 4),)),
        "bias_qkv": centred(streams_of[6], (H, 3 * HD), 0.5, 3.0, ((0, 4),), jnp.float32),
        "weight_proj": centred(streams_of[7], (H, HD, D), (max(4, D // 64)) ** -0.5, 1.75, ((0, 4),)),
        "bias_proj": centred(streams_of[8], (D,), 0.3, 2.0, (), jnp.float32),
        "gain_mlp": jnp.clip(1.0 + 0.18 * jax.random.normal(streams_of[9], (D,), jnp.float32), 0.1, 1.9),
        "shift_mlp": centred(streams_of[10], (D,), 0.3, 2.0, (), jnp.float32),
        "weight_up": centred(streams_of[11], (D, FF), D ** -0.5, 0.21875, ((1, 4),)),
        "bias_up": centred(streams_of[12], (FF,), 0.3, 2.0, ((0, 4),), jnp.float32),
        "weight_down": centred(streams_of[13], (FF, D), FF ** -0.5, 0.109375, ((0, 4),)),
        "bias_down": centred(streams_of[14], (D,), 0.3, 2.0, (), jnp.float32),
    }


epsilon = 1e-05
floor_value = -1e+30
highest = lax.Precision.HIGHEST

@jax.custom_vjp
def low(v):
    return lax.optimization_barrier(v.astype(jnp.bfloat16)).astype(jnp.float32)

@jax.custom_vjp
def low_back(v):
    return v

def low_keep(v):
    return (low(v), None)

def low_pass(kept, grad):
    return (grad,)

def back_keep(v):
    return (v, None)

def back_low(kept, grad):
    return (low(grad),)
low.defvjp(low_keep, low_pass)
low_back.defvjp(back_keep, back_low)

def layer_norm(value, gain, shift):
    center = value - lax.optimization_barrier(jnp.mean(value, axis=-1, keepdims=True))
    spread = lax.optimization_barrier(jnp.mean(center * center, axis=-1, keepdims=True))
    return center * lax.rsqrt(spread + epsilon) * gain + shift

def segment_ids(row, count):
    ends = jnp.cumsum(row).astype(jnp.int32)
    places = jnp.arange(count, dtype=jnp.int32)
    return lax.optimization_barrier(jnp.sum((places[:, None] >= ends[None, :]).astype(jnp.int32), axis=1)).astype(jnp.int32)

def head_attention(queries, key_rows, values, allowed):
    scores = low_back(jnp.dot(queries, key_rows.T, precision=highest) * (1.0 / math.sqrt(HD)))
    magnitude = jnp.where(allowed, jnp.abs(scores), floor_value)
    row_top = lax.optimization_barrier(jnp.max(magnitude, axis=1, keepdims=True))
    exponent = jnp.where(allowed, jnp.exp(magnitude - row_top), 0.0)
    offset = jnp.where(allowed, jnp.exp(-row_top), 0.0)
    total = lax.optimization_barrier(jnp.sum(exponent, axis=1, keepdims=True))
    weights = low(jnp.sign(scores) * ((exponent - offset) / total))
    return jnp.dot(weights, values, precision=highest)

def group_forward(params, tokens, allowed):
    gain_attn, shift_attn, weight_qkv, bias_qkv, weight_proj, bias_proj, gain_mlp, shift_mlp, weight_up, bias_up, weight_down, bias_down = params
    h_one = low(layer_norm(tokens, gain_attn, shift_attn))
    pre_qkv = low_back(jnp.dot(h_one, weight_qkv.reshape(D, H * 3 * HD), precision=highest) + bias_qkv.reshape(H * 3 * HD))
    packed = low(pre_qkv).reshape(TOK_DEV, H, 3, HD)
    queries = jnp.transpose(packed[:, :, 0], (1, 0, 2))
    key_rows = jnp.transpose(packed[:, :, 1], (1, 0, 2))
    values = jnp.transpose(packed[:, :, 2], (1, 0, 2))
    one_head = jax.checkpoint(lambda triple: head_attention(triple[0], triple[1], triple[2], allowed))
    heads = lax.map(one_head, (queries, key_rows, values))
    merged = low(low_back(jnp.transpose(heads, (1, 0, 2)).reshape(TOK_DEV, H * HD)))
    attended = low_back(jnp.dot(merged, weight_proj.reshape(H * HD, D), precision=highest))
    resid = tokens + attended + bias_proj
    h_two = low(layer_norm(resid, gain_mlp, shift_mlp))
    pre_up = low_back(jnp.dot(h_two, weight_up, precision=highest) + bias_up)
    hidden_act = low(jax.nn.gelu(pre_up, approximate=True))
    down = low_back(jnp.dot(hidden_act, weight_down, precision=highest))
    return resid + down + bias_down

def reference(inputs, lengths, cotangent, gain_attn, shift_attn, weight_qkv, bias_qkv, weight_proj, bias_proj, gain_mlp, shift_mlp, weight_up, bias_up, weight_down, bias_down):
    params = tuple((item.astype(jnp.float32) for item in (gain_attn, shift_attn, weight_qkv, bias_qkv, weight_proj, bias_proj, gain_mlp, shift_mlp, weight_up, bias_up, weight_down, bias_down)))
    token_groups = inputs.astype(jnp.float32).reshape(GROUPS, TOK_DEV, D)
    grad_groups = cotangent.astype(jnp.float32).reshape(GROUPS, TOK_DEV, D)

    def group_step(totals, item):
        tokens, grad_rows, length_row = item
        segment = segment_ids(length_row, TOK_DEV)
        places = jnp.arange(TOK_DEV, dtype=jnp.int32)
        allowed = (segment[:, None] == segment[None, :]) & (places[None, :] <= places[:, None]) & ((segment[:, None] < SEQS) | (places[None, :] == places[:, None]))
        live = (segment < SEQS).astype(jnp.float32)[:, None]
        result, pull = jax.vjp(lambda weights, rows: group_forward(weights, rows, allowed), params, tokens)
        grad_params, grad_tokens = pull(grad_rows * live)
        totals = jax.tree.map(jnp.add, totals, grad_params)
        return (totals, (result.astype(jnp.bfloat16), grad_tokens.astype(jnp.bfloat16)))
    zeros = jax.tree.map(jnp.zeros_like, params)
    totals, (results, grad_tokens) = lax.scan(group_step, zeros, (token_groups, grad_groups, lengths))
    return (results.reshape(TOKENS, D), grad_tokens.reshape(TOKENS, D), totals[0], totals[1], totals[2], totals[3], totals[4], totals[5], totals[6], totals[7], totals[8], totals[9], totals[10], totals[11])
```

```python
import functools
import math

import jax
import jax.numpy as jnp
from jax import lax
from jax.experimental import pallas as pl
from jax.experimental.pallas import tpu as pltpu
from jax.sharding import PartitionSpec as P

F32 = jnp.float32
BF = jnp.bfloat16
BLK = 256
NEG = -1e30
EPS = 1e-05
GELU_C = math.sqrt(2.0 / math.pi)
GELU_A = 0.044715


def dot_nn(a, b):
    return lax.dot_general(a, b, (((1,), (0,)), ((), ())), preferred_element_type=F32)


def dot_nt(a, b):
    return lax.dot_general(a, b, (((1,), (1,)), ((), ())), preferred_element_type=F32)


def dot_tn(a, b):
    return lax.dot_general(a, b, (((0,), (0,)), ((), ())), preferred_element_type=F32)


def cost(flops, nbytes, trans=0):
    return pl.CostEstimate(flops=int(flops), bytes_accessed=int(nbytes), transcendentals=int(trans))


def swap(x, axis, bits):
    size = lax.axis_size(axis)
    return lax.ppermute(x, axis, [(i, i ^ bits) for i in range(size)])


def normalize(v):
    center = v - jnp.mean(v, axis=-1, keepdims=True)
    rstd = lax.rsqrt(jnp.mean(center * center, axis=-1, keepdims=True) + EPS)
    return center * rstd, rstd


def qkv_kernel(heads, hd, steps, h_ref, a_ref, b_ref, v_ref, w_ref, bias_ref, *rest):
    q_out, k_out, v_out, vt_out = rest[-4:]
    t = pl.program_id(0)
    x = jnp.where(t < steps // 2, a_ref[...], b_ref[...]).astype(F32)
    xhat, _ = normalize(x)
    h1 = (xhat * v_ref[0:1, :] + v_ref[1:2, :]).astype(BF)
    bias = jnp.concatenate([bias_ref[h : h + 1, :] for h in range(heads)], axis=1)
    packed = (dot_nt(h1, w_ref[...]) + bias).astype(BF)
    for h in range(heads):
        o = 3 * hd * h
        q_out[h] = packed[:, o : o + hd]
        k_out[h] = packed[:, o + hd : o + 2 * hd]
        v = packed[:, o + 2 * hd : o + 3 * hd]
        v_out[h] = v
        vt_out[h] = v.T


def qkv_call(hid, a, b, vectors, w, bias, first, group_rows, before):
    rows, width = a.shape
    heads, triple = bias.shape
    hd = triple // 3
    per = rows // BLK
    steps = 2 * per
    place = lambda t, h: (h[0] ^ (first + t // per)) * per + t % per
    whole = lambda t, h: (0, 0)
    out_shape = tuple(
        jax.ShapeDtypeStruct(s, BF)
        for s in ((heads, group_rows, hd),) * 3 + ((heads, hd, group_rows),)
    )
    in_specs = [
        pl.BlockSpec((BLK, width), lambda t, h: (jnp.minimum(t, per - 1), 0)),
        pl.BlockSpec((BLK, width), lambda t, h: (jnp.maximum(t - per, 0), 0)),
        pl.BlockSpec(vectors.shape, whole),
        pl.BlockSpec(w.shape, whole),
        pl.BlockSpec(bias.shape, whole),
    ] + [pl.BlockSpec(memory_space=pl.ANY)] * len(before)
    return pl.pallas_call(
        functools.partial(qkv_kernel, heads, hd, steps),
        out_shape=out_shape,
        grid_spec=pltpu.PrefetchScalarGridSpec(
            num_scalar_prefetch=1,
            grid=(steps,),
            in_specs=in_specs,
            out_specs=[pl.BlockSpec((heads, BLK, hd), lambda t, h: (0, place(t, h), 0))] * 3
            + [pl.BlockSpec((heads, hd, BLK), lambda t, h: (0, 0, place(t, h)))],
        ),
        input_output_aliases={6 + i: i for i in range(len(before))},
        cost_estimate=cost(4 * rows * width * w.shape[0], 12 * rows * width),
        name="qkv",
    )(hid, a, b, vectors, w, bias, *before)


def row_segment(len_ref, row):
    low = row
    high = row + 1
    start = jnp.int32(0)
    for k in range(len_ref.shape[0] - 1):
        stop = start + len_ref[k]
        inside = (row >= start) & (row < stop)
        low = jnp.where(inside, start, low)
        high = jnp.where(inside, stop, high)
        start = stop
    return low, high


def lane_starts(len_ref, row, width):
    i = row + lax.broadcasted_iota(jnp.int32, (1, width), 1)
    start = jnp.zeros((1, width), jnp.int32)
    stop = jnp.int32(0)
    for k in range(len_ref.shape[0] - 1):
        stop = stop + len_ref[k]
        start = jnp.where(i >= stop, stop, start)
    return jnp.where(i >= stop, i, start), i


def attend_kernel(heads, first, per, scale, len_ref, h_ref, q_ref, k_ref, vt_ref, o_ref, l_ref, m_s, z_s, acc_s):
    t = pl.program_id(0)
    row = ((h_ref[0] ^ (first + t // per)) * per + t % per) * BLK
    start, i = lane_starts(len_ref, row, BLK)
    low, _ = row_segment(len_ref, row)
    m_s[...] = jnp.full_like(m_s, NEG)
    z_s[...] = jnp.zeros_like(z_s)
    acc_s[...] = jnp.zeros_like(acc_s)
    qs = [q_ref[h] * jnp.asarray(scale, BF) for h in range(heads)]

    def body(jb, carry):
        j0 = pl.multiple_of(jb * BLK, BLK)
        j = j0 + lax.broadcasted_iota(jnp.int32, (BLK, BLK), 0)
        mask = (j >= start) & (j <= i)
        for h in range(heads):
            s = dot_nt(k_ref[h, pl.ds(j0, BLK), :], qs[h])
            magnitude = jnp.where(mask, jnp.abs(s), NEG)
            old = m_s[h : h + 1, :]
            top = jnp.maximum(old, jnp.max(magnitude, axis=0, keepdims=True))
            decay = jnp.exp(old - top)
            e = jnp.exp(magnitude - top)
            z_s[h : h + 1, :] = z_s[h : h + 1, :] * decay + jnp.sum(e, axis=0, keepdims=True)
            m_s[h : h + 1, :] = top
            u = e - jnp.where(mask, jnp.exp(-top), 0.0)
            w = jnp.where(s < 0, -u, u).astype(BF)
            acc_s[h] = acc_s[h] * decay + dot_nn(vt_ref[h, :, pl.ds(j0, BLK)], w)
        return carry

    lax.fori_loop(low // BLK, row // BLK + 1, body, 0)
    outs = []
    for h in range(heads):
        z = z_s[h : h + 1, :]
        outs.append((acc_s[h] / z).T)
        l_ref[h : h + 1, :] = m_s[h : h + 1, :] + jnp.log(z)
    o_ref[...] = jnp.concatenate(outs, axis=1).astype(BF)


def attend_call(lengths, hid, q, k, vt, first, chunk):
    heads, rows, hd = q.shape
    per = chunk // BLK
    steps = 2 * per
    place = lambda t, n, h: (0, (h[0] ^ (first + t // per)) * per + t % per, 0)
    whole = lambda t, n, h: (0, 0, 0)
    return pl.pallas_call(
        functools.partial(attend_kernel, heads, first, per, 1.0 / math.sqrt(hd)),
        out_shape=(
            jax.ShapeDtypeStruct((steps * BLK, heads * hd), BF),
            jax.ShapeDtypeStruct((8, steps * BLK), F32),
        ),
        grid_spec=pltpu.PrefetchScalarGridSpec(
            num_scalar_prefetch=2,
            grid=(steps,),
            in_specs=[
                pl.BlockSpec((heads, BLK, hd), place),
                pl.BlockSpec((heads, rows, hd), whole),
                pl.BlockSpec((heads, hd, rows), whole),
            ],
            out_specs=[
                pl.BlockSpec((BLK, heads * hd), lambda t, n, h: (t, 0)),
                pl.BlockSpec((8, BLK), lambda t, n, h: (0, t)),
            ],
            scratch_shapes=[
                pltpu.VMEM((8, BLK), F32),
                pltpu.VMEM((8, BLK), F32),
                pltpu.VMEM((heads, hd, BLK), F32),
            ],
        ),
        cost_estimate=cost(heads * rows * rows * hd * 4, 12 * rows * heads * hd, heads * rows * rows // 4),
        name="attend",
    )(lengths, hid, q, k, vt)


def attend_back_kernel(chunk, scale, len_ref, h_ref, q_ref, k_ref, v_ref, *rest):
    g_refs, o_refs, l_refs = rest[0:4], rest[4:6], rest[6:8]
    gp_ref, q_s, g_s, kt_s, l_s, c_s, d_s, dq_s, dk_s, dv_s = rest[8:]
    heads, rows, hd = q_ref.shape
    blocks = rows // BLK
    per = chunk // BLK
    own = h_ref[0]
    for c in range(4):
        r0 = pl.multiple_of((own ^ c) * chunk, chunk)
        part = slice((c % 2) * chunk, (c % 2 + 1) * chunk)
        g = g_refs[c][part, :]
        o = o_refs[c // 2][part, :]
        for h in range(heads):
            gh = g[:, h * hd : (h + 1) * hd]
            g_s[h, pl.ds(r0, chunk), :] = gh
            both = gh.astype(F32) * o[:, h * hd : (h + 1) * hd].astype(F32)
            d_s[h : h + 1, pl.ds(r0, chunk)] = jnp.sum(both.T, axis=0, keepdims=True)
        level = l_refs[c // 2][:, part]
        l_s[:, pl.ds(r0, chunk)] = level
        c_s[:, pl.ds(r0, chunk)] = jnp.exp(-level)
    for h in range(heads):
        q_s[h] = q_ref[h] * jnp.asarray(scale, BF)
    dq_s[...] = jnp.zeros_like(dq_s)

    def out_row(block):
        return pl.multiple_of(((own ^ (block // per)) * per + block % per) * BLK, BLK)

    def outer(jb, carry):
        j0 = pl.multiple_of(jb * BLK, BLK)
        dk_s[...] = jnp.zeros_like(dk_s)
        dv_s[...] = jnp.zeros_like(dv_s)
        for h in range(heads):
            kt_s[h] = k_ref[h, pl.ds(j0, BLK), :].T
        _, stop = row_segment(len_ref, j0 + BLK - 1)
        j = j0 + lax.broadcasted_iota(jnp.int32, (BLK, BLK), 0)

        def inner(ib, carry):
            i0 = pl.multiple_of(ib * BLK, BLK)
            start, i = lane_starts(len_ref, i0, BLK)
            mask = (j >= start) & (j <= i)
            for h in range(heads):
                qh = q_s[h, pl.ds(i0, BLK), :]
                gh = g_s[h, pl.ds(i0, BLK), :]
                s = dot_nt(k_ref[h, pl.ds(j0, BLK), :], qh)
                gw = dot_nt(v_ref[h, pl.ds(j0, BLK), :], gh)
                level = l_s[h : h + 1, pl.ds(i0, BLK)]
                offset = c_s[h : h + 1, pl.ds(i0, BLK)]
                d = d_s[h : h + 1, pl.ds(i0, BLK)]
                p = jnp.exp(jnp.where(mask, jnp.abs(s), NEG) - level)
                u = p - jnp.where(mask, offset, 0.0)
                minus = s < 0
                w = jnp.where(minus, -u, u).astype(BF)
                signed = jnp.where(minus, -d, jnp.where(s == 0, 0.0, d))
                gs = (p * (gw - signed)).astype(BF)
                dv_s[h] += dot_nn(w, gh)
                dk_s[h] += dot_nn(gs, qh)
                dq_s[h, :, pl.ds(i0, BLK)] += dot_nn(kt_s[h], gs)
            return carry

        lax.fori_loop(jb, (stop - 1) // BLK + 1, inner, 0)
        for h in range(heads):
            at = pl.ds(out_row(jb), BLK)
            gp_ref[at, (3 * h + 1) * hd : (3 * h + 2) * hd] = dk_s[h].astype(BF)
            gp_ref[at, (3 * h + 2) * hd : (3 * h + 3) * hd] = dv_s[h].astype(BF)
        return carry

    lax.fori_loop(0, blocks, outer, 0)

    def finish(ib, carry):
        i0 = pl.multiple_of(ib * BLK, BLK)
        for h in range(heads):
            dq = (dq_s[h, :, pl.ds(i0, BLK)] * scale).T.astype(BF)
            gp_ref[pl.ds(out_row(ib), BLK), 3 * h * hd : (3 * h + 1) * hd] = dq
        return carry

    lax.fori_loop(0, blocks, finish, 0)


def attend_back_call(lengths, hid, q, k, v, grads, outs, levels, chunk):
    heads, rows, hd = q.shape
    vm = pl.BlockSpec(memory_space=pltpu.VMEM)
    sm = pl.BlockSpec(memory_space=pltpu.SMEM)
    return pl.pallas_call(
        functools.partial(attend_back_kernel, chunk, 1.0 / math.sqrt(hd)),
        out_shape=jax.ShapeDtypeStruct((rows, heads * 3 * hd), BF),
        in_specs=[sm, sm] + [vm] * 11,
        out_specs=vm,
        scratch_shapes=[
            pltpu.VMEM((heads, rows, hd), BF),
            pltpu.VMEM((heads, rows, hd), BF),
            pltpu.VMEM((heads, hd, BLK), BF),
            pltpu.VMEM((8, rows), F32),
            pltpu.VMEM((8, rows), F32),
            pltpu.VMEM((8, rows), F32),
            pltpu.VMEM((heads, hd, rows), F32),
            pltpu.VMEM((heads, BLK, hd), F32),
            pltpu.VMEM((heads, BLK, hd), F32),
        ],
        cost_estimate=cost(heads * rows * rows * hd * 20, 30 * rows * heads * hd, heads * rows * rows // 2),
        name="attend_back",
    )(lengths, hid, q, k, v, *grads, *outs, *levels)


def feed_kernel(steps, ha_ref, hb_ref, ga_ref, gb_ref, up_ref, v_ref, down_ref, *rest):
    act_ref, gup_ref, gn_ref, out_ref = rest[-4:]
    early = pl.program_id(0) < steps // 2
    h2 = jnp.where(early, ha_ref[...], hb_ref[...])
    grad = jnp.where(early, ga_ref[...], gb_ref[...])
    u = dot_nn(h2, up_ref[...]) + v_ref[5:6, :]
    square = u * u
    tanh = jnp.tanh(u * (GELU_C + (GELU_C * GELU_A) * square))
    half = 0.5 * (1.0 + tanh)
    act = (u * half).astype(BF)
    slope = half + (0.5 * u) * (1.0 - tanh * tanh) * (GELU_C + (3.0 * GELU_C * GELU_A) * square)
    gup = (dot_nt(grad, down_ref[...]) * slope).astype(BF)
    act_ref[...] = act
    gup_ref[...] = gup
    gn_ref[...] = dot_nt(gup, up_ref[...]).astype(BF)
    out_ref[...] = dot_nn(act, down_ref[...]).astype(BF)


def feed_call(ha, hb, ga, gb, up, vectors, down, first, group_rows, before):
    rows, width = ha.shape
    hidden = up.shape[1]
    per = rows // BLK
    steps = 2 * per
    whole = lambda t: (0, 0)
    early = pl.BlockSpec((BLK, width), lambda t: (jnp.minimum(t, per - 1), 0))
    late = pl.BlockSpec((BLK, width), lambda t: (jnp.maximum(t - per, 0), 0))
    return pl.pallas_call(
        functools.partial(feed_kernel, steps),
        out_shape=(
            jax.ShapeDtypeStruct((group_rows, hidden), BF),
            jax.ShapeDtypeStruct((group_rows, hidden), BF),
            jax.ShapeDtypeStruct((2 * rows, width), BF),
            jax.ShapeDtypeStruct((2 * rows, width), BF),
        ),
        grid=(steps,),
        in_specs=[
            early,
            late,
            early,
            late,
            pl.BlockSpec(up.shape, whole),
            pl.BlockSpec(vectors.shape, whole),
            pl.BlockSpec(down.shape, whole),
        ]
        + [pl.BlockSpec(memory_space=pl.ANY)] * len(before),
        out_specs=[
            pl.BlockSpec((BLK, hidden), lambda t: (first * per + t, 0)),
            pl.BlockSpec((BLK, hidden), lambda t: (first * per + t, 0)),
            pl.BlockSpec((BLK, width), lambda t: (t, 0)),
            pl.BlockSpec((BLK, width), lambda t: (t, 0)),
        ],
        input_output_aliases={7 + i: i for i in range(len(before))},
        cost_estimate=cost(16 * rows * width * hidden, 16 * rows * width, 2 * rows * hidden),
        name="feed",
    )(ha, hb, ga, gb, up, vectors, down, *before)


def spots(b_ref, pieces):
    return [b_ref[0] ^ (2 * (spot % 4) + spot // 4) for spot in range(pieces)]


def split_out(b_ref, acc, keep_ref, send_ref):
    piece = acc.shape[0] // 8
    for spot, block in enumerate(spots(b_ref, 8)):
        out = keep_ref if spot < 4 else send_ref
        value = acc[pl.ds(pl.multiple_of(block * piece, 8), piece), :]
        out[(spot % 4) * piece : (spot % 4 + 1) * piece, :] = value.astype(BF)


def weigh_kernel(tiles, b_ref, h0, h1, h2, h3, act_ref, up_ref, g0, g1, g2, g3, keep_ref, send_ref, bias_ref, acc):
    t = pl.program_id(0)
    tile = acc.shape[0] // (2 * tiles)
    chunk = h0.shape[0]
    at = pl.ds(pl.multiple_of(t * tile, tile), tile)

    @pl.when(t == 0)
    def _():
        bias_ref[...] = jnp.sum(up_ref[...].astype(F32), axis=0, keepdims=True)

    @pl.when(t < tiles)
    def _():
        total = dot_tn(h0[...], up_ref[:chunk, :])
        for k, h in enumerate((h1, h2, h3)):
            total = total + dot_tn(h[...], up_ref[(k + 1) * chunk : (k + 2) * chunk, :])
        acc[at, :] = total

    @pl.when(t >= tiles)
    def _():
        total = dot_tn(act_ref[:chunk, :], g0[...])
        for k, g in enumerate((g1, g2, g3)):
            total = total + dot_tn(act_ref[(k + 1) * chunk : (k + 2) * chunk, :], g[...])
        acc[at, :] = total

    @pl.when(t == 2 * tiles - 1)
    def _():
        split_out(b_ref, acc, keep_ref, send_ref)


def weigh_call(bid, hs, act, up, grads):
    chunk, width = hs[0].shape
    rows, hidden = act.shape
    tile = 256
    tiles = width // tile
    whole = lambda t, b: (0, 0)
    total = width + hidden
    half = jax.ShapeDtypeStruct((total // 2, width), BF)
    return pl.pallas_call(
        functools.partial(weigh_kernel, tiles),
        out_shape=(half, half, jax.ShapeDtypeStruct((1, hidden), F32)),
        grid_spec=pltpu.PrefetchScalarGridSpec(
            num_scalar_prefetch=1,
            grid=(2 * tiles,),
            in_specs=[pl.BlockSpec((chunk, tile), lambda t, b: (0, jnp.minimum(t, tiles - 1)))] * 4
            + [
                pl.BlockSpec((rows, tile), lambda t, b: (0, jnp.maximum(t - tiles, 0))),
                pl.BlockSpec((rows, hidden), whole),
            ]
            + [pl.BlockSpec((chunk, width), whole)] * 4,
            out_specs=[
                pl.BlockSpec(half.shape, whole),
                pl.BlockSpec(half.shape, whole),
                pl.BlockSpec((1, hidden), whole),
            ],
            scratch_shapes=[pltpu.VMEM((total, width), F32)],
        ),
        cost_estimate=cost(4 * rows * width * hidden, 12 * rows * width),
        name="weigh",
    )(bid, *hs, act, up, *grads)


def mix_kernel(m0, m1, m2, m3, p0, p1, p2, p3, x_ref, v_ref, resid_ref, h_ref):
    total = x_ref[...].astype(F32) + v_ref[2:3, :]
    for m, p in ((m0, p0), (m1, p1), (m2, p2), (m3, p3)):
        total = total + dot_nn(m[...], p[...])
    resid_ref[...] = total
    hat, _ = normalize(total)
    h_ref[...] = (hat * v_ref[3:4, :] + v_ref[4:5, :]).astype(BF)


def mix_call(parts, projs, x, vectors):
    rows, width = x.shape
    per = rows // BLK
    inner = parts[0].shape[1]
    low = pl.BlockSpec((BLK, inner), lambda t: (t, 0))
    high = pl.BlockSpec((BLK, inner), lambda t: (t + per, 0))
    whole = lambda t: (0, 0)
    return pl.pallas_call(
        mix_kernel,
        out_shape=(jax.ShapeDtypeStruct((rows, width), F32), jax.ShapeDtypeStruct((rows, width), BF)),
        grid=(per,),
        in_specs=[low, high, low, high]
        + [pl.BlockSpec(projs[0].shape, whole)] * 4
        + [pl.BlockSpec((BLK, width), lambda t: (t, 0)), pl.BlockSpec(vectors.shape, whole)],
        out_specs=[pl.BlockSpec((BLK, width), lambda t: (t, 0))] * 2,
        cost_estimate=cost(8 * rows * width * inner, 12 * rows * width),
        name="mix",
    )(*parts, *projs, x, vectors)


def turn_kernel(n_ref, s_ref, f_ref, resid_ref, cot_ref, v_ref, p0, p1, p2, p3, gr_ref, ga_ref, gn_ref, gf_ref, sum_ref):
    grad = n_ref[...].astype(F32) + s_ref[...].astype(F32) + f_ref[...].astype(F32)
    hat, rstd = normalize(resid_ref[...])
    cot = cot_ref[...].astype(F32)
    e = grad * v_ref[3:4, :]
    back = e - jnp.mean(e, axis=-1, keepdims=True) - hat * jnp.mean(e * hat, axis=-1, keepdims=True)
    grad_resid = cot + rstd * back
    gr_ref[...] = grad_resid
    att = grad_resid.astype(BF)
    ga_ref[...] = att
    gn_ref[0] = dot_nt(att, p0[...]).astype(BF)
    gn_ref[1] = dot_nt(att, p1[...]).astype(BF)
    gf_ref[0] = dot_nt(att, p2[...]).astype(BF)
    gf_ref[1] = dot_nt(att, p3[...]).astype(BF)

    @pl.when(pl.program_id(0) == 0)
    def _():
        sum_ref[...] = jnp.zeros_like(sum_ref)

    for k, v in enumerate((grad_resid, grad * hat, grad, cot)):
        sum_ref[k + 4 : k + 5, :] += jnp.sum(v, axis=0, keepdims=True)


def turn_call(near, swapped, far, resid, cot, vectors, projs):
    rows, width = resid.shape
    per = rows // BLK
    inner = projs[0].shape[0]
    low = pl.BlockSpec((BLK, width), lambda t: (t, 0))
    high = pl.BlockSpec((BLK, width), lambda t: (t + per, 0))
    whole = lambda t: (0, 0)
    pair = jax.ShapeDtypeStruct((2, rows, inner), BF)
    pair_spec = pl.BlockSpec((2, BLK, inner), lambda t: (0, t, 0))
    return pl.pallas_call(
        turn_kernel,
        out_shape=(
            jax.ShapeDtypeStruct((rows, width), F32),
            jax.ShapeDtypeStruct((rows, width), BF),
            pair,
            pair,
            jax.ShapeDtypeStruct((8, width), F32),
        ),
        grid=(per,),
        in_specs=[low, high, low, low, low, pl.BlockSpec(vectors.shape, whole)]
        + [pl.BlockSpec(projs[0].shape, whole)] * 4,
        out_specs=[low, low, pair_spec, pair_spec, pl.BlockSpec((8, width), whole)],
        cost_estimate=cost(8 * rows * width * inner, 20 * rows * width),
        name="turn",
    )(near, swapped, far, resid, cot, vectors, *projs)


def close_kernel(per, b_ref, x0, x1, x2, x3, gp_ref, w_ref, v_ref, pw_ref, up_ref, s_ref, near_ref, far_ref, keep_ref, send_ref, sum_ref, acc):
    t = pl.program_id(0)
    steps = 4 * per
    x = jnp.where(t < 2 * per, jnp.where(t < per, x0[...], x1[...]), jnp.where(t < 3 * per, x2[...], x3[...]))
    hat, _ = normalize(x.astype(F32))
    h1 = (hat * v_ref[0:1, :] + v_ref[1:2, :]).astype(BF)
    gp = gp_ref[...]
    cols = gp.shape[1]
    e = dot_nn(gp, w_ref[...])

    @pl.when(t < 2 * per)
    def _():
        near_ref[...] = e.astype(BF)

    @pl.when(t >= 2 * per)
    def _():
        far_ref[...] = e.astype(BF)

    @pl.when(t == 0)
    def _():
        sum_ref[...] = s_ref[...]
        acc[...] = jnp.zeros_like(acc)
        acc[cols : cols + pw_ref.shape[0], :] = pw_ref[...]
        acc[cols + pw_ref.shape[0] + 1 : cols + pw_ref.shape[0] + 2, :] = up_ref[...]

    sum_ref[0:1, :] += jnp.sum(e * hat, axis=0, keepdims=True)
    sum_ref[1:2, :] += jnp.sum(e, axis=0, keepdims=True)
    acc[:cols, :] += dot_tn(gp, h1)
    base = cols + pw_ref.shape[0]
    acc[base : base + 1, :cols] += jnp.sum(gp.astype(F32), axis=0, keepdims=True)

    @pl.when(t == steps - 1)
    def _():
        split_out(b_ref, acc, keep_ref, send_ref)
        half = acc.shape[0] // 2
        keep_ref[half:, :] = sum_ref[...].astype(BF)
        send_ref[half:, :] = sum_ref[...].astype(BF)


def close_call(bid, rows, gp, w, vectors, proj_grad, up_grad, sums, total):
    chunk, width = rows[0].shape
    cols = gp.shape[1]
    per = chunk // BLK
    steps = 4 * per
    whole = lambda t, b: (0, 0)
    part = lambda k: pl.BlockSpec((BLK, width), lambda t, b: (jnp.clip(t - k * per, 0, per - 1), 0))
    half = jax.ShapeDtypeStruct((total // 2 + sums.shape[0], width), BF)
    return pl.pallas_call(
        functools.partial(close_kernel, per),
        out_shape=(
            jax.ShapeDtypeStruct((2 * chunk, width), BF),
            jax.ShapeDtypeStruct((2 * chunk, width), BF),
            half,
            half,
        ),
        grid_spec=pltpu.PrefetchScalarGridSpec(
            num_scalar_prefetch=1,
            grid=(steps,),
            in_specs=[part(0), part(1), part(2), part(3)]
            + [pl.BlockSpec((BLK, cols), lambda t, b: (t, 0))]
            + [pl.BlockSpec(v.shape, whole) for v in (w, vectors, proj_grad, up_grad, sums)],
            out_specs=[
                pl.BlockSpec((BLK, width), lambda t, b: (jnp.minimum(t, 2 * per - 1), 0)),
                pl.BlockSpec((BLK, width), lambda t, b: (jnp.maximum(t - 2 * per, 0), 0)),
                pl.BlockSpec(half.shape, whole),
                pl.BlockSpec(half.shape, whole),
            ],
            scratch_shapes=[pltpu.VMEM((8, width), F32), pltpu.VMEM((total, width), F32)],
        ),
        cost_estimate=cost(16 * chunk * width * cols, 20 * chunk * width),
        name="close",
    )(bid, *rows, gp, w, vectors, proj_grad, up_grad, sums)


def unpack_kernel(counts, b_ref, keep_ref, other_ref, *rest):
    acc = rest[-1]
    piece = acc.shape[0] // 8
    for spot, block in enumerate(spots(b_ref, 8)):
        src = keep_ref if spot < 4 else other_ref
        value = src[(spot % 4) * piece : (spot % 4 + 1) * piece, :].astype(F32)
        acc[pl.ds(pl.multiple_of(block * piece, 8), piece), :] = value
    start = 0
    for out, count in zip(rest[:-1], counts, strict=True):
        out[...] = acc[start : start + count, :]
        start += count


def unpack_call(bid, keep, other, counts):
    half, width = keep.shape
    vm = pl.BlockSpec(memory_space=pltpu.VMEM)
    return pl.pallas_call(
        functools.partial(unpack_kernel, counts),
        out_shape=tuple(jax.ShapeDtypeStruct((n, width), F32) for n in counts),
        in_specs=[pl.BlockSpec(memory_space=pltpu.SMEM), vm, vm],
        out_specs=[vm] * len(counts),
        scratch_shapes=[pltpu.VMEM((2 * half, width), F32)],
        cost_estimate=cost(half * width, 12 * half * width),
        name="unpack",
    )(bid, keep, other)


def tie(x, *needed):
    return lax.optimization_barrier((x,) + needed)[0]


def across(pieces):
    return [swap(piece, "batch", 2 * d) for d, piece in enumerate(pieces, 1)]


def sum_rest(x):
    for level in range(3, lax.axis_size("batch").bit_length() - 1):
        x = (x.astype(F32) + swap(x, "batch", 1 << level).astype(F32)).astype(x.dtype)
    return x


def fold(kept, got):
    piece = kept.shape[0] // 4
    total = kept[:piece].astype(F32)
    for g in got:
        total = total + g[:piece].astype(F32)
    return sum_rest(total.astype(BF))


def quarters(x):
    piece = x.shape[0] // 4
    return [x[d * piece : (d + 1) * piece] for d in range(1, 4)]


def sum_group(x):
    x = x + swap(x, "head", 1)
    return x + swap(x, "head", 2)


def per_device(
    inputs,
    lengths,
    cotangent,
    gain_attn,
    shift_attn,
    weight_qkv,
    bias_qkv,
    weight_proj,
    bias_proj,
    gain_mlp,
    shift_mlp,
    weight_up,
    bias_up,
    weight_down,
    bias_down,
):
    chunk, width = inputs.shape
    group_rows = chunk * lax.axis_size("head")
    heads, triple = weight_qkv.shape[1:]
    cols = heads * triple
    inner = cols // 3
    own = lax.axis_index("head")
    hid = own.astype(jnp.int32).reshape(1)
    bid = (lax.axis_index("batch") % 8).astype(jnp.int32).reshape(1)
    lens = lengths[0]
    live_rows = jnp.sum(lens[:-1])
    places = own * chunk + jnp.arange(chunk, dtype=jnp.int32)
    live = (places < live_rows)[:, None]
    qkv_t = weight_qkv.transpose(1, 2, 0).reshape(cols, width)
    proj = weight_proj.reshape(inner, width)
    zero = jnp.zeros((width,), F32)
    vectors = jnp.stack(
        (gain_attn, shift_attn, bias_proj, gain_mlp, shift_mlp, bias_up, bias_down, zero)
    )

    x_far = swap(inputs, "head", 2)
    x_near = swap(inputs, "head", 1)
    begun = qkv_call(hid, inputs, x_near, vectors, qkv_t, bias_qkv, 0, group_rows, ())
    x_far = tie(x_far, begun[0])
    x_last = swap(x_far, "head", 1)
    queries, keys, values, values_t = qkv_call(
        hid, x_far, x_last, vectors, qkv_t, bias_qkv, 2, group_rows, begun
    )
    rows = (inputs, x_near, x_far, x_last)
    grad_own = jnp.where(live, cotangent, jnp.zeros_like(cotangent))
    grad_far = swap(tie(grad_own, x_far), "head", 2)
    proj_far = swap(tie(proj, x_far), "head", 2)
    projs = (proj, swap(proj, "head", 1), proj_far, swap(proj_far, "head", 1))

    merged_far, level_far = attend_call(lens, hid, queries, keys, values_t, 2, chunk)
    from_far = swap(merged_far, "head", 2)
    merged_near, level_near = attend_call(
        lens, hid, tie(queries, merged_far, grad_far), keys, values_t, 0, chunk
    )
    grads = (grad_own, swap(grad_own, "head", 1), grad_far, swap(grad_far, "head", 1))
    parts = (merged_near, swap(merged_near, "head", 1), from_far, swap(from_far, "head", 1))
    resid, h_own = mix_call(parts, projs, inputs, vectors)
    h_far = swap(h_own, "head", 2)
    h_near = swap(h_own, "head", 1)

    near = feed_call(h_own, h_near, grads[0], grads[1], weight_up, vectors, weight_down, 0, group_rows, ())
    h_far = tie(h_far, near[0])
    h_last = swap(h_far, "head", 1)
    act, grad_up, grad_norm_far, down_far = feed_call(
        h_far, h_last, grads[2], grads[3], weight_up, vectors, weight_down, 2, group_rows, near[:2]
    )
    swapped = swap(grad_norm_far, "head", 1)
    far_sum = (grad_norm_far[:chunk].astype(F32) + swapped[chunk:].astype(F32)).astype(BF)
    grad_far_sum = swap(far_sum, "head", 2)
    near_swapped = swap(near[2], "head", 1)

    keep_feed, send_feed, grad_bup = weigh_call(
        bid, (h_own, h_near, h_far, h_last), tie(act, far_sum), grad_up, grads
    )
    other_feed = swap(send_feed, "batch", 1)

    grad_resid, grad_att, grad_near, grad_cross, sums = turn_call(
        near[2], near_swapped, tie(grad_far_sum, grad_bup), resid, grad_own, vectors, projs
    )
    grad_near = grad_near.reshape(2 * chunk, inner)
    got = swap(grad_cross.reshape(2 * chunk, inner), "head", 2)
    grad_mate = swap(grad_near, "head", 1)
    grad_att = tie(grad_att, grad_mate)
    low = slice(0, chunk)
    high = slice(chunk, 2 * chunk)
    grad_proj = [
        dot_tn(p[at], grad_att) for p, at in zip(parts, (low, high, low, high), strict=True)
    ]
    near_sent, far_sent = grad_proj[1].astype(BF), grad_proj[3].astype(BF)
    got = tie(got, near_sent, far_sent)
    merged_grads = (grad_near, grad_mate, got, swap(got, "head", 1))
    grad_near_proj = grad_proj[0] + swap(near_sent, "head", 1).astype(F32)
    far_proj = (grad_proj[2] + swap(far_sent, "head", 1).astype(F32)).astype(BF)
    far_proj = swap(far_proj, "head", 2)

    kept_feed = (keep_feed.astype(F32) + tie(other_feed, got).astype(F32)).astype(BF)
    got_feed = across(quarters(kept_feed))

    grad_packed = attend_back_call(
        lens,
        hid,
        tie(queries, kept_feed, grad_near_proj),
        keys,
        values,
        merged_grads,
        (merged_near, merged_far),
        (level_near, level_far),
        chunk,
    )
    got_feed = [tie(g, grad_packed) for g in got_feed]
    grad_wproj = grad_near_proj + tie(far_proj, grad_packed).astype(F32)
    total_feed = fold(kept_feed, got_feed)
    gathered_feed = across([total_feed] * 3)
    total = -(-(cols + inner + 8) // 64) * 64
    e_near, e_far, keep, send = close_call(
        bid, rows, tie(grad_packed, total_feed), qkv_t, vectors, grad_wproj, grad_bup, sums, total
    )
    e_swapped = swap(e_far, "head", 1)
    e_sum = (e_far[:chunk].astype(F32) + e_swapped[chunk:].astype(F32)).astype(BF)
    e_other = swap(e_sum, "head", 2)
    e_mate = swap(e_near, "head", 1)
    e_own = e_near[:chunk].astype(F32) + e_mate[chunk:].astype(F32) + e_other.astype(F32)
    half_feed = jnp.concatenate([total_feed] + [tie(g, e_far) for g in gathered_feed], axis=0)
    last_feed = swap(tie(half_feed, e_sum), "batch", 1)
    other = tie(swap(send, "batch", 1), half_feed)
    kept = (keep.astype(F32) + other.astype(F32)).astype(BF)
    kept, small = kept[:-8], kept[-8:]
    got_attn = across([jnp.concatenate((q, small), axis=0) for q in quarters(kept)])
    tiny = [small.astype(F32)] + [g[-8:].astype(F32) for g in got_attn]
    small = sum_group(sum_rest((tiny[0] + tiny[1]) + (tiny[2] + tiny[3])))
    total_attn = fold(kept, got_attn)

    down_swapped = swap(tie(down_far, kept), "head", 1)
    down_sum = (down_far[:chunk].astype(F32) + down_swapped[chunk:].astype(F32)).astype(BF)
    down_other = swap(tie(down_sum, e_other), "head", 2)
    near_down = near[3][:chunk].astype(F32) + swap(tie(near[3], kept), "head", 1)[chunk:].astype(F32)
    output = (resid + near_down + down_other.astype(F32) + bias_down).astype(BF)

    half = jnp.concatenate([total_attn] + across([total_attn] * 3), axis=0)
    last = swap(tie(half, last_feed), "batch", 1)
    sum_wup, sum_wdown = unpack_call(bid, half_feed, tie(last_feed, half), (width, width))
    sum_wqkv, sum_wproj, sum_bias = unpack_call(bid, half, tie(last, sum_wup), (cols, inner, 8))

    x_hat, x_rstd = normalize(inputs.astype(F32))
    e_own = e_own * gain_attn
    grad_inputs = (
        grad_resid
        + x_rstd
        * (
            e_own
            - jnp.mean(e_own, axis=-1, keepdims=True)
            - x_hat * jnp.mean(e_own * x_hat, axis=-1, keepdims=True)
        )
    ).astype(BF)
    return (
        output,
        grad_inputs,
        small[0],
        small[1],
        sum_wqkv.reshape(heads, triple, width).transpose(2, 0, 1),
        sum_bias[0, :cols].reshape(heads, triple),
        sum_wproj.reshape(heads, inner // heads, width),
        small[4],
        small[5],
        small[6],
        sum_wup,
        sum_bias[1],
        sum_wdown,
        small[7],
    )


def solution(mesh):
    rows = P(("batch", "head"), None)
    in_specs = (
        rows,
        P("batch", None),
        rows,
        P(),
        P(),
        P(None, "head", None),
        P("head", None),
        P("head", None, None),
        P(),
        P(),
        P(),
        P(None, "head"),
        P("head"),
        P("head", None),
        P(),
    )
    out_specs = (
        rows,
        rows,
        P(),
        P(),
        P(None, "head", None),
        P("head", None),
        P("head", None, None),
        P(),
        P(),
        P(),
        P(None, "head"),
        P("head"),
        P("head", None),
        P(),
    )
    return jax.shard_map(
        per_device, mesh=mesh, in_specs=in_specs, out_specs=out_specs, check_vma=False
    )
```

```python
import functools
import math

import jax
import jax.numpy as jnp
from jax import lax
from jax.experimental import pallas as pl
from jax.experimental.pallas import tpu as pltpu
from jax.sharding import PartitionSpec as P

F32 = jnp.float32
BF = jnp.bfloat16
BLK = 256
NEG = -1e30
EPS = 1e-05
GELU_C = math.sqrt(2.0 / math.pi)
GELU_A = 0.044715


def dot_nn(a, b):
    return lax.dot_general(a, b, (((1,), (0,)), ((), ())), preferred_element_type=F32)


def dot_nt(a, b):
    return lax.dot_general(a, b, (((1,), (1,)), ((), ())), preferred_element_type=F32)


def dot_tn(a, b):
    return lax.dot_general(a, b, (((0,), (0,)), ((), ())), preferred_element_type=F32)


def cost(flops, nbytes, trans=0):
    return pl.CostEstimate(flops=int(flops), bytes_accessed=int(nbytes), transcendentals=int(trans))


def swap(x, axis, bits):
    size = lax.axis_size(axis)
    return lax.ppermute(x, axis, [(i, i ^ bits) for i in range(size)])


def normalize(v):
    center = v - jnp.mean(v, axis=-1, keepdims=True)
    rstd = lax.rsqrt(jnp.mean(center * center, axis=-1, keepdims=True) + EPS)
    return center * rstd, rstd


def qkv_kernel(heads, hd, steps, h_ref, a_ref, b_ref, v_ref, w_ref, bias_ref, *rest):
    q_out, k_out, v_out, vt_out, hat_out = rest[-5:]
    t = pl.program_id(0)
    x = jnp.where(t < steps // 2, a_ref[...], b_ref[...]).astype(F32)
    xhat, _ = normalize(x)
    hat_out[...] = xhat.astype(BF)
    h1 = (xhat * v_ref[0:1, :] + v_ref[1:2, :]).astype(BF)
    bias = jnp.concatenate([bias_ref[h : h + 1, :] for h in range(heads)], axis=1)
    packed = (dot_nt(h1, w_ref[...]) + bias).astype(BF)
    for h in range(heads):
        o = 3 * hd * h
        q_out[h] = packed[:, o : o + hd]
        k_out[h] = packed[:, o + hd : o + 2 * hd]
        v = packed[:, o + 2 * hd : o + 3 * hd]
        v_out[h] = v
        vt_out[h] = v.T


def qkv_call(hid, a, b, vectors, w, bias, first, group_rows, before):
    rows, width = a.shape
    heads, triple = bias.shape
    hd = triple // 3
    per = rows // BLK
    steps = 2 * per
    place = lambda t, h: (h[0] ^ (first + t // per)) * per + t % per
    whole = lambda t, h: (0, 0)
    out_shape = tuple(
        jax.ShapeDtypeStruct(s, BF)
        for s in ((heads, group_rows, hd),) * 3 + ((heads, hd, group_rows), (group_rows, width))
    )
    in_specs = [
        pl.BlockSpec((BLK, width), lambda t, h: (jnp.minimum(t, per - 1), 0)),
        pl.BlockSpec((BLK, width), lambda t, h: (jnp.maximum(t - per, 0), 0)),
        pl.BlockSpec(vectors.shape, whole),
        pl.BlockSpec(w.shape, whole),
        pl.BlockSpec(bias.shape, whole),
    ] + [pl.BlockSpec(memory_space=pl.ANY)] * len(before)
    return pl.pallas_call(
        functools.partial(qkv_kernel, heads, hd, steps),
        out_shape=out_shape,
        grid_spec=pltpu.PrefetchScalarGridSpec(
            num_scalar_prefetch=1,
            grid=(steps,),
            in_specs=in_specs,
            out_specs=[pl.BlockSpec((heads, BLK, hd), lambda t, h: (0, place(t, h), 0))] * 3
            + [
                pl.BlockSpec((heads, hd, BLK), lambda t, h: (0, 0, place(t, h))),
                pl.BlockSpec((BLK, width), lambda t, h: (first * per + t, 0)),
            ],
        ),
        input_output_aliases={6 + i: i for i in range(len(before))},
        cost_estimate=cost(4 * rows * width * w.shape[0], 12 * rows * width),
        name="qkv",
    )(hid, a, b, vectors, w, bias, *before)


def row_segment(len_ref, row):
    low = row
    high = row + 1
    start = jnp.int32(0)
    for k in range(len_ref.shape[0] - 1):
        stop = start + len_ref[k]
        inside = (row >= start) & (row < stop)
        low = jnp.where(inside, start, low)
        high = jnp.where(inside, stop, high)
        start = stop
    return low, high


def lane_starts(len_ref, row, width):
    i = row + lax.broadcasted_iota(jnp.int32, (1, width), 1)
    start = jnp.zeros((1, width), jnp.int32)
    stop = jnp.int32(0)
    for k in range(len_ref.shape[0] - 1):
        stop = stop + len_ref[k]
        start = jnp.where(i >= stop, stop, start)
    return jnp.where(i >= stop, i, start), i


def attend_kernel(heads, first, per, scale, len_ref, h_ref, q_ref, k_ref, vt_ref, o_ref, l_ref, m_s, z_s, acc_s):
    t = pl.program_id(0)
    row = ((h_ref[0] ^ (first + t // per)) * per + t % per) * BLK
    start, i = lane_starts(len_ref, row, BLK)
    low, _ = row_segment(len_ref, row)
    m_s[...] = jnp.full_like(m_s, NEG)
    z_s[...] = jnp.zeros_like(z_s)
    acc_s[...] = jnp.zeros_like(acc_s)
    qs = [q_ref[h] * jnp.asarray(scale, BF) for h in range(heads)]

    def body(jb, carry):
        j0 = pl.multiple_of(jb * BLK, BLK)
        j = j0 + lax.broadcasted_iota(jnp.int32, (BLK, BLK), 0)
        mask = (j >= start) & (j <= i)
        for h in range(heads):
            s = dot_nt(k_ref[h, pl.ds(j0, BLK), :], qs[h])
            magnitude = jnp.where(mask, jnp.abs(s), NEG)
            old = m_s[h : h + 1, :]
            top = jnp.maximum(old, jnp.max(magnitude, axis=0, keepdims=True))
            decay = jnp.exp(old - top)
            e = jnp.exp(magnitude - top)
            z_s[h : h + 1, :] = z_s[h : h + 1, :] * decay + jnp.sum(e, axis=0, keepdims=True)
            m_s[h : h + 1, :] = top
            u = e - jnp.where(mask, jnp.exp(-top), 0.0)
            w = jnp.where(s < 0, -u, u).astype(BF)
            acc_s[h] = acc_s[h] * decay + dot_nn(vt_ref[h, :, pl.ds(j0, BLK)], w)
        return carry

    lax.fori_loop(low // BLK, row // BLK + 1, body, 0)
    outs = []
    for h in range(heads):
        z = z_s[h : h + 1, :]
        outs.append((acc_s[h] / z).T)
        l_ref[h : h + 1, :] = m_s[h : h + 1, :] + jnp.log(z)
    o_ref[...] = jnp.concatenate(outs, axis=1).astype(BF)


def attend_call(lengths, hid, q, k, vt, first, chunk):
    heads, rows, hd = q.shape
    per = chunk // BLK
    steps = 2 * per
    place = lambda t, n, h: (0, (h[0] ^ (first + t // per)) * per + t % per, 0)
    whole = lambda t, n, h: (0, 0, 0)
    return pl.pallas_call(
        functools.partial(attend_kernel, heads, first, per, 1.0 / math.sqrt(hd)),
        out_shape=(
            jax.ShapeDtypeStruct((steps * BLK, heads * hd), BF),
            jax.ShapeDtypeStruct((8, steps * BLK), F32),
        ),
        grid_spec=pltpu.PrefetchScalarGridSpec(
            num_scalar_prefetch=2,
            grid=(steps,),
            in_specs=[
                pl.BlockSpec((heads, BLK, hd), place),
                pl.BlockSpec((heads, rows, hd), whole),
                pl.BlockSpec((heads, hd, rows), whole),
            ],
            out_specs=[
                pl.BlockSpec((BLK, heads * hd), lambda t, n, h: (t, 0)),
                pl.BlockSpec((8, BLK), lambda t, n, h: (0, t)),
            ],
            scratch_shapes=[
                pltpu.VMEM((8, BLK), F32),
                pltpu.VMEM((8, BLK), F32),
                pltpu.VMEM((heads, hd, BLK), F32),
            ],
        ),
        cost_estimate=cost(heads * rows * rows * hd * 4, 12 * rows * heads * hd, heads * rows * rows // 4),
        name="attend",
    )(lengths, hid, q, k, vt)


def attend_back_kernel(chunk, scale, len_ref, h_ref, q_ref, k_ref, v_ref, *rest):
    g_refs, o_refs, l_refs = rest[0:4], rest[4:6], rest[6:8]
    gp_ref, q_s, g_s, kt_s, l_s, c_s, d_s, dq_s, dk_s, dv_s = rest[8:]
    heads, rows, hd = q_ref.shape
    blocks = rows // BLK
    per = chunk // BLK
    own = h_ref[0]
    for c in range(4):
        r0 = pl.multiple_of((own ^ c) * chunk, chunk)
        part = slice((c % 2) * chunk, (c % 2 + 1) * chunk)
        g = g_refs[c][part, :]
        o = o_refs[c // 2][part, :]
        for h in range(heads):
            gh = g[:, h * hd : (h + 1) * hd]
            g_s[h, pl.ds(r0, chunk), :] = gh
            both = gh.astype(F32) * o[:, h * hd : (h + 1) * hd].astype(F32)
            d_s[h : h + 1, pl.ds(r0, chunk)] = jnp.sum(both.T, axis=0, keepdims=True)
        level = l_refs[c // 2][:, part]
        l_s[:, pl.ds(r0, chunk)] = level
        c_s[:, pl.ds(r0, chunk)] = jnp.exp(-level)
    for h in range(heads):
        q_s[h] = q_ref[h] * jnp.asarray(scale, BF)
    dq_s[...] = jnp.zeros_like(dq_s)

    def out_row(block):
        return pl.multiple_of(((own ^ (block // per)) * per + block % per) * BLK, BLK)

    def outer(jb, carry):
        j0 = pl.multiple_of(jb * BLK, BLK)
        dk_s[...] = jnp.zeros_like(dk_s)
        dv_s[...] = jnp.zeros_like(dv_s)
        for h in range(heads):
            kt_s[h] = k_ref[h, pl.ds(j0, BLK), :].T
        _, stop = row_segment(len_ref, j0 + BLK - 1)
        j = j0 + lax.broadcasted_iota(jnp.int32, (BLK, BLK), 0)

        def inner(ib, carry):
            i0 = pl.multiple_of(ib * BLK, BLK)
            start, i = lane_starts(len_ref, i0, BLK)
            mask = (j >= start) & (j <= i)
            for h in range(heads):
                qh = q_s[h, pl.ds(i0, BLK), :]
                gh = g_s[h, pl.ds(i0, BLK), :]
                s = dot_nt(k_ref[h, pl.ds(j0, BLK), :], qh)
                gw = dot_nt(v_ref[h, pl.ds(j0, BLK), :], gh)
                level = l_s[h : h + 1, pl.ds(i0, BLK)]
                offset = c_s[h : h + 1, pl.ds(i0, BLK)]
                d = d_s[h : h + 1, pl.ds(i0, BLK)]
                p = jnp.exp(jnp.where(mask, jnp.abs(s), NEG) - level)
                u = p - jnp.where(mask, offset, 0.0)
                minus = s < 0
                w = jnp.where(minus, -u, u).astype(BF)
                signed = jnp.where(minus, -d, jnp.where(s == 0, 0.0, d))
                gs = (p * (gw - signed)).astype(BF)
                dv_s[h] += dot_nn(w, gh)
                dk_s[h] += dot_nn(gs, qh)
                dq_s[h, :, pl.ds(i0, BLK)] += dot_nn(kt_s[h], gs)
            return carry

        lax.fori_loop(jb, (stop - 1) // BLK + 1, inner, 0)
        for h in range(heads):
            at = pl.ds(out_row(jb), BLK)
            gp_ref[at, (3 * h + 1) * hd : (3 * h + 2) * hd] = dk_s[h].astype(BF)
            gp_ref[at, (3 * h + 2) * hd : (3 * h + 3) * hd] = dv_s[h].astype(BF)
        return carry

    lax.fori_loop(0, blocks, outer, 0)

    def finish(ib, carry):
        i0 = pl.multiple_of(ib * BLK, BLK)
        for h in range(heads):
            dq = (dq_s[h, :, pl.ds(i0, BLK)] * scale).T.astype(BF)
            gp_ref[pl.ds(out_row(ib), BLK), 3 * h * hd : (3 * h + 1) * hd] = dq
        return carry

    lax.fori_loop(0, blocks, finish, 0)


def attend_back_call(lengths, hid, q, k, v, grads, outs, levels, chunk):
    heads, rows, hd = q.shape
    vm = pl.BlockSpec(memory_space=pltpu.VMEM)
    sm = pl.BlockSpec(memory_space=pltpu.SMEM)
    return pl.pallas_call(
        functools.partial(attend_back_kernel, chunk, 1.0 / math.sqrt(hd)),
        out_shape=jax.ShapeDtypeStruct((rows, heads * 3 * hd), BF),
        in_specs=[sm, sm] + [vm] * 11,
        out_specs=vm,
        scratch_shapes=[
            pltpu.VMEM((heads, rows, hd), BF),
            pltpu.VMEM((heads, rows, hd), BF),
            pltpu.VMEM((heads, hd, BLK), BF),
            pltpu.VMEM((8, rows), F32),
            pltpu.VMEM((8, rows), F32),
            pltpu.VMEM((8, rows), F32),
            pltpu.VMEM((heads, hd, rows), F32),
            pltpu.VMEM((heads, BLK, hd), F32),
            pltpu.VMEM((heads, BLK, hd), F32),
        ],
        cost_estimate=cost(heads * rows * rows * hd * 20, 30 * rows * heads * hd, heads * rows * rows // 2),
        name="attend_back",
    )(lengths, hid, q, k, v, *grads, *outs, *levels)


def feed_kernel(steps, ha_ref, hb_ref, ga_ref, gb_ref, up_ref, v_ref, down_ref, *rest):
    act_ref, gup_ref, gn_ref, out_ref = rest[-4:]
    early = pl.program_id(0) < steps // 2
    h2 = jnp.where(early, ha_ref[...], hb_ref[...])
    grad = jnp.where(early, ga_ref[...], gb_ref[...])
    u = dot_nn(h2, up_ref[...]) + v_ref[5:6, :]
    square = u * u
    tanh = jnp.tanh(u * (GELU_C + (GELU_C * GELU_A) * square))
    half = 0.5 * (1.0 + tanh)
    act = (u * half).astype(BF)
    slope = half + (0.5 * u) * (1.0 - tanh * tanh) * (GELU_C + (3.0 * GELU_C * GELU_A) * square)
    gup = (dot_nt(grad, down_ref[...]) * slope).astype(BF)
    act_ref[...] = act
    gup_ref[...] = gup
    gn_ref[...] = dot_nt(gup, up_ref[...]).astype(BF)
    out_ref[...] = dot_nn(act, down_ref[...]).astype(BF)


def feed_call(ha, hb, ga, gb, up, vectors, down, first, group_rows, before):
    rows, width = ha.shape
    hidden = up.shape[1]
    per = rows // BLK
    steps = 2 * per
    whole = lambda t: (0, 0)
    early = pl.BlockSpec((BLK, width), lambda t: (jnp.minimum(t, per - 1), 0))
    late = pl.BlockSpec((BLK, width), lambda t: (jnp.maximum(t - per, 0), 0))
    return pl.pallas_call(
        functools.partial(feed_kernel, steps),
        out_shape=(
            jax.ShapeDtypeStruct((group_rows, hidden), BF),
            jax.ShapeDtypeStruct((group_rows, hidden), BF),
            jax.ShapeDtypeStruct((2 * rows, width), BF),
            jax.ShapeDtypeStruct((2 * rows, width), BF),
        ),
        grid=(steps,),
        in_specs=[
            early,
            late,
            early,
            late,
            pl.BlockSpec(up.shape, whole),
            pl.BlockSpec(vectors.shape, whole),
            pl.BlockSpec(down.shape, whole),
        ]
        + [pl.BlockSpec(memory_space=pl.ANY)] * len(before),
        out_specs=[
            pl.BlockSpec((BLK, hidden), lambda t: (first * per + t, 0)),
            pl.BlockSpec((BLK, hidden), lambda t: (first * per + t, 0)),
            pl.BlockSpec((BLK, width), lambda t: (t, 0)),
            pl.BlockSpec((BLK, width), lambda t: (t, 0)),
        ],
        input_output_aliases={7 + i: i for i in range(len(before))},
        cost_estimate=cost(16 * rows * width * hidden, 16 * rows * width, 2 * rows * hidden),
        name="feed",
    )(ha, hb, ga, gb, up, vectors, down, *before)


def spots(b_ref, pieces):
    return [b_ref[0] ^ (2 * (spot % 4) + spot // 4) for spot in range(pieces)]


def split_out(b_ref, acc, keep_ref, send_ref):
    piece = acc.shape[0] // 8
    for spot, block in enumerate(spots(b_ref, 8)):
        out = keep_ref if spot < 4 else send_ref
        value = acc[pl.ds(pl.multiple_of(block * piece, 8), piece), :]
        out[(spot % 4) * piece : (spot % 4 + 1) * piece, :] = value.astype(BF)


def weigh_kernel(tiles, b_ref, h0, h1, h2, h3, act_ref, up_ref, g0, g1, g2, g3, keep_ref, send_ref, bias_ref, acc):
    t = pl.program_id(0)
    tile = acc.shape[0] // (2 * tiles)
    chunk = h0.shape[0]
    at = pl.ds(pl.multiple_of(t * tile, tile), tile)

    @pl.when(t == 0)
    def _():
        bias_ref[...] = jnp.sum(up_ref[...].astype(F32), axis=0, keepdims=True)

    @pl.when(t < tiles)
    def _():
        total = dot_tn(h0[...], up_ref[:chunk, :])
        for k, h in enumerate((h1, h2, h3)):
            total = total + dot_tn(h[...], up_ref[(k + 1) * chunk : (k + 2) * chunk, :])
        acc[at, :] = total

    @pl.when(t >= tiles)
    def _():
        total = dot_tn(act_ref[:chunk, :], g0[...])
        for k, g in enumerate((g1, g2, g3)):
            total = total + dot_tn(act_ref[(k + 1) * chunk : (k + 2) * chunk, :], g[...])
        acc[at, :] = total

    @pl.when(t == 2 * tiles - 1)
    def _():
        split_out(b_ref, acc, keep_ref, send_ref)


def weigh_call(bid, hs, act, up, grads):
    chunk, width = hs[0].shape
    rows, hidden = act.shape
    tile = 256
    tiles = width // tile
    whole = lambda t, b: (0, 0)
    total = width + hidden
    half = jax.ShapeDtypeStruct((total // 2, width), BF)
    return pl.pallas_call(
        functools.partial(weigh_kernel, tiles),
        out_shape=(half, half, jax.ShapeDtypeStruct((1, hidden), F32)),
        grid_spec=pltpu.PrefetchScalarGridSpec(
            num_scalar_prefetch=1,
            grid=(2 * tiles,),
            in_specs=[pl.BlockSpec((chunk, tile), lambda t, b: (0, jnp.minimum(t, tiles - 1)))] * 4
            + [
                pl.BlockSpec((rows, tile), lambda t, b: (0, jnp.maximum(t - tiles, 0))),
                pl.BlockSpec((rows, hidden), whole),
            ]
            + [pl.BlockSpec((chunk, width), whole)] * 4,
            out_specs=[
                pl.BlockSpec(half.shape, whole),
                pl.BlockSpec(half.shape, whole),
                pl.BlockSpec((1, hidden), whole),
            ],
            scratch_shapes=[pltpu.VMEM((total, width), F32)],
        ),
        cost_estimate=cost(4 * rows * width * hidden, 12 * rows * width),
        name="weigh",
    )(bid, *hs, act, up, *grads)


def mix_kernel(m0, m1, m2, m3, p0, p1, p2, p3, x_ref, v_ref, resid_ref, h_ref):
    total = x_ref[...].astype(F32) + v_ref[2:3, :]
    for m, p in ((m0, p0), (m1, p1), (m2, p2), (m3, p3)):
        total = total + dot_nn(m[...], p[...])
    resid_ref[...] = total
    hat, _ = normalize(total)
    h_ref[...] = (hat * v_ref[3:4, :] + v_ref[4:5, :]).astype(BF)


def mix_call(parts, projs, x, vectors):
    rows, width = x.shape
    per = rows // BLK
    inner = parts[0].shape[1]
    low = pl.BlockSpec((BLK, inner), lambda t: (t, 0))
    high = pl.BlockSpec((BLK, inner), lambda t: (t + per, 0))
    whole = lambda t: (0, 0)
    return pl.pallas_call(
        mix_kernel,
        out_shape=(jax.ShapeDtypeStruct((rows, width), F32), jax.ShapeDtypeStruct((rows, width), BF)),
        grid=(per,),
        in_specs=[low, high, low, high]
        + [pl.BlockSpec(projs[0].shape, whole)] * 4
        + [pl.BlockSpec((BLK, width), lambda t: (t, 0)), pl.BlockSpec(vectors.shape, whole)],
        out_specs=[pl.BlockSpec((BLK, width), lambda t: (t, 0))] * 2,
        cost_estimate=cost(8 * rows * width * inner, 12 * rows * width),
        name="mix",
    )(*parts, *projs, x, vectors)


def turn_kernel(n_ref, s_ref, f_ref, resid_ref, cot_ref, v_ref, p0, p1, p2, p3, gr_ref, ga_ref, gn_ref, gf_ref, sum_ref):
    grad = n_ref[...].astype(F32) + s_ref[...].astype(F32) + f_ref[...].astype(F32)
    hat, rstd = normalize(resid_ref[...])
    cot = cot_ref[...].astype(F32)
    e = grad * v_ref[3:4, :]
    back = e - jnp.mean(e, axis=-1, keepdims=True) - hat * jnp.mean(e * hat, axis=-1, keepdims=True)
    grad_resid = cot + rstd * back
    gr_ref[...] = grad_resid
    att = grad_resid.astype(BF)
    ga_ref[...] = att
    gn_ref[0] = dot_nt(att, p0[...]).astype(BF)
    gn_ref[1] = dot_nt(att, p1[...]).astype(BF)
    gf_ref[0] = dot_nt(att, p2[...]).astype(BF)
    gf_ref[1] = dot_nt(att, p3[...]).astype(BF)

    @pl.when(pl.program_id(0) == 0)
    def _():
        sum_ref[...] = jnp.zeros_like(sum_ref)

    for k, v in enumerate((grad_resid, grad * hat, grad, cot)):
        sum_ref[k + 4 : k + 5, :] += jnp.sum(v, axis=0, keepdims=True)


def turn_call(near, swapped, far, resid, cot, vectors, projs):
    rows, width = resid.shape
    per = rows // BLK
    inner = projs[0].shape[0]
    low = pl.BlockSpec((BLK, width), lambda t: (t, 0))
    high = pl.BlockSpec((BLK, width), lambda t: (t + per, 0))
    whole = lambda t: (0, 0)
    pair = jax.ShapeDtypeStruct((2, rows, inner), BF)
    pair_spec = pl.BlockSpec((2, BLK, inner), lambda t: (0, t, 0))
    return pl.pallas_call(
        turn_kernel,
        out_shape=(
            jax.ShapeDtypeStruct((rows, width), F32),
            jax.ShapeDtypeStruct((rows, width), BF),
            pair,
            pair,
            jax.ShapeDtypeStruct((8, width), F32),
        ),
        grid=(per,),
        in_specs=[low, high, low, low, low, pl.BlockSpec(vectors.shape, whole)]
        + [pl.BlockSpec(projs[0].shape, whole)] * 4,
        out_specs=[low, low, pair_spec, pair_spec, pl.BlockSpec((8, width), whole)],
        cost_estimate=cost(8 * rows * width * inner, 20 * rows * width),
        name="turn",
    )(near, swapped, far, resid, cot, vectors, *projs)


def tally_kernel(steps, b_ref, gp_ref, hat_ref, w_ref, v_ref, pw_ref, up_ref, s_ref, keep_ref, send_ref, acc, col):
    t = pl.program_id(0)
    gp = gp_ref[...]
    cols = gp.shape[1]
    half = acc.shape[0] // 2

    @pl.when(t == 0)
    def _():
        acc[:cols, :] = jnp.zeros((cols, acc.shape[1]), F32)
        acc[cols:, :] = pw_ref[...]
        col[...] = jnp.zeros_like(col)

    acc[:cols, :] += dot_tn(gp, hat_ref[...])
    col[...] += dot_tn(gp, jnp.ones((gp.shape[0], 128), BF))

    @pl.when(t == steps - 1)
    def _():
        total = col[:, 0:1]
        moment = acc[:cols, :]
        w = w_ref[...].astype(F32)
        small = s_ref[...]
        row = lax.broadcasted_iota(jnp.int32, small.shape, 0)
        small = jnp.where(row == 0, jnp.sum(w * moment, axis=0, keepdims=True), small)
        small = jnp.where(row == 1, jnp.sum(w * total, axis=0, keepdims=True), small)
        bias = jnp.concatenate((col[...].T[0:1, :], jnp.zeros((1, small.shape[1] - cols), F32)), axis=1)
        small = jnp.where(row == 2, bias, small)
        small = jnp.where(row == 3, up_ref[...], small).astype(BF)
        acc[:cols, :] = moment * v_ref[0:1, :] + total * v_ref[1:2, :]
        split_out(b_ref, acc, keep_ref, send_ref)
        keep_ref[half:, :] = small
        send_ref[half:, :] = small


def tally_call(bid, gp, hat, w, vectors, proj_grad, up_grad, sums):
    rows, width = hat.shape
    cols = gp.shape[1]
    total = cols + proj_grad.shape[0]
    block = 2 * BLK
    steps = rows // block
    whole = lambda t, b: (0, 0)
    half = jax.ShapeDtypeStruct((total // 2 + sums.shape[0], width), BF)
    return pl.pallas_call(
        functools.partial(tally_kernel, steps),
        out_shape=(half, half),
        grid_spec=pltpu.PrefetchScalarGridSpec(
            num_scalar_prefetch=1,
            grid=(steps,),
            in_specs=[
                pl.BlockSpec((block, cols), lambda t, b: (t, 0)),
                pl.BlockSpec((block, width), lambda t, b: (t, 0)),
            ]
            + [pl.BlockSpec(v.shape, whole) for v in (w, vectors, proj_grad, up_grad, sums)],
            out_specs=[pl.BlockSpec(half.shape, whole)] * 2,
            scratch_shapes=[pltpu.VMEM((total, width), F32), pltpu.VMEM((cols, 128), F32)],
        ),
        cost_estimate=cost(cols, width),
        name="tally",
    )(bid, gp, hat, w, vectors, proj_grad, up_grad, sums)


def spread_kernel(steps, gp_ref, w_ref, near_ref, far_ref):
    t = pl.program_id(0)
    e = dot_nn(gp_ref[...], w_ref[...]).astype(BF)

    @pl.when(t < steps // 2)
    def _():
        near_ref[...] = e

    @pl.when(t >= steps // 2)
    def _():
        far_ref[...] = e


def spread_call(gp, w):
    rows, cols = gp.shape
    width = w.shape[1]
    block = 2 * BLK
    steps = rows // block
    return pl.pallas_call(
        functools.partial(spread_kernel, steps),
        out_shape=(jax.ShapeDtypeStruct((rows // 2, width), BF),) * 2,
        grid=(steps,),
        in_specs=[pl.BlockSpec((block, cols), lambda t: (t, 0)), pl.BlockSpec(w.shape, lambda t: (0, 0))],
        out_specs=[
            pl.BlockSpec((block, width), lambda t: (jnp.minimum(t, steps // 2 - 1), 0)),
            pl.BlockSpec((block, width), lambda t: (jnp.maximum(t - steps // 2, 0), 0)),
        ],
        cost_estimate=cost(cols, width),
        name="spread",
    )(gp, w)


def unpack_kernel(counts, parts, b_ref, *rest):
    acc = rest[-1]
    piece = acc.shape[0] // 8
    per = 8 // parts
    for spot, block in enumerate(spots(b_ref, 8)):
        at = spot % per * piece
        value = rest[spot // per][at : at + piece, :].astype(F32)
        acc[pl.ds(pl.multiple_of(block * piece, 8), piece), :] = value
    start = 0
    for out, count in zip(rest[parts:-1], counts, strict=True):
        out[...] = acc[start : start + count, :]
        start += count


def unpack_call(bid, parts, counts):
    total = sum(part.shape[0] for part in parts)
    width = parts[0].shape[1]
    vm = pl.BlockSpec(memory_space=pltpu.VMEM)
    return pl.pallas_call(
        functools.partial(unpack_kernel, counts, len(parts)),
        out_shape=tuple(jax.ShapeDtypeStruct((n, width), F32) for n in counts),
        in_specs=[pl.BlockSpec(memory_space=pltpu.SMEM)] + [vm] * len(parts),
        out_specs=[vm] * len(counts),
        scratch_shapes=[pltpu.VMEM((total, width), F32)],
        cost_estimate=cost(total, width),
        name="unpack",
    )(bid, *parts)


def tie(x, *needed):
    return lax.optimization_barrier((x,) + needed)[0]


def across(pieces):
    return [swap(piece, "batch", 2 * d) for d, piece in enumerate(pieces, 1)]


def sum_rest(x):
    for level in range(3, lax.axis_size("batch").bit_length() - 1):
        x = (x.astype(F32) + swap(x, "batch", 1 << level).astype(F32)).astype(x.dtype)
    return x


def fold(kept, got):
    piece = kept.shape[0] // 4
    total = kept[:piece].astype(F32)
    for g in got:
        total = total + g[:piece].astype(F32)
    return sum_rest(total.astype(BF))


def quarters(x):
    piece = x.shape[0] // 4
    return [x[d * piece : (d + 1) * piece] for d in range(1, 4)]


def sum_group(x):
    x = x + swap(x, "head", 1)
    return x + swap(x, "head", 2)


def per_device(
    inputs,
    lengths,
    cotangent,
    gain_attn,
    shift_attn,
    weight_qkv,
    bias_qkv,
    weight_proj,
    bias_proj,
    gain_mlp,
    shift_mlp,
    weight_up,
    bias_up,
    weight_down,
    bias_down,
):
    chunk, width = inputs.shape
    group_rows = chunk * lax.axis_size("head")
    heads, triple = weight_qkv.shape[1:]
    cols = heads * triple
    inner = cols // 3
    own = lax.axis_index("head")
    hid = own.astype(jnp.int32).reshape(1)
    bid = (lax.axis_index("batch") % 8).astype(jnp.int32).reshape(1)
    lens = lengths[0]
    live_rows = jnp.sum(lens[:-1])
    places = own * chunk + jnp.arange(chunk, dtype=jnp.int32)
    live = (places < live_rows)[:, None]
    qkv_t = weight_qkv.transpose(1, 2, 0).reshape(cols, width)
    proj = weight_proj.reshape(inner, width)
    zero = jnp.zeros((width,), F32)
    vectors = jnp.stack(
        (gain_attn, shift_attn, bias_proj, gain_mlp, shift_mlp, bias_up, bias_down, zero)
    )

    x_far = swap(inputs, "head", 2)
    x_near = swap(inputs, "head", 1)
    begun = qkv_call(hid, inputs, x_near, vectors, qkv_t, bias_qkv, 0, group_rows, ())
    x_far = tie(x_far, begun[0])
    x_last = swap(x_far, "head", 1)
    queries, keys, values, values_t, hats = qkv_call(
        hid, x_far, x_last, vectors, qkv_t, bias_qkv, 2, group_rows, begun
    )
    grad_own = jnp.where(live, cotangent, jnp.zeros_like(cotangent))
    grad_far = swap(tie(grad_own, x_far), "head", 2)
    proj_far = swap(tie(proj, x_far), "head", 2)
    projs = (proj, swap(proj, "head", 1), proj_far, swap(proj_far, "head", 1))

    merged_far, level_far = attend_call(lens, hid, queries, keys, values_t, 2, chunk)
    from_far = swap(merged_far, "head", 2)
    merged_near, level_near = attend_call(
        lens, hid, tie(queries, merged_far, grad_far), keys, values_t, 0, chunk
    )
    grads = (grad_own, swap(grad_own, "head", 1), grad_far, swap(grad_far, "head", 1))
    parts = (merged_near, swap(merged_near, "head", 1), from_far, swap(from_far, "head", 1))
    resid, h_own = mix_call(parts, projs, inputs, vectors)
    h_far = swap(h_own, "head", 2)
    h_near = swap(h_own, "head", 1)

    near = feed_call(h_own, h_near, grads[0], grads[1], weight_up, vectors, weight_down, 0, group_rows, ())
    h_far = tie(h_far, near[0])
    h_last = swap(h_far, "head", 1)
    act, grad_up, grad_norm_far, down_far = feed_call(
        h_far, h_last, grads[2], grads[3], weight_up, vectors, weight_down, 2, group_rows, near[:2]
    )
    swapped = swap(grad_norm_far, "head", 1)
    far_sum = (grad_norm_far[:chunk].astype(F32) + swapped[chunk:].astype(F32)).astype(BF)
    grad_far_sum = swap(far_sum, "head", 2)
    near_swapped = swap(near[2], "head", 1)
    down_swapped = swap(tie(down_far, far_sum), "head", 1)
    near_down = swap(tie(near[3], far_sum), "head", 1)

    keep_feed, send_feed, grad_bup = weigh_call(
        bid, (h_own, h_near, h_far, h_last), tie(act, far_sum), grad_up, grads
    )
    other_feed = swap(send_feed, "batch", 1)
    grad_resid, grad_att, grad_near, grad_cross, sums = turn_call(
        near[2], near_swapped, tie(grad_far_sum, grad_bup, down_swapped, near_down), resid, grad_own, vectors, projs
    )
    grad_near = grad_near.reshape(2 * chunk, inner)
    got = swap(grad_cross.reshape(2 * chunk, inner), "head", 2)
    grad_mate = swap(grad_near, "head", 1)
    grad_att = tie(grad_att, grad_mate)
    low = slice(0, chunk)
    high = slice(chunk, 2 * chunk)
    grad_proj = [
        dot_tn(p[at], grad_att) for p, at in zip(parts, (low, high, low, high), strict=True)
    ]
    near_sent, far_sent = grad_proj[1].astype(BF), grad_proj[3].astype(BF)
    down_far = tie(down_far, grad_att)
    down_sum = (down_far[:chunk].astype(F32) + down_swapped[chunk:].astype(F32)).astype(BF)
    got = tie(got, near_sent, far_sent, down_sum)
    merged_grads = (grad_near, grad_mate, got, swap(got, "head", 1))
    grad_near_proj = grad_proj[0] + swap(near_sent, "head", 1).astype(F32)
    far_proj = (grad_proj[2] + swap(far_sent, "head", 1).astype(F32)).astype(BF)
    far_proj = swap(far_proj, "head", 2)

    kept_feed = (keep_feed.astype(F32) + tie(other_feed, got).astype(F32)).astype(BF)
    got_feed = across(quarters(kept_feed))
    down_other = swap(tie(down_sum, kept_feed), "head", 2)

    grad_packed = attend_back_call(
        lens,
        hid,
        tie(queries, kept_feed, grad_near_proj),
        keys,
        values,
        merged_grads,
        (merged_near, merged_far),
        (level_near, level_far),
        chunk,
    )
    got_feed = [tie(g, grad_packed) for g in got_feed]
    grad_wproj = grad_near_proj + tie(far_proj, grad_packed).astype(F32)
    total_feed = fold(kept_feed, got_feed)
    gathered_feed = across([total_feed] * 3)
    keep, send = tally_call(
        bid, tie(grad_packed, total_feed, down_other), hats, qkv_t, vectors, grad_wproj, grad_bup, sums
    )
    other = swap(send, "batch", 1)
    e_near, e_far = spread_call(tie(grad_packed, keep), qkv_t)
    gathered_feed, e_near, e_far = lax.optimization_barrier((gathered_feed, e_near, e_far))

    feed_a = jnp.concatenate((total_feed, gathered_feed[0]), axis=0)
    feed_b = jnp.concatenate(gathered_feed[1:], axis=0)
    last_a = swap(feed_a, "batch", 1)
    summed = (keep.astype(F32) + tie(other, feed_a, feed_b).astype(F32)).astype(BF)
    kept, small = summed[:-8], summed[-8:]
    pieces = [jnp.concatenate((q, small), axis=0) for q in quarters(kept)]
    e_swapped = swap(tie(e_far, *pieces), "head", 1)
    e_sum = (e_far[:chunk].astype(F32) + e_swapped[chunk:].astype(F32)).astype(BF)
    got_attn = [tie(g, last_a, e_sum) for g in across(pieces)]

    tiny = [small.astype(F32)] + [g[-8:].astype(F32) for g in got_attn]
    small = sum_rest((tiny[0] + tiny[1]) + (tiny[2] + tiny[3]))
    total_attn = fold(kept, got_attn)
    gathered_attn = across([total_attn] * 3)
    last_b = swap(tie(feed_b, total_attn), "batch", 1)
    e_other = swap(tie(e_sum, total_attn), "head", 2)
    half = jnp.concatenate([total_attn] + [tie(g, last_b) for g in gathered_attn], axis=0)
    e_mate = swap(tie(e_near, half), "head", 1)
    last = swap(half, "batch", 1)
    biases = small[2:4]
    small = sum_group(tie(small, half))
    e_own = e_near[:chunk].astype(F32) + e_mate[chunk:].astype(F32) + tie(e_other, half).astype(F32)

    near_down = near[3][:chunk].astype(F32) + near_down[chunk:].astype(F32)
    output = (resid + near_down + tie(down_other, half).astype(F32) + bias_down).astype(BF)
    x_hat, x_rstd = normalize(tie(inputs, half).astype(F32))
    e_own = e_own * gain_attn
    grad_inputs = (
        grad_resid
        + x_rstd
        * (
            e_own
            - jnp.mean(e_own, axis=-1, keepdims=True)
            - x_hat * jnp.mean(e_own * x_hat, axis=-1, keepdims=True)
        )
    ).astype(BF)
    sum_wup, sum_wdown = unpack_call(bid, (feed_a, feed_b, last_a, tie(last_b, half)), (width, width))
    sum_wqkv, sum_wproj = unpack_call(bid, (half, tie(last, sum_wup, grad_inputs)), (cols, inner))
    return (
        output,
        grad_inputs,
        small[0],
        small[1],
        sum_wqkv.reshape(heads, triple, width).transpose(2, 0, 1),
        biases[0, :cols].reshape(heads, triple),
        sum_wproj.reshape(heads, inner // heads, width),
        small[4],
        small[5],
        small[6],
        sum_wup,
        biases[1],
        sum_wdown,
        small[7],
    )


def solution(mesh):
    rows = P(("batch", "head"), None)
    in_specs = (
        rows,
        P("batch", None),
        rows,
        P(),
        P(),
        P(None, "head", None),
        P("head", None),
        P("head", None, None),
        P(),
        P(),
        P(),
        P(None, "head"),
        P("head"),
        P("head", None),
        P(),
    )
    out_specs = (
        rows,
        rows,
        P(),
        P(),
        P(None, "head", None),
        P("head", None),
        P("head", None, None),
        P(),
        P(),
        P(),
        P(None, "head"),
        P("head"),
        P("head", None),
        P(),
    )
    return jax.shard_map(
        per_device, mesh=mesh, in_specs=in_specs, out_specs=out_specs, check_vma=False
    )
```

```python
import functools
import math

import jax
import jax.numpy as jnp
from jax import lax
from jax.experimental import pallas as pl
from jax.experimental.pallas import tpu as pltpu
from jax.sharding import PartitionSpec as P

F32 = jnp.float32
BF = jnp.bfloat16
BLK = 256
NEG = -1e30
EPS = 1e-05
GELU_C = math.sqrt(2.0 / math.pi)
GELU_A = 0.044715


def dot_nn(a, b):
    return lax.dot_general(a, b, (((1,), (0,)), ((), ())), preferred_element_type=F32)


def dot_nt(a, b):
    return lax.dot_general(a, b, (((1,), (1,)), ((), ())), preferred_element_type=F32)


def dot_tn(a, b):
    return lax.dot_general(a, b, (((0,), (0,)), ((), ())), preferred_element_type=F32)


def cost(flops, nbytes, trans=0):
    return pl.CostEstimate(flops=int(flops), bytes_accessed=int(nbytes), transcendentals=int(trans))


def swap(x, axis, bits):
    size = lax.axis_size(axis)
    return lax.ppermute(x, axis, [(i, i ^ bits) for i in range(size)])


def normalize(v):
    center = v - jnp.mean(v, axis=-1, keepdims=True)
    rstd = lax.rsqrt(jnp.mean(center * center, axis=-1, keepdims=True) + EPS)
    return center * rstd, rstd


def qkv_kernel(heads, hd, steps, h_ref, a_ref, b_ref, v_ref, w_ref, bias_ref, *rest):
    q_out, k_out, v_out, vt_out, hat_out = rest[-5:]
    t = pl.program_id(0)
    x = jnp.where(t < steps // 2, a_ref[...], b_ref[...]).astype(F32)
    xhat, _ = normalize(x)
    hat_out[...] = xhat.astype(BF)
    h1 = (xhat * v_ref[0:1, :] + v_ref[1:2, :]).astype(BF)
    bias = jnp.concatenate([bias_ref[h : h + 1, :] for h in range(heads)], axis=1)
    packed = (dot_nt(h1, w_ref[...]) + bias).astype(BF)
    for h in range(heads):
        o = 3 * hd * h
        q_out[h] = packed[:, o : o + hd]
        k_out[h] = packed[:, o + hd : o + 2 * hd]
        v = packed[:, o + 2 * hd : o + 3 * hd]
        v_out[h] = v
        vt_out[h] = v.T


def qkv_call(hid, a, b, vectors, w, bias, first, group_rows, before):
    rows, width = a.shape
    heads, triple = bias.shape
    hd = triple // 3
    per = rows // BLK
    steps = 2 * per
    place = lambda t, h: (h[0] ^ (first + t // per)) * per + t % per
    whole = lambda t, h: (0, 0)
    out_shape = tuple(
        jax.ShapeDtypeStruct(s, BF)
        for s in ((heads, group_rows, hd),) * 3 + ((heads, hd, group_rows), (group_rows, width))
    )
    in_specs = [
        pl.BlockSpec((BLK, width), lambda t, h: (jnp.minimum(t, per - 1), 0)),
        pl.BlockSpec((BLK, width), lambda t, h: (jnp.maximum(t - per, 0), 0)),
        pl.BlockSpec(vectors.shape, whole),
        pl.BlockSpec(w.shape, whole),
        pl.BlockSpec(bias.shape, whole),
    ] + [pl.BlockSpec(memory_space=pl.ANY)] * len(before)
    return pl.pallas_call(
        functools.partial(qkv_kernel, heads, hd, steps),
        out_shape=out_shape,
        grid_spec=pltpu.PrefetchScalarGridSpec(
            num_scalar_prefetch=1,
            grid=(steps,),
            in_specs=in_specs,
            out_specs=[pl.BlockSpec((heads, BLK, hd), lambda t, h: (0, place(t, h), 0))] * 3
            + [
                pl.BlockSpec((heads, hd, BLK), lambda t, h: (0, 0, place(t, h))),
                pl.BlockSpec((BLK, width), lambda t, h: (first * per + t, 0)),
            ],
        ),
        input_output_aliases={6 + i: i for i in range(len(before))},
        cost_estimate=cost(4 * rows * width * w.shape[0], 12 * rows * width),
        name="qkv",
    )(hid, a, b, vectors, w, bias, *before)


def row_segment(len_ref, row):
    low = row
    high = row + 1
    start = jnp.int32(0)
    for k in range(len_ref.shape[0] - 1):
        stop = start + len_ref[k]
        inside = (row >= start) & (row < stop)
        low = jnp.where(inside, start, low)
        high = jnp.where(inside, stop, high)
        start = stop
    return low, high


def lane_starts(len_ref, row, width):
    i = row + lax.broadcasted_iota(jnp.int32, (1, width), 1)
    start = jnp.zeros((1, width), jnp.int32)
    stop = jnp.int32(0)
    for k in range(len_ref.shape[0] - 1):
        stop = stop + len_ref[k]
        start = jnp.where(i >= stop, stop, start)
    return jnp.where(i >= stop, i, start), i


def attend_kernel(heads, first, per, scale, len_ref, h_ref, q_ref, k_ref, vt_ref, o_ref, l_ref, m_s, z_s, acc_s):
    t = pl.program_id(0)
    row = ((h_ref[0] ^ (first + t // per)) * per + t % per) * BLK
    start, i = lane_starts(len_ref, row, BLK)
    low, _ = row_segment(len_ref, row)
    m_s[...] = jnp.full_like(m_s, NEG)
    z_s[...] = jnp.zeros_like(z_s)
    acc_s[...] = jnp.zeros_like(acc_s)
    qs = [q_ref[h] * jnp.asarray(scale, BF) for h in range(heads)]

    def body(jb, carry):
        j0 = pl.multiple_of(jb * BLK, BLK)
        j = j0 + lax.broadcasted_iota(jnp.int32, (BLK, BLK), 0)
        mask = (j >= start) & (j <= i)
        for h in range(heads):
            s = dot_nt(k_ref[h, pl.ds(j0, BLK), :], qs[h])
            magnitude = jnp.where(mask, jnp.abs(s), NEG)
            old = m_s[h : h + 1, :]
            top = jnp.maximum(old, jnp.max(magnitude, axis=0, keepdims=True))
            decay = jnp.exp(old - top)
            e = jnp.exp(magnitude - top)
            z_s[h : h + 1, :] = z_s[h : h + 1, :] * decay + jnp.sum(e, axis=0, keepdims=True)
            m_s[h : h + 1, :] = top
            u = e - jnp.where(mask, jnp.exp(-top), 0.0)
            w = jnp.where(s < 0, -u, u).astype(BF)
            acc_s[h] = acc_s[h] * decay + dot_nn(vt_ref[h, :, pl.ds(j0, BLK)], w)
        return carry

    lax.fori_loop(low // BLK, row // BLK + 1, body, 0)
    outs = []
    for h in range(heads):
        z = z_s[h : h + 1, :]
        outs.append((acc_s[h] / z).T)
        l_ref[h : h + 1, :] = m_s[h : h + 1, :] + jnp.log(z)
    o_ref[...] = jnp.concatenate(outs, axis=1).astype(BF)


def attend_call(lengths, hid, q, k, vt, first, chunk):
    heads, rows, hd = q.shape
    per = chunk // BLK
    steps = 2 * per
    place = lambda t, n, h: (0, (h[0] ^ (first + t // per)) * per + t % per, 0)
    whole = lambda t, n, h: (0, 0, 0)
    return pl.pallas_call(
        functools.partial(attend_kernel, heads, first, per, 1.0 / math.sqrt(hd)),
        out_shape=(
            jax.ShapeDtypeStruct((steps * BLK, heads * hd), BF),
            jax.ShapeDtypeStruct((8, steps * BLK), F32),
        ),
        grid_spec=pltpu.PrefetchScalarGridSpec(
            num_scalar_prefetch=2,
            grid=(steps,),
            in_specs=[
                pl.BlockSpec((heads, BLK, hd), place),
                pl.BlockSpec((heads, rows, hd), whole),
                pl.BlockSpec((heads, hd, rows), whole),
            ],
            out_specs=[
                pl.BlockSpec((BLK, heads * hd), lambda t, n, h: (t, 0)),
                pl.BlockSpec((8, BLK), lambda t, n, h: (0, t)),
            ],
            scratch_shapes=[
                pltpu.VMEM((8, BLK), F32),
                pltpu.VMEM((8, BLK), F32),
                pltpu.VMEM((heads, hd, BLK), F32),
            ],
        ),
        cost_estimate=cost(heads * rows * rows * hd * 4, 12 * rows * heads * hd, heads * rows * rows // 4),
        name="attend",
    )(lengths, hid, q, k, vt)


def attend_back_kernel(chunk, scale, len_ref, h_ref, q_ref, k_ref, v_ref, *rest):
    g_refs, o_refs, l_refs = rest[0:4], rest[4:6], rest[6:8]
    gp_ref, q_s, g_s, kt_s, l_s, c_s, d_s, dq_s, dk_s, dv_s = rest[8:]
    heads, rows, hd = q_ref.shape
    blocks = rows // BLK
    per = chunk // BLK
    own = h_ref[0]
    for c in range(4):
        r0 = pl.multiple_of((own ^ c) * chunk, chunk)
        part = slice((c % 2) * chunk, (c % 2 + 1) * chunk)
        g = g_refs[c][...]
        o = o_refs[c // 2][part, :]
        for h in range(heads):
            gh = g[:, h * hd : (h + 1) * hd]
            g_s[h, pl.ds(r0, chunk), :] = gh
            both = gh.astype(F32) * o[:, h * hd : (h + 1) * hd].astype(F32)
            d_s[h : h + 1, pl.ds(r0, chunk)] = jnp.sum(both.T, axis=0, keepdims=True)
        level = l_refs[c // 2][:, part]
        l_s[:, pl.ds(r0, chunk)] = level
        c_s[:, pl.ds(r0, chunk)] = jnp.exp(-level)
    for h in range(heads):
        q_s[h] = q_ref[h] * jnp.asarray(scale, BF)
    dq_s[...] = jnp.zeros_like(dq_s)

    def out_row(block):
        return pl.multiple_of(((own ^ (block // per)) * per + block % per) * BLK, BLK)

    def outer(jb, carry):
        j0 = pl.multiple_of(jb * BLK, BLK)
        dk_s[...] = jnp.zeros_like(dk_s)
        dv_s[...] = jnp.zeros_like(dv_s)
        for h in range(heads):
            kt_s[h] = k_ref[h, pl.ds(j0, BLK), :].T
        _, stop = row_segment(len_ref, j0 + BLK - 1)
        j = j0 + lax.broadcasted_iota(jnp.int32, (BLK, BLK), 0)

        def inner(ib, carry):
            i0 = pl.multiple_of(ib * BLK, BLK)
            start, i = lane_starts(len_ref, i0, BLK)
            mask = (j >= start) & (j <= i)
            for h in range(heads):
                qh = q_s[h, pl.ds(i0, BLK), :]
                gh = g_s[h, pl.ds(i0, BLK), :]
                s = dot_nt(k_ref[h, pl.ds(j0, BLK), :], qh)
                gw = dot_nt(v_ref[h, pl.ds(j0, BLK), :], gh)
                level = l_s[h : h + 1, pl.ds(i0, BLK)]
                offset = c_s[h : h + 1, pl.ds(i0, BLK)]
                d = d_s[h : h + 1, pl.ds(i0, BLK)]
                p = jnp.exp(jnp.where(mask, jnp.abs(s), NEG) - level)
                u = p - jnp.where(mask, offset, 0.0)
                minus = s < 0
                w = jnp.where(minus, -u, u).astype(BF)
                signed = jnp.where(minus, -d, jnp.where(s == 0, 0.0, d))
                gs = (p * (gw - signed)).astype(BF)
                dv_s[h] += dot_nn(w, gh)
                dk_s[h] += dot_nn(gs, qh)
                dq_s[h, :, pl.ds(i0, BLK)] += dot_nn(kt_s[h], gs)
            return carry

        lax.fori_loop(jb, (stop - 1) // BLK + 1, inner, 0)
        for h in range(heads):
            at = pl.ds(out_row(jb), BLK)
            gp_ref[at, (3 * h + 1) * hd : (3 * h + 2) * hd] = dk_s[h].astype(BF)
            gp_ref[at, (3 * h + 2) * hd : (3 * h + 3) * hd] = dv_s[h].astype(BF)
        return carry

    lax.fori_loop(0, blocks, outer, 0)

    def finish(ib, carry):
        i0 = pl.multiple_of(ib * BLK, BLK)
        for h in range(heads):
            dq = (dq_s[h, :, pl.ds(i0, BLK)] * scale).T.astype(BF)
            gp_ref[pl.ds(out_row(ib), BLK), 3 * h * hd : (3 * h + 1) * hd] = dq
        return carry

    lax.fori_loop(0, blocks, finish, 0)


def attend_back_call(lengths, hid, q, k, v, grads, outs, levels, chunk):
    heads, rows, hd = q.shape
    vm = pl.BlockSpec(memory_space=pltpu.VMEM)
    sm = pl.BlockSpec(memory_space=pltpu.SMEM)
    return pl.pallas_call(
        functools.partial(attend_back_kernel, chunk, 1.0 / math.sqrt(hd)),
        out_shape=jax.ShapeDtypeStruct((rows, heads * 3 * hd), BF),
        in_specs=[sm, sm] + [vm] * 11,
        out_specs=vm,
        scratch_shapes=[
            pltpu.VMEM((heads, rows, hd), BF),
            pltpu.VMEM((heads, rows, hd), BF),
            pltpu.VMEM((heads, hd, BLK), BF),
            pltpu.VMEM((8, rows), F32),
            pltpu.VMEM((8, rows), F32),
            pltpu.VMEM((8, rows), F32),
            pltpu.VMEM((heads, hd, rows), F32),
            pltpu.VMEM((heads, BLK, hd), F32),
            pltpu.VMEM((heads, BLK, hd), F32),
        ],
        cost_estimate=cost(heads * rows * rows * hd * 20, 30 * rows * heads * hd, heads * rows * rows // 2),
        name="attend_back",
    )(lengths, hid, q, k, v, *grads, *outs, *levels)


def feed_kernel(steps, ha_ref, hb_ref, ga_ref, gb_ref, up_ref, v_ref, down_ref, *rest):
    act_ref, gup_ref, gna_ref, gnb_ref, outa_ref, outb_ref = rest[-6:]
    early = pl.program_id(0) < steps // 2
    h2 = jnp.where(early, ha_ref[...], hb_ref[...])
    grad = jnp.where(early, ga_ref[...], gb_ref[...])
    u = dot_nn(h2, up_ref[...]) + v_ref[5:6, :]
    square = u * u
    tanh = jnp.tanh(u * (GELU_C + (GELU_C * GELU_A) * square))
    half = 0.5 * (1.0 + tanh)
    act = (u * half).astype(BF)
    slope = half + (0.5 * u) * (1.0 - tanh * tanh) * (GELU_C + (3.0 * GELU_C * GELU_A) * square)
    gup = (dot_nt(grad, down_ref[...]) * slope).astype(BF)
    act_ref[...] = act
    gup_ref[...] = gup
    gn = dot_nt(gup, up_ref[...]).astype(BF)
    out = dot_nn(act, down_ref[...]).astype(BF)

    @pl.when(early)
    def _():
        gna_ref[...] = gn
        outa_ref[...] = out

    @pl.when(jnp.logical_not(early))
    def _():
        gnb_ref[...] = gn
        outb_ref[...] = out


def feed_call(ha, hb, ga, gb, up, vectors, down, first, group_rows, before):
    rows, width = ha.shape
    hidden = up.shape[1]
    per = rows // BLK
    steps = 2 * per
    whole = lambda t: (0, 0)
    early = pl.BlockSpec((BLK, width), lambda t: (jnp.minimum(t, per - 1), 0))
    late = pl.BlockSpec((BLK, width), lambda t: (jnp.maximum(t - per, 0), 0))
    return pl.pallas_call(
        functools.partial(feed_kernel, steps),
        out_shape=(
            jax.ShapeDtypeStruct((group_rows, hidden), BF),
            jax.ShapeDtypeStruct((group_rows, hidden), BF),
        )
        + (jax.ShapeDtypeStruct((rows, width), BF),) * 4,
        grid=(steps,),
        in_specs=[
            early,
            late,
            early,
            late,
            pl.BlockSpec(up.shape, whole),
            pl.BlockSpec(vectors.shape, whole),
            pl.BlockSpec(down.shape, whole),
        ]
        + [pl.BlockSpec(memory_space=pl.ANY)] * len(before),
        out_specs=[
            pl.BlockSpec((BLK, hidden), lambda t: (first * per + t, 0)),
            pl.BlockSpec((BLK, hidden), lambda t: (first * per + t, 0)),
            early,
            late,
            early,
            late,
        ],
        input_output_aliases={7 + i: i for i in range(len(before))},
        cost_estimate=cost(16 * rows * width * hidden, 16 * rows * width, 2 * rows * hidden),
        name="feed",
    )(ha, hb, ga, gb, up, vectors, down, *before)


def spots(b_ref, pieces):
    return [b_ref[0] ^ (2 * (spot % 4) + spot // 4) for spot in range(pieces)]


def split_out(b_ref, acc, keep_ref, send_ref):
    piece = acc.shape[0] // 8
    for spot, block in enumerate(spots(b_ref, 8)):
        out = keep_ref if spot < 4 else send_ref
        value = acc[pl.ds(pl.multiple_of(block * piece, 8), piece), :]
        out[(spot % 4) * piece : (spot % 4 + 1) * piece, :] = value.astype(BF)


def weigh_kernel(tiles, b_ref, h0, h1, h2, h3, act_ref, up_ref, g0, g1, g2, g3, keep_ref, send_ref, bias_ref, acc):
    t = pl.program_id(0)
    tile = acc.shape[0] // (2 * tiles)
    chunk = h0.shape[0]
    at = pl.ds(pl.multiple_of(t * tile, tile), tile)

    @pl.when(t == 0)
    def _():
        bias_ref[...] = jnp.sum(up_ref[...].astype(F32), axis=0, keepdims=True)

    @pl.when(t < tiles)
    def _():
        total = dot_tn(h0[...], up_ref[:chunk, :])
        for k, h in enumerate((h1, h2, h3)):
            total = total + dot_tn(h[...], up_ref[(k + 1) * chunk : (k + 2) * chunk, :])
        acc[at, :] = total

    @pl.when(t >= tiles)
    def _():
        total = dot_tn(act_ref[:chunk, :], g0[...])
        for k, g in enumerate((g1, g2, g3)):
            total = total + dot_tn(act_ref[(k + 1) * chunk : (k + 2) * chunk, :], g[...])
        acc[at, :] = total

    @pl.when(t == 2 * tiles - 1)
    def _():
        split_out(b_ref, acc, keep_ref, send_ref)


def weigh_call(bid, hs, act, up, grads):
    chunk, width = hs[0].shape
    rows, hidden = act.shape
    tile = 256
    tiles = width // tile
    whole = lambda t, b: (0, 0)
    total = width + hidden
    half = jax.ShapeDtypeStruct((total // 2, width), BF)
    return pl.pallas_call(
        functools.partial(weigh_kernel, tiles),
        out_shape=(half, half, jax.ShapeDtypeStruct((1, hidden), F32)),
        grid_spec=pltpu.PrefetchScalarGridSpec(
            num_scalar_prefetch=1,
            grid=(2 * tiles,),
            in_specs=[pl.BlockSpec((chunk, tile), lambda t, b: (0, jnp.minimum(t, tiles - 1)))] * 4
            + [
                pl.BlockSpec((rows, tile), lambda t, b: (0, jnp.maximum(t - tiles, 0))),
                pl.BlockSpec((rows, hidden), whole),
            ]
            + [pl.BlockSpec((chunk, width), whole)] * 4,
            out_specs=[
                pl.BlockSpec(half.shape, whole),
                pl.BlockSpec(half.shape, whole),
                pl.BlockSpec((1, hidden), whole),
            ],
            scratch_shapes=[pltpu.VMEM((total, width), F32)],
        ),
        cost_estimate=cost(4 * rows * width * hidden, 12 * rows * width),
        name="weigh",
    )(bid, *hs, act, up, *grads)


def mix_kernel(m0, m1, m2, m3, p0, p1, p2, p3, x_ref, v_ref, resid_ref, h_ref):
    total = x_ref[...].astype(F32) + v_ref[2:3, :]
    for m, p in ((m0, p0), (m1, p1), (m2, p2), (m3, p3)):
        total = total + dot_nn(m[...], p[...])
    resid_ref[...] = total
    hat, _ = normalize(total)
    h_ref[...] = (hat * v_ref[3:4, :] + v_ref[4:5, :]).astype(BF)


def mix_call(parts, projs, x, vectors):
    rows, width = x.shape
    per = rows // BLK
    inner = parts[0].shape[1]
    low = pl.BlockSpec((BLK, inner), lambda t: (t, 0))
    high = pl.BlockSpec((BLK, inner), lambda t: (t + per, 0))
    whole = lambda t: (0, 0)
    return pl.pallas_call(
        mix_kernel,
        out_shape=(jax.ShapeDtypeStruct((rows, width), F32), jax.ShapeDtypeStruct((rows, width), BF)),
        grid=(per,),
        in_specs=[low, high, low, high]
        + [pl.BlockSpec(projs[0].shape, whole)] * 4
        + [pl.BlockSpec((BLK, width), lambda t: (t, 0)), pl.BlockSpec(vectors.shape, whole)],
        out_specs=[pl.BlockSpec((BLK, width), lambda t: (t, 0))] * 2,
        cost_estimate=cost(8 * rows * width * inner, 12 * rows * width),
        name="mix",
    )(*parts, *projs, x, vectors)


def turn_kernel(n_ref, s_ref, f_ref, resid_ref, cot_ref, v_ref, p0, p1, p2, p3, gr_ref, ga_ref, g0, g1, g2, g3, sum_ref):
    grad = n_ref[...].astype(F32) + s_ref[...].astype(F32) + f_ref[...].astype(F32)
    hat, rstd = normalize(resid_ref[...])
    cot = cot_ref[...].astype(F32)
    e = grad * v_ref[3:4, :]
    back = e - jnp.mean(e, axis=-1, keepdims=True) - hat * jnp.mean(e * hat, axis=-1, keepdims=True)
    grad_resid = cot + rstd * back
    gr_ref[...] = grad_resid
    att = grad_resid.astype(BF)
    ga_ref[...] = att
    for g, p in ((g0, p0), (g1, p1), (g2, p2), (g3, p3)):
        g[...] = dot_nt(att, p[...]).astype(BF)

    @pl.when(pl.program_id(0) == 0)
    def _():
        sum_ref[...] = jnp.zeros_like(sum_ref)

    for k, v in enumerate((grad_resid, grad * hat, grad, cot)):
        sum_ref[k + 4 : k + 5, :] += jnp.sum(v, axis=0, keepdims=True)


def turn_call(near, swapped, far, resid, cot, vectors, projs):
    rows, width = resid.shape
    per = rows // BLK
    inner = projs[0].shape[0]
    low = pl.BlockSpec((BLK, width), lambda t: (t, 0))
    whole = lambda t: (0, 0)
    return pl.pallas_call(
        turn_kernel,
        out_shape=(
            jax.ShapeDtypeStruct((rows, width), F32),
            jax.ShapeDtypeStruct((rows, width), BF),
        )
        + (jax.ShapeDtypeStruct((rows, inner), BF),) * 4
        + (jax.ShapeDtypeStruct((8, width), F32),),
        grid=(per,),
        in_specs=[low] * 5
        + [pl.BlockSpec(vectors.shape, whole)]
        + [pl.BlockSpec(projs[0].shape, whole)] * 4,
        out_specs=[low, low]
        + [pl.BlockSpec((BLK, inner), lambda t: (t, 0))] * 4
        + [pl.BlockSpec((8, width), whole)],
        cost_estimate=cost(rows, width),
        name="turn",
    )(near, swapped, far, resid, cot, vectors, *projs)


def tally_kernel(steps, b_ref, gp_ref, hat_ref, w_ref, v_ref, pw_ref, up_ref, s_ref, keep_ref, send_ref, acc, col):
    t = pl.program_id(0)
    gp = gp_ref[...]
    cols = gp.shape[1]
    half = acc.shape[0] // 2

    @pl.when(t == 0)
    def _():
        acc[:cols, :] = jnp.zeros((cols, acc.shape[1]), F32)
        acc[cols:, :] = pw_ref[...]
        col[...] = jnp.zeros_like(col)

    acc[:cols, :] += dot_tn(gp, hat_ref[...])
    col[...] += dot_tn(gp, jnp.ones((gp.shape[0], 128), BF))

    @pl.when(t == steps - 1)
    def _():
        total = col[:, 0:1]
        moment = acc[:cols, :]
        w = w_ref[...].astype(F32)
        small = s_ref[...]
        row = lax.broadcasted_iota(jnp.int32, small.shape, 0)
        small = jnp.where(row == 0, jnp.sum(w * moment, axis=0, keepdims=True), small)
        small = jnp.where(row == 1, jnp.sum(w * total, axis=0, keepdims=True), small)
        bias = jnp.concatenate((col[...].T[0:1, :], jnp.zeros((1, small.shape[1] - cols), F32)), axis=1)
        small = jnp.where(row == 2, bias, small)
        small = jnp.where(row == 3, up_ref[...], small).astype(BF)
        acc[:cols, :] = moment * v_ref[0:1, :] + total * v_ref[1:2, :]
        split_out(b_ref, acc, keep_ref, send_ref)
        keep_ref[half:, :] = small
        send_ref[half:, :] = small


def tally_call(bid, gp, hat, w, vectors, proj_grad, up_grad, sums):
    rows, width = hat.shape
    cols = gp.shape[1]
    total = cols + proj_grad.shape[0]
    block = 2 * BLK
    steps = rows // block
    whole = lambda t, b: (0, 0)
    half = jax.ShapeDtypeStruct((total // 2 + sums.shape[0], width), BF)
    return pl.pallas_call(
        functools.partial(tally_kernel, steps),
        out_shape=(half, half),
        grid_spec=pltpu.PrefetchScalarGridSpec(
            num_scalar_prefetch=1,
            grid=(steps,),
            in_specs=[
                pl.BlockSpec((block, cols), lambda t, b: (t, 0)),
                pl.BlockSpec((block, width), lambda t, b: (t, 0)),
            ]
            + [pl.BlockSpec(v.shape, whole) for v in (w, vectors, proj_grad, up_grad, sums)],
            out_specs=[pl.BlockSpec(half.shape, whole)] * 2,
            scratch_shapes=[pltpu.VMEM((total, width), F32), pltpu.VMEM((cols, 128), F32)],
        ),
        cost_estimate=cost(cols, width),
        name="tally",
    )(bid, gp, hat, w, vectors, proj_grad, up_grad, sums)


def spread_kernel(gp_ref, w_ref, *outs):
    e = dot_nn(gp_ref[...], w_ref[...]).astype(BF)
    for k, out in enumerate(outs):

        @pl.when(pl.program_id(0) == k)
        def _(out=out):
            out[...] = e


def spread_call(gp, w, chunk):
    cols, width = w.shape
    whole = lambda t: (0, 0)
    return pl.pallas_call(
        spread_kernel,
        out_shape=(jax.ShapeDtypeStruct((chunk, width), BF),) * 4,
        grid=(4,),
        in_specs=[pl.BlockSpec((chunk, cols), lambda t: (t, 0)), pl.BlockSpec(w.shape, whole)],
        out_specs=[pl.BlockSpec((chunk, width), whole)] * 4,
        cost_estimate=cost(cols, width),
        name="spread",
    )(gp, w)


def unpack_kernel(counts, parts, b_ref, *rest):
    acc = rest[-1]
    piece = acc.shape[0] // 8
    per = 8 // parts
    for spot, block in enumerate(spots(b_ref, 8)):
        at = spot % per * piece
        value = rest[spot // per][at : at + piece, :].astype(F32)
        acc[pl.ds(pl.multiple_of(block * piece, 8), piece), :] = value
    start = 0
    for out, count in zip(rest[parts:-1], counts, strict=True):
        out[...] = acc[start : start + count, :]
        start += count


def unpack_call(bid, parts, counts):
    total = sum(part.shape[0] for part in parts)
    width = parts[0].shape[1]
    vm = pl.BlockSpec(memory_space=pltpu.VMEM)
    return pl.pallas_call(
        functools.partial(unpack_kernel, counts, len(parts)),
        out_shape=tuple(jax.ShapeDtypeStruct((n, width), F32) for n in counts),
        in_specs=[pl.BlockSpec(memory_space=pltpu.SMEM)] + [vm] * len(parts),
        out_specs=[vm] * len(counts),
        scratch_shapes=[pltpu.VMEM((total, width), F32)],
        cost_estimate=cost(total, width),
        name="unpack",
    )(bid, *parts)


def tie(x, *needed):
    return lax.optimization_barrier((x,) + needed)[0]


def across(pieces):
    return [swap(piece, "batch", 2 * d) for d, piece in enumerate(pieces, 1)]


def sum_rest(x):
    for level in range(3, lax.axis_size("batch").bit_length() - 1):
        x = (x.astype(F32) + swap(x, "batch", 1 << level).astype(F32)).astype(x.dtype)
    return x


def fold(kept, got):
    piece = kept.shape[0] // 4
    total = kept[:piece].astype(F32)
    for g in got:
        total = total + g[:piece].astype(F32)
    return sum_rest(total.astype(BF))


def quarters(x):
    piece = x.shape[0] // 4
    return [x[d * piece : (d + 1) * piece] for d in range(1, 4)]


def sum_group(x):
    x = x + swap(x, "head", 1)
    return x + swap(x, "head", 2)


def per_device(
    inputs,
    lengths,
    cotangent,
    gain_attn,
    shift_attn,
    weight_qkv,
    bias_qkv,
    weight_proj,
    bias_proj,
    gain_mlp,
    shift_mlp,
    weight_up,
    bias_up,
    weight_down,
    bias_down,
):
    chunk, width = inputs.shape
    group_rows = chunk * lax.axis_size("head")
    heads, triple = weight_qkv.shape[1:]
    cols = heads * triple
    inner = cols // 3
    own = lax.axis_index("head")
    hid = own.astype(jnp.int32).reshape(1)
    bid = (lax.axis_index("batch") % 8).astype(jnp.int32).reshape(1)
    lens = lengths[0]
    live_rows = jnp.sum(lens[:-1])
    places = own * chunk + jnp.arange(chunk, dtype=jnp.int32)
    live = (places < live_rows)[:, None]
    qkv_t = weight_qkv.transpose(1, 2, 0).reshape(cols, width)
    proj = weight_proj.reshape(inner, width)
    zero = jnp.zeros((width,), F32)
    vectors = jnp.stack(
        (gain_attn, shift_attn, bias_proj, gain_mlp, shift_mlp, bias_up, bias_down, zero)
    )

    x_far = swap(inputs, "head", 2)
    x_near = swap(inputs, "head", 1)
    begun = qkv_call(hid, inputs, x_near, vectors, qkv_t, bias_qkv, 0, group_rows, ())
    x_far = tie(x_far, begun[0])
    x_last = swap(x_far, "head", 1)
    queries, keys, values, values_t, hats = qkv_call(
        hid, x_far, x_last, vectors, qkv_t, bias_qkv, 2, group_rows, begun
    )
    grad_own = jnp.where(live, cotangent, jnp.zeros_like(cotangent))
    grad_far = swap(tie(grad_own, x_far), "head", 2)
    proj_far = swap(tie(proj, x_far), "head", 2)
    projs = (proj, swap(proj, "head", 1), proj_far, swap(proj_far, "head", 1))

    merged_far, level_far = attend_call(lens, hid, queries, keys, values_t, 2, chunk)
    from_far = swap(merged_far, "head", 2)
    merged_near, level_near = attend_call(
        lens, hid, tie(queries, merged_far, grad_far), keys, values_t, 0, chunk
    )
    grads = (grad_own, swap(grad_own, "head", 1), grad_far, swap(grad_far, "head", 1))
    parts = (merged_near, swap(merged_near, "head", 1), from_far, swap(from_far, "head", 1))
    resid, h_own = mix_call(parts, projs, inputs, vectors)
    h_far = swap(h_own, "head", 2)
    h_near = swap(h_own, "head", 1)

    near = feed_call(h_own, h_near, grads[0], grads[1], weight_up, vectors, weight_down, 0, group_rows, ())
    h_far = tie(h_far, near[0])
    h_last = swap(h_far, "head", 1)
    act, grad_up, norm_far, norm_last, down_far, down_last = feed_call(
        h_far, h_last, grads[2], grads[3], weight_up, vectors, weight_down, 2, group_rows, near[:2]
    )
    far_sum = (norm_far.astype(F32) + swap(norm_last, "head", 1).astype(F32)).astype(BF)
    grad_far_sum = swap(far_sum, "head", 2)
    near_swapped = swap(near[3], "head", 1)
    down_swapped = swap(tie(down_last, far_sum), "head", 1)
    near_down = swap(tie(near[5], far_sum), "head", 1)

    keep_feed, send_feed, grad_bup = weigh_call(
        bid, (h_own, h_near, h_far, h_last), tie(act, far_sum), grad_up, grads
    )
    other_feed = swap(send_feed, "batch", 1)
    grad_resid, grad_att, grad_near, grad_mate, grad_cross, grad_last, sums = turn_call(
        near[2],
        near_swapped,
        tie(grad_far_sum, grad_bup, down_swapped, near_down),
        resid,
        grad_own,
        vectors,
        projs,
    )
    got_last = swap(grad_last, "head", 2)
    got = swap(grad_cross, "head", 2)
    grad_mate = swap(grad_mate, "head", 1)
    grad_att = tie(grad_att, grad_mate)
    low = slice(0, chunk)
    high = slice(chunk, 2 * chunk)
    grad_proj = [
        dot_tn(p[at], grad_att) for p, at in zip(parts, (low, high, low, high), strict=True)
    ]
    near_sent, far_sent = grad_proj[1].astype(BF), grad_proj[3].astype(BF)
    down_far = tie(down_far, grad_att)
    down_sum = (down_far.astype(F32) + down_swapped.astype(F32)).astype(BF)
    got_last = tie(got_last, near_sent, far_sent, down_sum)
    merged_grads = (grad_near, grad_mate, got, swap(got_last, "head", 1))
    grad_near_proj = grad_proj[0] + swap(near_sent, "head", 1).astype(F32)
    far_proj = (grad_proj[2] + swap(far_sent, "head", 1).astype(F32)).astype(BF)
    far_proj = swap(far_proj, "head", 2)

    kept_feed = (keep_feed.astype(F32) + tie(other_feed, got).astype(F32)).astype(BF)
    got_feed = across(quarters(kept_feed))
    down_other = swap(tie(down_sum, kept_feed), "head", 2)

    grad_packed = attend_back_call(
        lens,
        hid,
        tie(queries, kept_feed, grad_near_proj),
        keys,
        values,
        merged_grads,
        (merged_near, merged_far),
        (level_near, level_far),
        chunk,
    )
    got_feed = [tie(g, grad_packed) for g in got_feed]
    grad_wproj = grad_near_proj + tie(far_proj, grad_packed).astype(F32)
    total_feed = fold(kept_feed, got_feed)
    gathered_feed = across([total_feed] * 3)
    keep, send = tally_call(
        bid, tie(grad_packed, total_feed, down_other), hats, qkv_t, vectors, grad_wproj, grad_bup, sums
    )
    other = swap(send, "batch", 1)
    spread = spread_call(tie(grad_packed, keep), qkv_t, chunk)
    gathered_feed, spread = lax.optimization_barrier((gathered_feed, spread))
    e_own, e_near, e_far, e_last = spread

    feed_a = jnp.concatenate((total_feed, gathered_feed[0]), axis=0)
    feed_b = jnp.concatenate(gathered_feed[1:], axis=0)
    last_a = swap(feed_a, "batch", 1)
    summed = (keep.astype(F32) + tie(other, feed_a, feed_b).astype(F32)).astype(BF)
    kept, small = summed[:-8], summed[-8:]
    pieces = [jnp.concatenate((q, small), axis=0) for q in quarters(kept)]
    e_swapped = swap(tie(e_last, *pieces), "head", 1)
    e_sum = (e_far.astype(F32) + e_swapped.astype(F32)).astype(BF)
    got_attn = [tie(g, last_a, e_sum) for g in across(pieces)]

    tiny = [small.astype(F32)] + [g[-8:].astype(F32) for g in got_attn]
    small = sum_rest((tiny[0] + tiny[1]) + (tiny[2] + tiny[3]))
    total_attn = fold(kept, got_attn)
    gathered_attn = across([total_attn] * 3)
    last_b = swap(tie(feed_b, total_attn), "batch", 1)
    e_other = swap(tie(e_sum, total_attn), "head", 2)
    half = jnp.concatenate([total_attn] + [tie(g, last_b) for g in gathered_attn], axis=0)
    e_mate = swap(tie(e_near, half), "head", 1)
    last = swap(half, "batch", 1)
    biases = small[2:4]
    small = sum_group(tie(small, half))
    e_own = e_own.astype(F32) + e_mate.astype(F32) + tie(e_other, half).astype(F32)

    near_down = near[4].astype(F32) + near_down.astype(F32)
    output = (resid + near_down + tie(down_other, half).astype(F32) + bias_down).astype(BF)
    x_hat, x_rstd = normalize(tie(inputs, half).astype(F32))
    e_own = e_own * gain_attn
    grad_inputs = (
        grad_resid
        + x_rstd
        * (
            e_own
            - jnp.mean(e_own, axis=-1, keepdims=True)
            - x_hat * jnp.mean(e_own * x_hat, axis=-1, keepdims=True)
        )
    ).astype(BF)
    sum_wup, sum_wdown = unpack_call(bid, (feed_a, feed_b, last_a, tie(last_b, half)), (width, width))
    sum_wqkv, sum_wproj = unpack_call(bid, (half, tie(last, sum_wup, grad_inputs)), (cols, inner))
    return (
        output,
        grad_inputs,
        small[0],
        small[1],
        sum_wqkv.reshape(heads, triple, width).transpose(2, 0, 1),
        biases[0, :cols].reshape(heads, triple),
        sum_wproj.reshape(heads, inner // heads, width),
        small[4],
        small[5],
        small[6],
        sum_wup,
        biases[1],
        sum_wdown,
        small[7],
    )


def solution(mesh):
    rows = P(("batch", "head"), None)
    in_specs = (
        rows,
        P("batch", None),
        rows,
        P(),
        P(),
        P(None, "head", None),
        P("head", None),
        P("head", None, None),
        P(),
        P(),
        P(),
        P(None, "head"),
        P("head"),
        P("head", None),
        P(),
    )
    out_specs = (
        rows,
        rows,
        P(),
        P(),
        P(None, "head", None),
        P("head", None),
        P("head", None, None),
        P(),
        P(),
        P(),
        P(None, "head"),
        P("head"),
        P("head", None),
        P(),
    )
    return jax.shard_map(
        per_device, mesh=mesh, in_specs=in_specs, out_specs=out_specs, check_vma=False
    )
```

```python
import functools
import math

import jax
import jax.numpy as jnp
from jax import lax
from jax.experimental import pallas as pl
from jax.experimental.pallas import tpu as pltpu
from jax.sharding import PartitionSpec as P

F32 = jnp.float32
BF = jnp.bfloat16
BLK = 256
NEG = -1e30
EPS = 1e-05
GELU_C = math.sqrt(2.0 / math.pi)
GELU_A = 0.044715


def dot_nn(a, b):
    return lax.dot_general(a, b, (((1,), (0,)), ((), ())), preferred_element_type=F32)


def dot_nt(a, b):
    return lax.dot_general(a, b, (((1,), (1,)), ((), ())), preferred_element_type=F32)


def dot_tn(a, b):
    return lax.dot_general(a, b, (((0,), (0,)), ((), ())), preferred_element_type=F32)


def cost(flops, nbytes, trans=0):
    return pl.CostEstimate(flops=int(flops), bytes_accessed=int(nbytes), transcendentals=int(trans))


def swap(x, axis, bits):
    size = lax.axis_size(axis)
    return lax.ppermute(x, axis, [(i, i ^ bits) for i in range(size)])


def normalize(v):
    center = v - jnp.mean(v, axis=-1, keepdims=True)
    rstd = lax.rsqrt(jnp.mean(center * center, axis=-1, keepdims=True) + EPS)
    return center * rstd, rstd


def qkv_kernel(heads, hd, steps, h_ref, a_ref, b_ref, v_ref, w_ref, bias_ref, *rest):
    q_out, k_out, v_out, vt_out, hat_out = rest[-5:]
    t = pl.program_id(0)
    x = jnp.where(t < steps // 2, a_ref[...], b_ref[...]).astype(F32)
    xhat, _ = normalize(x)
    hat_out[...] = xhat.astype(BF)
    h1 = (xhat * v_ref[0:1, :] + v_ref[1:2, :]).astype(BF)
    bias = jnp.concatenate([bias_ref[h : h + 1, :] for h in range(heads)], axis=1)
    packed = (dot_nt(h1, w_ref[...]) + bias).astype(BF)
    for h in range(heads):
        o = 3 * hd * h
        q_out[h] = packed[:, o : o + hd]
        k_out[h] = packed[:, o + hd : o + 2 * hd]
        v = packed[:, o + 2 * hd : o + 3 * hd]
        v_out[h] = v
        vt_out[h] = v.T


def qkv_call(hid, a, b, vectors, w, bias, first, group_rows, before):
    rows, width = a.shape
    heads, triple = bias.shape
    hd = triple // 3
    per = rows // BLK
    steps = 2 * per
    place = lambda t, h: (h[0] ^ (first + t // per)) * per + t % per
    whole = lambda t, h: (0, 0)
    out_shape = tuple(
        jax.ShapeDtypeStruct(s, BF)
        for s in ((heads, group_rows, hd),) * 3 + ((heads, hd, group_rows), (group_rows, width))
    )
    in_specs = [
        pl.BlockSpec((BLK, width), lambda t, h: (jnp.minimum(t, per - 1), 0)),
        pl.BlockSpec((BLK, width), lambda t, h: (jnp.maximum(t - per, 0), 0)),
        pl.BlockSpec(vectors.shape, whole),
        pl.BlockSpec(w.shape, whole),
        pl.BlockSpec(bias.shape, whole),
    ] + [pl.BlockSpec(memory_space=pl.ANY)] * len(before)
    return pl.pallas_call(
        functools.partial(qkv_kernel, heads, hd, steps),
        out_shape=out_shape,
        grid_spec=pltpu.PrefetchScalarGridSpec(
            num_scalar_prefetch=1,
            grid=(steps,),
            in_specs=in_specs,
            out_specs=[pl.BlockSpec((heads, BLK, hd), lambda t, h: (0, place(t, h), 0))] * 3
            + [
                pl.BlockSpec((heads, hd, BLK), lambda t, h: (0, 0, place(t, h))),
                pl.BlockSpec((BLK, width), lambda t, h: (first * per + t, 0)),
            ],
        ),
        input_output_aliases={6 + i: i for i in range(len(before))},
        cost_estimate=cost(4 * rows * width * w.shape[0], 12 * rows * width),
        name="qkv",
    )(hid, a, b, vectors, w, bias, *before)


def row_segment(len_ref, row):
    low = row
    high = row + 1
    start = jnp.int32(0)
    for k in range(len_ref.shape[0] - 1):
        stop = start + len_ref[k]
        inside = (row >= start) & (row < stop)
        low = jnp.where(inside, start, low)
        high = jnp.where(inside, stop, high)
        start = stop
    return low, high


def lane_starts(len_ref, row, width):
    i = row + lax.broadcasted_iota(jnp.int32, (1, width), 1)
    start = jnp.zeros((1, width), jnp.int32)
    stop = jnp.int32(0)
    for k in range(len_ref.shape[0] - 1):
        stop = stop + len_ref[k]
        start = jnp.where(i >= stop, stop, start)
    return jnp.where(i >= stop, i, start), i


def slot_at(slots, t, per):
    at = jnp.int32(slots[0])
    for k, slot in enumerate(slots[1:], 1):
        at = jnp.where(t >= k * per, slot, at)
    return at


def attend_kernel(heads, slots, per, scale, len_ref, h_ref, q_ref, k_ref, vt_ref, *rest):
    o_refs, l_refs = rest[: len(slots)], rest[len(slots) : -3]
    m_s, z_s, acc_s = rest[-3:]
    t = pl.program_id(0)
    row = ((h_ref[0] ^ slot_at(slots, t, per)) * per + t % per) * BLK
    start, i = lane_starts(len_ref, row, BLK)
    low, _ = row_segment(len_ref, row)
    m_s[...] = jnp.full_like(m_s, NEG)
    z_s[...] = jnp.zeros_like(z_s)
    acc_s[...] = jnp.zeros_like(acc_s)
    qs = [q_ref[h] * jnp.asarray(scale, BF) for h in range(heads)]

    def body(jb, carry):
        j0 = pl.multiple_of(jb * BLK, BLK)
        j = j0 + lax.broadcasted_iota(jnp.int32, (BLK, BLK), 0)
        mask = (j >= start) & (j <= i)
        for h in range(heads):
            s = dot_nt(k_ref[h, pl.ds(j0, BLK), :], qs[h])
            magnitude = jnp.where(mask, jnp.abs(s), NEG)
            old = m_s[h : h + 1, :]
            top = jnp.maximum(old, jnp.max(magnitude, axis=0, keepdims=True))
            decay = jnp.exp(old - top)
            e = jnp.exp(magnitude - top)
            z_s[h : h + 1, :] = z_s[h : h + 1, :] * decay + jnp.sum(e, axis=0, keepdims=True)
            m_s[h : h + 1, :] = top
            u = e - jnp.where(mask, jnp.exp(-top), 0.0)
            w = jnp.where(s < 0, -u, u).astype(BF)
            acc_s[h] = acc_s[h] * decay + dot_nn(vt_ref[h, :, pl.ds(j0, BLK)], w)
        return carry

    lax.fori_loop(low // BLK, row // BLK + 1, body, 0)
    for k, (o_ref, l_ref) in enumerate(zip(o_refs, l_refs, strict=True)):

        @pl.when(t // per == k)
        def _(o_ref=o_ref, l_ref=l_ref):
            outs = []
            for h in range(heads):
                z = z_s[h : h + 1, :]
                outs.append((acc_s[h] / z).T)
                l_ref[h : h + 1, :] = m_s[h : h + 1, :] + jnp.log(z)
            o_ref[...] = jnp.concatenate(outs, axis=1).astype(BF)


def attend_call(lengths, hid, q, k, vt, slots, chunk):
    heads, rows, hd = q.shape
    per = chunk // BLK
    count = len(slots)
    place = lambda t, n, h: (0, (h[0] ^ slot_at(slots, t, per)) * per + t % per, 0)
    whole = lambda t, n, h: (0, 0, 0)
    out = pl.pallas_call(
        functools.partial(attend_kernel, heads, slots, per, 1.0 / math.sqrt(hd)),
        out_shape=(jax.ShapeDtypeStruct((chunk, heads * hd), BF),) * count
        + (jax.ShapeDtypeStruct((8, chunk), F32),) * count,
        grid_spec=pltpu.PrefetchScalarGridSpec(
            num_scalar_prefetch=2,
            grid=(count * per,),
            in_specs=[
                pl.BlockSpec((heads, BLK, hd), place),
                pl.BlockSpec((heads, rows, hd), whole),
                pl.BlockSpec((heads, hd, rows), whole),
            ],
            out_specs=[
                pl.BlockSpec((BLK, heads * hd), lambda t, n, h, k=k: (jnp.clip(t - k * per, 0, per - 1), 0))
                for k in range(count)
            ]
            + [
                pl.BlockSpec((8, BLK), lambda t, n, h, k=k: (0, jnp.clip(t - k * per, 0, per - 1)))
                for k in range(count)
            ],
            scratch_shapes=[
                pltpu.VMEM((8, BLK), F32),
                pltpu.VMEM((8, BLK), F32),
                pltpu.VMEM((heads, hd, BLK), F32),
            ],
        ),
        cost_estimate=cost(heads * rows * chunk * count * hd * 2, 6 * rows * heads * hd, heads * rows * chunk * count // 8),
        name="attend",
    )(lengths, hid, q, k, vt)
    return out[:count], out[count:]


def attend_back_kernel(chunk, scale, len_ref, h_ref, q_ref, k_ref, v_ref, *rest):
    g_refs, o_refs, l_refs = rest[0:4], rest[4:8], rest[8:12]
    gp_ref, q_s, g_s, kt_s, l_s, c_s, d_s, dq_s, dk_s, dv_s = rest[12:]
    heads, rows, hd = q_ref.shape
    blocks = rows // BLK
    per = chunk // BLK
    own = h_ref[0]
    for c in range(4):
        r0 = pl.multiple_of((own ^ c) * chunk, chunk)
        g = g_refs[c][...]
        o = o_refs[c][...]
        for h in range(heads):
            gh = g[:, h * hd : (h + 1) * hd]
            g_s[h, pl.ds(r0, chunk), :] = gh
            both = gh.astype(F32) * o[:, h * hd : (h + 1) * hd].astype(F32)
            d_s[h : h + 1, pl.ds(r0, chunk)] = jnp.sum(both.T, axis=0, keepdims=True)
        level = l_refs[c][...]
        l_s[:, pl.ds(r0, chunk)] = level
        c_s[:, pl.ds(r0, chunk)] = jnp.exp(-level)
    for h in range(heads):
        q_s[h] = q_ref[h] * jnp.asarray(scale, BF)
    dq_s[...] = jnp.zeros_like(dq_s)

    def out_row(block):
        return pl.multiple_of(((own ^ (block // per)) * per + block % per) * BLK, BLK)

    def outer(jb, carry):
        j0 = pl.multiple_of(jb * BLK, BLK)
        dk_s[...] = jnp.zeros_like(dk_s)
        dv_s[...] = jnp.zeros_like(dv_s)
        for h in range(heads):
            kt_s[h] = k_ref[h, pl.ds(j0, BLK), :].T
        _, stop = row_segment(len_ref, j0 + BLK - 1)
        j = j0 + lax.broadcasted_iota(jnp.int32, (BLK, BLK), 0)

        def inner(ib, carry):
            i0 = pl.multiple_of(ib * BLK, BLK)
            start, i = lane_starts(len_ref, i0, BLK)
            mask = (j >= start) & (j <= i)
            for h in range(heads):
                qh = q_s[h, pl.ds(i0, BLK), :]
                gh = g_s[h, pl.ds(i0, BLK), :]
                s = dot_nt(k_ref[h, pl.ds(j0, BLK), :], qh)
                gw = dot_nt(v_ref[h, pl.ds(j0, BLK), :], gh)
                level = l_s[h : h + 1, pl.ds(i0, BLK)]
                offset = c_s[h : h + 1, pl.ds(i0, BLK)]
                d = d_s[h : h + 1, pl.ds(i0, BLK)]
                p = jnp.exp(jnp.where(mask, jnp.abs(s), NEG) - level)
                u = p - jnp.where(mask, offset, 0.0)
                minus = s < 0
                w = jnp.where(minus, -u, u).astype(BF)
                signed = jnp.where(minus, -d, jnp.where(s == 0, 0.0, d))
                gs = (p * (gw - signed)).astype(BF)
                dv_s[h] += dot_nn(w, gh)
                dk_s[h] += dot_nn(gs, qh)
                dq_s[h, :, pl.ds(i0, BLK)] += dot_nn(kt_s[h], gs)
            return carry

        lax.fori_loop(jb, (stop - 1) // BLK + 1, inner, 0)
        for h in range(heads):
            at = pl.ds(out_row(jb), BLK)
            gp_ref[at, (3 * h + 1) * hd : (3 * h + 2) * hd] = dk_s[h].astype(BF)
            gp_ref[at, (3 * h + 2) * hd : (3 * h + 3) * hd] = dv_s[h].astype(BF)
        return carry

    lax.fori_loop(0, blocks, outer, 0)

    def finish(ib, carry):
        i0 = pl.multiple_of(ib * BLK, BLK)
        for h in range(heads):
            dq = (dq_s[h, :, pl.ds(i0, BLK)] * scale).T.astype(BF)
            gp_ref[pl.ds(out_row(ib), BLK), 3 * h * hd : (3 * h + 1) * hd] = dq
        return carry

    lax.fori_loop(0, blocks, finish, 0)


def attend_back_call(lengths, hid, q, k, v, grads, outs, levels, chunk):
    heads, rows, hd = q.shape
    vm = pl.BlockSpec(memory_space=pltpu.VMEM)
    sm = pl.BlockSpec(memory_space=pltpu.SMEM)
    return pl.pallas_call(
        functools.partial(attend_back_kernel, chunk, 1.0 / math.sqrt(hd)),
        out_shape=jax.ShapeDtypeStruct((rows, heads * 3 * hd), BF),
        in_specs=[sm, sm] + [vm] * 15,
        out_specs=vm,
        scratch_shapes=[
            pltpu.VMEM((heads, rows, hd), BF),
            pltpu.VMEM((heads, rows, hd), BF),
            pltpu.VMEM((heads, hd, BLK), BF),
            pltpu.VMEM((8, rows), F32),
            pltpu.VMEM((8, rows), F32),
            pltpu.VMEM((8, rows), F32),
            pltpu.VMEM((heads, hd, rows), F32),
            pltpu.VMEM((heads, BLK, hd), F32),
            pltpu.VMEM((heads, BLK, hd), F32),
        ],
        cost_estimate=cost(heads * rows * rows * hd * 20, 30 * rows * heads * hd, heads * rows * rows // 2),
        name="attend_back",
    )(lengths, hid, q, k, v, *grads, *outs, *levels)


def feed_kernel(steps, ha_ref, hb_ref, ga_ref, gb_ref, up_ref, v_ref, down_ref, *rest):
    act_ref, gup_ref, gna_ref, gnb_ref, outa_ref, outb_ref = rest[-6:]
    early = pl.program_id(0) < steps // 2
    h2 = jnp.where(early, ha_ref[...], hb_ref[...])
    grad = jnp.where(early, ga_ref[...], gb_ref[...])
    u = dot_nn(h2, up_ref[...]) + v_ref[5:6, :]
    square = u * u
    tanh = jnp.tanh(u * (GELU_C + (GELU_C * GELU_A) * square))
    half = 0.5 * (1.0 + tanh)
    act = (u * half).astype(BF)
    slope = half + (0.5 * u) * (1.0 - tanh * tanh) * (GELU_C + (3.0 * GELU_C * GELU_A) * square)
    gup = (dot_nt(grad, down_ref[...]) * slope).astype(BF)
    act_ref[...] = act
    gup_ref[...] = gup
    gn = dot_nt(gup, up_ref[...]).astype(BF)
    out = dot_nn(act, down_ref[...]).astype(BF)

    @pl.when(early)
    def _():
        gna_ref[...] = gn
        outa_ref[...] = out

    @pl.when(jnp.logical_not(early))
    def _():
        gnb_ref[...] = gn
        outb_ref[...] = out


def feed_call(ha, hb, ga, gb, up, vectors, down, first, group_rows, before):
    rows, width = ha.shape
    hidden = up.shape[1]
    per = rows // BLK
    steps = 2 * per
    whole = lambda t: (0, 0)
    early = pl.BlockSpec((BLK, width), lambda t: (jnp.minimum(t, per - 1), 0))
    late = pl.BlockSpec((BLK, width), lambda t: (jnp.maximum(t - per, 0), 0))
    return pl.pallas_call(
        functools.partial(feed_kernel, steps),
        out_shape=(
            jax.ShapeDtypeStruct((group_rows, hidden), BF),
            jax.ShapeDtypeStruct((group_rows, hidden), BF),
        )
        + (jax.ShapeDtypeStruct((rows, width), BF),) * 4,
        grid=(steps,),
        in_specs=[
            early,
            late,
            early,
            late,
            pl.BlockSpec(up.shape, whole),
            pl.BlockSpec(vectors.shape, whole),
            pl.BlockSpec(down.shape, whole),
        ]
        + [pl.BlockSpec(memory_space=pl.ANY)] * len(before),
        out_specs=[
            pl.BlockSpec((BLK, hidden), lambda t: (first * per + t, 0)),
            pl.BlockSpec((BLK, hidden), lambda t: (first * per + t, 0)),
            early,
            late,
            early,
            late,
        ],
        input_output_aliases={7 + i: i for i in range(len(before))},
        cost_estimate=cost(16 * rows * width * hidden, 16 * rows * width, 2 * rows * hidden),
        name="feed",
    )(ha, hb, ga, gb, up, vectors, down, *before)


def spots(b_ref, pieces):
    return [b_ref[0] ^ (2 * (spot % 4) + spot // 4) for spot in range(pieces)]


def split_out(b_ref, acc, keep_ref, send_ref):
    piece = acc.shape[0] // 8
    for spot, block in enumerate(spots(b_ref, 8)):
        out = keep_ref if spot < 4 else send_ref
        value = acc[pl.ds(pl.multiple_of(block * piece, 8), piece), :]
        out[(spot % 4) * piece : (spot % 4 + 1) * piece, :] = value.astype(BF)


def weigh_kernel(tiles, b_ref, h0, h1, h2, h3, act_ref, up_ref, g0, g1, g2, g3, keep_ref, send_ref, bias_ref, acc):
    t = pl.program_id(0)
    tile = acc.shape[0] // (2 * tiles)
    chunk = h0.shape[0]
    at = pl.ds(pl.multiple_of(t * tile, tile), tile)

    @pl.when(t == 0)
    def _():
        bias_ref[...] = jnp.sum(up_ref[...].astype(F32), axis=0, keepdims=True)

    @pl.when(t < tiles)
    def _():
        total = dot_tn(h0[...], up_ref[:chunk, :])
        for k, h in enumerate((h1, h2, h3)):
            total = total + dot_tn(h[...], up_ref[(k + 1) * chunk : (k + 2) * chunk, :])
        acc[at, :] = total

    @pl.when(t >= tiles)
    def _():
        total = dot_tn(act_ref[:chunk, :], g0[...])
        for k, g in enumerate((g1, g2, g3)):
            total = total + dot_tn(act_ref[(k + 1) * chunk : (k + 2) * chunk, :], g[...])
        acc[at, :] = total

    @pl.when(t == 2 * tiles - 1)
    def _():
        split_out(b_ref, acc, keep_ref, send_ref)


def weigh_call(bid, hs, act, up, grads):
    chunk, width = hs[0].shape
    rows, hidden = act.shape
    tile = 256
    tiles = width // tile
    whole = lambda t, b: (0, 0)
    total = width + hidden
    half = jax.ShapeDtypeStruct((total // 2, width), BF)
    return pl.pallas_call(
        functools.partial(weigh_kernel, tiles),
        out_shape=(half, half, jax.ShapeDtypeStruct((1, hidden), F32)),
        grid_spec=pltpu.PrefetchScalarGridSpec(
            num_scalar_prefetch=1,
            grid=(2 * tiles,),
            in_specs=[pl.BlockSpec((chunk, tile), lambda t, b: (0, jnp.minimum(t, tiles - 1)))] * 4
            + [
                pl.BlockSpec((rows, tile), lambda t, b: (0, jnp.maximum(t - tiles, 0))),
                pl.BlockSpec((rows, hidden), whole),
            ]
            + [pl.BlockSpec((chunk, width), whole)] * 4,
            out_specs=[
                pl.BlockSpec(half.shape, whole),
                pl.BlockSpec(half.shape, whole),
                pl.BlockSpec((1, hidden), whole),
            ],
            scratch_shapes=[pltpu.VMEM((total, width), F32)],
        ),
        cost_estimate=cost(4 * rows * width * hidden, 12 * rows * width),
        name="weigh",
    )(bid, *hs, act, up, *grads)


def mix_kernel(m0, m1, m2, m3, p0, p1, p2, p3, x_ref, v_ref, resid_ref, h_ref):
    total = x_ref[...].astype(F32) + v_ref[2:3, :]
    for m, p in ((m0, p0), (m1, p1), (m2, p2), (m3, p3)):
        total = total + dot_nn(m[...], p[...])
    resid_ref[...] = total
    hat, _ = normalize(total)
    h_ref[...] = (hat * v_ref[3:4, :] + v_ref[4:5, :]).astype(BF)


def mix_call(parts, projs, x, vectors):
    rows, width = x.shape
    per = rows // BLK
    inner = parts[0].shape[1]
    low = pl.BlockSpec((BLK, inner), lambda t: (t, 0))
    whole = lambda t: (0, 0)
    return pl.pallas_call(
        mix_kernel,
        out_shape=(jax.ShapeDtypeStruct((rows, width), F32), jax.ShapeDtypeStruct((rows, width), BF)),
        grid=(per,),
        in_specs=[low] * 4
        + [pl.BlockSpec(projs[0].shape, whole)] * 4
        + [pl.BlockSpec((BLK, width), lambda t: (t, 0)), pl.BlockSpec(vectors.shape, whole)],
        out_specs=[pl.BlockSpec((BLK, width), lambda t: (t, 0))] * 2,
        cost_estimate=cost(8 * rows * width * inner, 12 * rows * width),
        name="mix",
    )(*parts, *projs, x, vectors)


def turn_kernel(n_ref, s_ref, f_ref, resid_ref, cot_ref, v_ref, p0, p1, p2, p3, gr_ref, ga_ref, g0, g1, g2, g3, sum_ref):
    grad = n_ref[...].astype(F32) + s_ref[...].astype(F32) + f_ref[...].astype(F32)
    hat, rstd = normalize(resid_ref[...])
    cot = cot_ref[...].astype(F32)
    e = grad * v_ref[3:4, :]
    back = e - jnp.mean(e, axis=-1, keepdims=True) - hat * jnp.mean(e * hat, axis=-1, keepdims=True)
    grad_resid = cot + rstd * back
    gr_ref[...] = grad_resid
    att = grad_resid.astype(BF)
    ga_ref[...] = att
    for g, p in ((g0, p0), (g1, p1), (g2, p2), (g3, p3)):
        g[...] = dot_nt(att, p[...]).astype(BF)

    @pl.when(pl.program_id(0) == 0)
    def _():
        sum_ref[...] = jnp.zeros_like(sum_ref)

    for k, v in enumerate((grad_resid, grad * hat, grad, cot)):
        sum_ref[k + 4 : k + 5, :] += jnp.sum(v, axis=0, keepdims=True)


def turn_call(near, swapped, far, resid, cot, vectors, projs):
    rows, width = resid.shape
    per = rows // BLK
    inner = projs[0].shape[0]
    low = pl.BlockSpec((BLK, width), lambda t: (t, 0))
    whole = lambda t: (0, 0)
    return pl.pallas_call(
        turn_kernel,
        out_shape=(
            jax.ShapeDtypeStruct((rows, width), F32),
            jax.ShapeDtypeStruct((rows, width), BF),
        )
        + (jax.ShapeDtypeStruct((rows, inner), BF),) * 4
        + (jax.ShapeDtypeStruct((8, width), F32),),
        grid=(per,),
        in_specs=[low] * 5
        + [pl.BlockSpec(vectors.shape, whole)]
        + [pl.BlockSpec(projs[0].shape, whole)] * 4,
        out_specs=[low, low]
        + [pl.BlockSpec((BLK, inner), lambda t: (t, 0))] * 4
        + [pl.BlockSpec((8, width), whole)],
        cost_estimate=cost(rows, width),
        name="turn",
    )(near, swapped, far, resid, cot, vectors, *projs)


def tally_kernel(steps, b_ref, gp_ref, hat_ref, w_ref, v_ref, pw_ref, up_ref, s_ref, keep_ref, send_ref, acc, col):
    t = pl.program_id(0)
    gp = gp_ref[...]
    cols = gp.shape[1]
    half = acc.shape[0] // 2

    @pl.when(t == 0)
    def _():
        acc[:cols, :] = jnp.zeros((cols, acc.shape[1]), F32)
        acc[cols:, :] = pw_ref[...]
        col[...] = jnp.zeros_like(col)

    acc[:cols, :] += dot_tn(gp, hat_ref[...])
    col[...] += dot_tn(gp, jnp.ones((gp.shape[0], 128), BF))

    @pl.when(t == steps - 1)
    def _():
        total = col[:, 0:1]
        moment = acc[:cols, :]
        w = w_ref[...].astype(F32)
        small = s_ref[...]
        row = lax.broadcasted_iota(jnp.int32, small.shape, 0)
        small = jnp.where(row == 0, jnp.sum(w * moment, axis=0, keepdims=True), small)
        small = jnp.where(row == 1, jnp.sum(w * total, axis=0, keepdims=True), small)
        bias = jnp.concatenate((col[...].T[0:1, :], jnp.zeros((1, small.shape[1] - cols), F32)), axis=1)
        small = jnp.where(row == 2, bias, small)
        small = jnp.where(row == 3, up_ref[...], small).astype(BF)
        acc[:cols, :] = moment * v_ref[0:1, :] + total * v_ref[1:2, :]
        split_out(b_ref, acc, keep_ref, send_ref)
        keep_ref[half:, :] = small
        send_ref[half:, :] = small


def tally_call(bid, gp, hat, w, vectors, proj_grad, up_grad, sums):
    rows, width = hat.shape
    cols = gp.shape[1]
    total = cols + proj_grad.shape[0]
    block = 2 * BLK
    steps = rows // block
    whole = lambda t, b: (0, 0)
    half = jax.ShapeDtypeStruct((total // 2 + sums.shape[0], width), BF)
    return pl.pallas_call(
        functools.partial(tally_kernel, steps),
        out_shape=(half, half),
        grid_spec=pltpu.PrefetchScalarGridSpec(
            num_scalar_prefetch=1,
            grid=(steps,),
            in_specs=[
                pl.BlockSpec((block, cols), lambda t, b: (t, 0)),
                pl.BlockSpec((block, width), lambda t, b: (t, 0)),
            ]
            + [pl.BlockSpec(v.shape, whole) for v in (w, vectors, proj_grad, up_grad, sums)],
            out_specs=[pl.BlockSpec(half.shape, whole)] * 2,
            scratch_shapes=[pltpu.VMEM((total, width), F32), pltpu.VMEM((cols, 128), F32)],
        ),
        cost_estimate=cost(cols, width),
        name="tally",
    )(bid, gp, hat, w, vectors, proj_grad, up_grad, sums)


def spread_kernel(gp_ref, w_ref, *outs):
    e = dot_nn(gp_ref[...], w_ref[...]).astype(BF)
    for k, out in enumerate(outs):

        @pl.when(pl.program_id(0) == k)
        def _(out=out):
            out[...] = e


def spread_call(gp, w, chunk):
    cols, width = w.shape
    whole = lambda t: (0, 0)
    return pl.pallas_call(
        spread_kernel,
        out_shape=(jax.ShapeDtypeStruct((chunk, width), BF),) * 4,
        grid=(4,),
        in_specs=[pl.BlockSpec((chunk, cols), lambda t: (t, 0)), pl.BlockSpec(w.shape, whole)],
        out_specs=[pl.BlockSpec((chunk, width), whole)] * 4,
        cost_estimate=cost(cols, width),
        name="spread",
    )(gp, w)


def unpack_kernel(counts, parts, b_ref, *rest):
    acc = rest[-1]
    piece = acc.shape[0] // 8
    per = 8 // parts
    for spot, block in enumerate(spots(b_ref, 8)):
        at = spot % per * piece
        value = rest[spot // per][at : at + piece, :].astype(F32)
        acc[pl.ds(pl.multiple_of(block * piece, 8), piece), :] = value
    start = 0
    for out, count in zip(rest[parts:-1], counts, strict=True):
        out[...] = acc[start : start + count, :]
        start += count


def unpack_call(bid, parts, counts):
    total = sum(part.shape[0] for part in parts)
    width = parts[0].shape[1]
    vm = pl.BlockSpec(memory_space=pltpu.VMEM)
    return pl.pallas_call(
        functools.partial(unpack_kernel, counts, len(parts)),
        out_shape=tuple(jax.ShapeDtypeStruct((n, width), F32) for n in counts),
        in_specs=[pl.BlockSpec(memory_space=pltpu.SMEM)] + [vm] * len(parts),
        out_specs=[vm] * len(counts),
        scratch_shapes=[pltpu.VMEM((total, width), F32)],
        cost_estimate=cost(total, width),
        name="unpack",
    )(bid, *parts)


def tie(x, *needed):
    return lax.optimization_barrier((x,) + needed)[0]


def across(pieces):
    return [swap(piece, "batch", 2 * d) for d, piece in enumerate(pieces, 1)]


def sum_rest(x):
    for level in range(3, lax.axis_size("batch").bit_length() - 1):
        x = (x.astype(F32) + swap(x, "batch", 1 << level).astype(F32)).astype(x.dtype)
    return x


def fold(kept, got):
    piece = kept.shape[0] // 4
    total = kept[:piece].astype(F32)
    for g in got:
        total = total + g[:piece].astype(F32)
    return sum_rest(total.astype(BF))


def quarters(x):
    piece = x.shape[0] // 4
    return [x[d * piece : (d + 1) * piece] for d in range(1, 4)]


def sum_group(x):
    x = x + swap(x, "head", 1)
    return x + swap(x, "head", 2)


def per_device(
    inputs,
    lengths,
    cotangent,
    gain_attn,
    shift_attn,
    weight_qkv,
    bias_qkv,
    weight_proj,
    bias_proj,
    gain_mlp,
    shift_mlp,
    weight_up,
    bias_up,
    weight_down,
    bias_down,
):
    chunk, width = inputs.shape
    group_rows = chunk * lax.axis_size("head")
    heads, triple = weight_qkv.shape[1:]
    cols = heads * triple
    inner = cols // 3
    own = lax.axis_index("head")
    hid = own.astype(jnp.int32).reshape(1)
    bid = (lax.axis_index("batch") % 8).astype(jnp.int32).reshape(1)
    lens = lengths[0]
    live_rows = jnp.sum(lens[:-1])
    places = own * chunk + jnp.arange(chunk, dtype=jnp.int32)
    live = (places < live_rows)[:, None]
    qkv_t = weight_qkv.transpose(1, 2, 0).reshape(cols, width)
    proj = weight_proj.reshape(inner, width)
    zero = jnp.zeros((width,), F32)
    vectors = jnp.stack(
        (gain_attn, shift_attn, bias_proj, gain_mlp, shift_mlp, bias_up, bias_down, zero)
    )

    x_far = swap(inputs, "head", 2)
    x_near = swap(inputs, "head", 1)
    begun = qkv_call(hid, inputs, x_near, vectors, qkv_t, bias_qkv, 0, group_rows, ())
    x_far = tie(x_far, begun[0])
    x_last = swap(x_far, "head", 1)
    queries, keys, values, values_t, hats = qkv_call(
        hid, x_far, x_last, vectors, qkv_t, bias_qkv, 2, group_rows, begun
    )
    grad_own = jnp.where(live, cotangent, jnp.zeros_like(cotangent))
    grad_far = swap(tie(grad_own, x_far), "head", 2)
    proj_far = swap(tie(proj, x_far), "head", 2)
    projs = (proj, swap(proj, "head", 1), proj_far, swap(proj_far, "head", 1))

    (out_far, out_own), (level_far, level_own) = attend_call(
        lens, hid, queries, keys, values_t, (2, 0), chunk
    )
    from_far = swap(out_far, "head", 2)
    (out_last,), (level_last,) = attend_call(
        lens, hid, tie(queries, out_own, grad_far), keys, values_t, (3,), chunk
    )
    from_last = swap(out_last, "head", 2)
    (out_mate,), (level_mate,) = attend_call(
        lens, hid, tie(queries, out_last, from_far), keys, values_t, (1,), chunk
    )
    grads = (grad_own, swap(grad_own, "head", 1), grad_far, swap(grad_far, "head", 1))
    from_last = swap(tie(from_last, out_mate), "head", 1)
    parts = (out_own, swap(out_mate, "head", 1), from_far, from_last)
    resid, h_own = mix_call(parts, projs, inputs, vectors)
    h_far = swap(h_own, "head", 2)
    h_near = swap(h_own, "head", 1)

    near = feed_call(h_own, h_near, grads[0], grads[1], weight_up, vectors, weight_down, 0, group_rows, ())
    h_far = tie(h_far, near[0])
    h_last = swap(h_far, "head", 1)
    act, grad_up, norm_far, norm_last, down_far, down_last = feed_call(
        h_far, h_last, grads[2], grads[3], weight_up, vectors, weight_down, 2, group_rows, near[:2]
    )
    far_sum = (norm_far.astype(F32) + swap(norm_last, "head", 1).astype(F32)).astype(BF)
    grad_far_sum = swap(far_sum, "head", 2)
    near_swapped = swap(near[3], "head", 1)
    down_swapped = swap(tie(down_last, far_sum), "head", 1)
    near_down = swap(tie(near[5], far_sum), "head", 1)

    keep_feed, send_feed, grad_bup = weigh_call(
        bid, (h_own, h_near, h_far, h_last), tie(act, far_sum), grad_up, grads
    )
    other_feed = swap(send_feed, "batch", 1)
    grad_resid, grad_att, grad_near, grad_mate, grad_cross, grad_last, sums = turn_call(
        near[2],
        near_swapped,
        tie(grad_far_sum, grad_bup, down_swapped, near_down),
        resid,
        grad_own,
        vectors,
        projs,
    )
    got_last = swap(grad_last, "head", 2)
    got = swap(grad_cross, "head", 2)
    grad_mate = swap(grad_mate, "head", 1)
    grad_att = tie(grad_att, grad_mate)
    grad_proj = [dot_tn(p, grad_att) for p in parts]
    near_sent, far_sent = grad_proj[1].astype(BF), grad_proj[3].astype(BF)
    down_far = tie(down_far, grad_att)
    down_sum = (down_far.astype(F32) + down_swapped.astype(F32)).astype(BF)
    got_last = tie(got_last, near_sent, far_sent, down_sum)
    merged_grads = (grad_near, grad_mate, got, swap(got_last, "head", 1))
    grad_near_proj = grad_proj[0] + swap(near_sent, "head", 1).astype(F32)
    far_proj = (grad_proj[2] + swap(far_sent, "head", 1).astype(F32)).astype(BF)
    far_proj = swap(far_proj, "head", 2)

    kept_feed = (keep_feed.astype(F32) + tie(other_feed, got).astype(F32)).astype(BF)
    got_feed = across(quarters(kept_feed))
    down_other = swap(tie(down_sum, kept_feed), "head", 2)

    grad_packed = attend_back_call(
        lens,
        hid,
        tie(queries, kept_feed, grad_near_proj),
        keys,
        values,
        merged_grads,
        (out_own, out_mate, out_far, out_last),
        (level_own, level_mate, level_far, level_last),
        chunk,
    )
    got_feed = [tie(g, grad_packed) for g in got_feed]
    grad_wproj = grad_near_proj + tie(far_proj, grad_packed).astype(F32)
    total_feed = fold(kept_feed, got_feed)
    gathered_feed = across([total_feed] * 3)
    keep, send = tally_call(
        bid, tie(grad_packed, total_feed, down_other), hats, qkv_t, vectors, grad_wproj, grad_bup, sums
    )
    other = swap(send, "batch", 1)
    spread = spread_call(tie(grad_packed, keep), qkv_t, chunk)
    gathered_feed, spread = lax.optimization_barrier((gathered_feed, spread))
    e_own, e_near, e_far, e_last = spread

    feed_a = jnp.concatenate((total_feed, gathered_feed[0]), axis=0)
    feed_b = jnp.concatenate(gathered_feed[1:], axis=0)
    last_a = swap(feed_a, "batch", 1)
    summed = (keep.astype(F32) + tie(other, feed_a, feed_b).astype(F32)).astype(BF)
    kept, small = summed[:-8], summed[-8:]
    pieces = [jnp.concatenate((q, small), axis=0) for q in quarters(kept)]
    e_swapped = swap(tie(e_last, *pieces), "head", 1)
    e_sum = (e_far.astype(F32) + e_swapped.astype(F32)).astype(BF)
    got_attn = [tie(g, last_a, e_sum) for g in across(pieces)]

    tiny = [small.astype(F32)] + [g[-8:].astype(F32) for g in got_attn]
    small = sum_rest((tiny[0] + tiny[1]) + (tiny[2] + tiny[3]))
    total_attn = fold(kept, got_attn)
    gathered_attn = across([total_attn] * 3)
    last_b = swap(tie(feed_b, total_attn), "batch", 1)
    e_other = swap(tie(e_sum, total_attn), "head", 2)
    half = jnp.concatenate([total_attn] + [tie(g, last_b) for g in gathered_attn], axis=0)
    e_mate = swap(tie(e_near, half), "head", 1)
    last = swap(half, "batch", 1)
    biases = small[2:4]
    small = sum_group(tie(small, half))
    e_own = e_own.astype(F32) + e_mate.astype(F32) + tie(e_other, half).astype(F32)

    near_down = near[4].astype(F32) + near_down.astype(F32)
    output = (resid + near_down + tie(down_other, half).astype(F32) + bias_down).astype(BF)
    x_hat, x_rstd = normalize(tie(inputs, half).astype(F32))
    e_own = e_own * gain_attn
    grad_inputs = (
        grad_resid
        + x_rstd
        * (
            e_own
            - jnp.mean(e_own, axis=-1, keepdims=True)
            - x_hat * jnp.mean(e_own * x_hat, axis=-1, keepdims=True)
        )
    ).astype(BF)
    sum_wup, sum_wdown = unpack_call(bid, (feed_a, feed_b, last_a, tie(last_b, half)), (width, width))
    sum_wqkv, sum_wproj = unpack_call(bid, (half, tie(last, sum_wup, grad_inputs)), (cols, inner))
    return (
        output,
        grad_inputs,
        small[0],
        small[1],
        sum_wqkv.reshape(heads, triple, width).transpose(2, 0, 1),
        biases[0, :cols].reshape(heads, triple),
        sum_wproj.reshape(heads, inner // heads, width),
        small[4],
        small[5],
        small[6],
        sum_wup,
        biases[1],
        sum_wdown,
        small[7],
    )


def solution(mesh):
    rows = P(("batch", "head"), None)
    in_specs = (
        rows,
        P("batch", None),
        rows,
        P(),
        P(),
        P(None, "head", None),
        P("head", None),
        P("head", None, None),
        P(),
        P(),
        P(),
        P(None, "head"),
        P("head"),
        P("head", None),
        P(),
    )
    out_specs = (
        rows,
        rows,
        P(),
        P(),
        P(None, "head", None),
        P("head", None),
        P("head", None, None),
        P(),
        P(),
        P(),
        P(None, "head"),
        P("head"),
        P("head", None),
        P(),
    )
    return jax.shard_map(
        per_device, mesh=mesh, in_specs=in_specs, out_specs=out_specs, check_vma=False
    )
```

```python
import functools
import math

import jax
import jax.numpy as jnp
from jax import lax
from jax.experimental import pallas as pl
from jax.experimental.pallas import tpu as pltpu
from jax.sharding import PartitionSpec as P

F32 = jnp.float32
BF = jnp.bfloat16
BLK = 256
NEG = -1e30
EPS = 1e-05
GELU_C = math.sqrt(2.0 / math.pi)
GELU_A = 0.044715


def dot_nn(a, b):
    return lax.dot_general(a, b, (((1,), (0,)), ((), ())), preferred_element_type=F32)


def dot_nt(a, b):
    return lax.dot_general(a, b, (((1,), (1,)), ((), ())), preferred_element_type=F32)


def dot_tn(a, b):
    return lax.dot_general(a, b, (((0,), (0,)), ((), ())), preferred_element_type=F32)


def cost(flops, nbytes, trans=0):
    return pl.CostEstimate(flops=int(flops), bytes_accessed=int(nbytes), transcendentals=int(trans))


def swap(x, axis, bits):
    size = lax.axis_size(axis)
    return lax.ppermute(x, axis, [(i, i ^ bits) for i in range(size)])


def normalize(v):
    center = v - jnp.mean(v, axis=-1, keepdims=True)
    rstd = lax.rsqrt(jnp.mean(center * center, axis=-1, keepdims=True) + EPS)
    return center * rstd, rstd


def qkv_kernel(heads, hd, steps, h_ref, a_ref, b_ref, v_ref, w_ref, bias_ref, *rest):
    q_out, k_out, v_out, vt_out, hat_out = rest[-5:]
    t = pl.program_id(0)
    x = jnp.where(t < steps // 2, a_ref[...], b_ref[...]).astype(F32)
    xhat, _ = normalize(x)
    hat_out[...] = xhat.astype(BF)
    h1 = (xhat * v_ref[0:1, :] + v_ref[1:2, :]).astype(BF)
    bias = jnp.concatenate([bias_ref[h : h + 1, :] for h in range(heads)], axis=1)
    packed = (dot_nt(h1, w_ref[...]) + bias).astype(BF)
    for h in range(heads):
        o = 3 * hd * h
        q_out[h] = packed[:, o : o + hd]
        k_out[h] = packed[:, o + hd : o + 2 * hd]
        v = packed[:, o + 2 * hd : o + 3 * hd]
        v_out[h] = v
        vt_out[h] = v.T


def qkv_call(hid, a, b, vectors, w, bias, first, group_rows, before):
    rows, width = a.shape
    heads, triple = bias.shape
    hd = triple // 3
    per = rows // BLK
    steps = 2 * per
    place = lambda t, h: (h[0] ^ (first + t // per)) * per + t % per
    whole = lambda t, h: (0, 0)
    out_shape = tuple(
        jax.ShapeDtypeStruct(s, BF)
        for s in ((heads, group_rows, hd),) * 3 + ((heads, hd, group_rows), (group_rows, width))
    )
    in_specs = [
        pl.BlockSpec((BLK, width), lambda t, h: (jnp.minimum(t, per - 1), 0)),
        pl.BlockSpec((BLK, width), lambda t, h: (jnp.maximum(t - per, 0), 0)),
        pl.BlockSpec(vectors.shape, whole),
        pl.BlockSpec(w.shape, whole),
        pl.BlockSpec(bias.shape, whole),
    ] + [pl.BlockSpec(memory_space=pl.ANY)] * len(before)
    return pl.pallas_call(
        functools.partial(qkv_kernel, heads, hd, steps),
        out_shape=out_shape,
        grid_spec=pltpu.PrefetchScalarGridSpec(
            num_scalar_prefetch=1,
            grid=(steps,),
            in_specs=in_specs,
            out_specs=[pl.BlockSpec((heads, BLK, hd), lambda t, h: (0, place(t, h), 0))] * 3
            + [
                pl.BlockSpec((heads, hd, BLK), lambda t, h: (0, 0, place(t, h))),
                pl.BlockSpec((BLK, width), lambda t, h: (first * per + t, 0)),
            ],
        ),
        input_output_aliases={6 + i: i for i in range(len(before))},
        cost_estimate=cost(4 * rows * width * w.shape[0], 12 * rows * width),
        name="qkv",
    )(hid, a, b, vectors, w, bias, *before)


def row_segment(len_ref, row):
    low = row
    high = row + 1
    start = jnp.int32(0)
    for k in range(len_ref.shape[0] - 1):
        stop = start + len_ref[k]
        inside = (row >= start) & (row < stop)
        low = jnp.where(inside, start, low)
        high = jnp.where(inside, stop, high)
        start = stop
    return low, high


def lane_starts(len_ref, row, width):
    i = row + lax.broadcasted_iota(jnp.int32, (1, width), 1)
    start = jnp.zeros((1, width), jnp.int32)
    stop = jnp.int32(0)
    for k in range(len_ref.shape[0] - 1):
        stop = stop + len_ref[k]
        start = jnp.where(i >= stop, stop, start)
    return jnp.where(i >= stop, i, start), i


def attend_kernel(heads, first, per, scale, len_ref, h_ref, q_ref, k_ref, vt_ref, o_ref, l_ref, s_s, m_s, z_s, acc_s):
    t = pl.program_id(0)
    row = ((h_ref[0] ^ (first + t // per)) * per + t % per) * BLK
    start, i = lane_starts(len_ref, row, BLK)
    low, _ = row_segment(len_ref, row)
    m_s[...] = jnp.zeros_like(m_s)
    z_s[...] = jnp.zeros_like(z_s)
    acc_s[...] = jnp.zeros_like(acc_s)
    qs = [q_ref[h] * jnp.asarray(scale, BF) for h in range(heads)]
    blocks = (low // BLK, row // BLK + 1)

    def measure(jb, carry):
        j0 = pl.multiple_of(jb * BLK, BLK)
        j = j0 + lax.broadcasted_iota(jnp.int32, (BLK, BLK), 0)
        mask = (j >= start) & (j <= i)
        scores = [dot_nt(k_ref[h, pl.ds(j0, BLK), :], qs[h]) for h in range(heads)]
        tops = [m_s[h : h + 1, :] for h in range(heads)]
        for h in range(heads):
            s = jnp.where(mask, scores[h], 0.0)
            s_s[h, pl.ds(j0, BLK), :] = s
            tops[h] = jnp.maximum(tops[h], jnp.max(jnp.abs(s), axis=0, keepdims=True))
        for h in range(heads):
            m_s[h : h + 1, :] = tops[h]
        return carry

    lax.fori_loop(*blocks, measure, 0)
    tops = [m_s[h : h + 1, :] for h in range(heads)]
    offsets = [jnp.exp(-top) for top in tops]

    def gather(jb, carry):
        j0 = pl.multiple_of(jb * BLK, BLK)
        sums, weights = [], []
        for h in range(heads):
            s = s_s[h, pl.ds(j0, BLK), :]
            u = jnp.exp(jnp.abs(s) - tops[h]) - offsets[h]
            sums.append(jnp.sum(u, axis=0, keepdims=True))
            weights.append(jnp.where(s < 0, -u, u).astype(BF))
        adds = [dot_nn(vt_ref[h, :, pl.ds(j0, BLK)], weights[h]) for h in range(heads)]
        for h in range(heads):
            z_s[h : h + 1, :] += sums[h]
            acc_s[h] += adds[h]
        return carry

    lax.fori_loop(*blocks, gather, 0)
    count = (i - start + 1).astype(F32)
    outs = []
    for h in range(heads):
        z = z_s[h : h + 1, :] + count * offsets[h]
        outs.append((acc_s[h] / z).T)
        l_ref[h : h + 1, :] = tops[h] + jnp.log(z)
    o_ref[...] = jnp.concatenate(outs, axis=1).astype(BF)


def attend_call(lengths, hid, q, k, vt, first, chunk):
    heads, rows, hd = q.shape
    per = chunk // BLK
    steps = 2 * per
    place = lambda t, n, h: (0, (h[0] ^ (first + t // per)) * per + t % per, 0)
    whole = lambda t, n, h: (0, 0, 0)
    return pl.pallas_call(
        functools.partial(attend_kernel, heads, first, per, 1.0 / math.sqrt(hd)),
        out_shape=(
            jax.ShapeDtypeStruct((steps * BLK, heads * hd), BF),
            jax.ShapeDtypeStruct((8, steps * BLK), F32),
        ),
        grid_spec=pltpu.PrefetchScalarGridSpec(
            num_scalar_prefetch=2,
            grid=(steps,),
            in_specs=[
                pl.BlockSpec((heads, BLK, hd), place),
                pl.BlockSpec((heads, rows, hd), whole),
                pl.BlockSpec((heads, hd, rows), whole),
            ],
            out_specs=[
                pl.BlockSpec((BLK, heads * hd), lambda t, n, h: (t, 0)),
                pl.BlockSpec((8, BLK), lambda t, n, h: (0, t)),
            ],
            scratch_shapes=[
                pltpu.VMEM((heads, rows, BLK), F32),
                pltpu.VMEM((8, BLK), F32),
                pltpu.VMEM((8, BLK), F32),
                pltpu.VMEM((heads, hd, BLK), F32),
            ],
        ),
        cost_estimate=cost(heads * rows * rows * hd * 4, 12 * rows * heads * hd, heads * rows * rows // 4),
        name="attend",
    )(lengths, hid, q, k, vt)


def attend_back_kernel(chunk, scale, len_ref, h_ref, q_ref, k_ref, v_ref, *rest):
    g_refs, o_refs, l_refs = rest[0:4], rest[4:6], rest[6:8]
    gp_ref, q_s, g_s, kt_s, l_s, c_s, d_s, dq_s, dk_s, dv_s = rest[8:]
    heads, rows, hd = q_ref.shape
    blocks = rows // BLK
    per = chunk // BLK
    own = h_ref[0]
    for c in range(4):
        r0 = pl.multiple_of((own ^ c) * chunk, chunk)
        part = slice((c % 2) * chunk, (c % 2 + 1) * chunk)
        g = g_refs[c][...]
        o = o_refs[c // 2][part, :]
        for h in range(heads):
            gh = g[:, h * hd : (h + 1) * hd]
            g_s[h, pl.ds(r0, chunk), :] = gh
            both = gh.astype(F32) * o[:, h * hd : (h + 1) * hd].astype(F32)
            d_s[h : h + 1, pl.ds(r0, chunk)] = jnp.sum(both.T, axis=0, keepdims=True)
        level = l_refs[c // 2][:, part]
        l_s[:, pl.ds(r0, chunk)] = level
        c_s[:, pl.ds(r0, chunk)] = jnp.exp(-level)
    for h in range(heads):
        q_s[h] = q_ref[h] * jnp.asarray(scale, BF)
    dq_s[...] = jnp.zeros_like(dq_s)

    def out_row(block):
        return pl.multiple_of(((own ^ (block // per)) * per + block % per) * BLK, BLK)

    def outer(jb, carry):
        j0 = pl.multiple_of(jb * BLK, BLK)
        dk_s[...] = jnp.zeros_like(dk_s)
        dv_s[...] = jnp.zeros_like(dv_s)
        for h in range(heads):
            kt_s[h] = k_ref[h, pl.ds(j0, BLK), :].T
        _, stop = row_segment(len_ref, j0 + BLK - 1)
        j = j0 + lax.broadcasted_iota(jnp.int32, (BLK, BLK), 0)

        def inner(ib, carry):
            i0 = pl.multiple_of(ib * BLK, BLK)
            start, i = lane_starts(len_ref, i0, BLK)
            mask = (j >= start) & (j <= i)
            at = pl.ds(i0, BLK)
            qh = [q_s[h, at, :] for h in range(heads)]
            gh = [g_s[h, at, :] for h in range(heads)]
            scores = [dot_nt(k_ref[h, pl.ds(j0, BLK), :], qh[h]) for h in range(heads)]
            gws = [dot_nt(v_ref[h, pl.ds(j0, BLK), :], gh[h]) for h in range(heads)]
            ws, gss = [], []
            for h in range(heads):
                s, gw = scores[h], gws[h]
                level = l_s[h : h + 1, at]
                offset = c_s[h : h + 1, at]
                d = d_s[h : h + 1, at]
                p = jnp.exp(jnp.where(mask, jnp.abs(s), NEG) - level)
                u = p - jnp.where(mask, offset, 0.0)
                sign = jnp.clip(s * 1e38, -1.0, 1.0)
                w = (sign * u).astype(BF)
                gs = (p * (gw - sign * d)).astype(BF)
                ws.append(w)
                gss.append(gs)
            dvs = [dot_nn(ws[h], gh[h]) for h in range(heads)]
            dks = [dot_nn(gss[h], qh[h]) for h in range(heads)]
            dqs = [dot_nn(kt_s[h], gss[h]) for h in range(heads)]
            for h in range(heads):
                dv_s[h] += dvs[h]
                dk_s[h] += dks[h]
                dq_s[h, :, at] += dqs[h]
            return carry

        lax.fori_loop(jb, (stop - 1) // BLK + 1, inner, 0)
        for h in range(heads):
            at = pl.ds(out_row(jb), BLK)
            gp_ref[at, (3 * h + 1) * hd : (3 * h + 2) * hd] = dk_s[h].astype(BF)
            gp_ref[at, (3 * h + 2) * hd : (3 * h + 3) * hd] = dv_s[h].astype(BF)
        return carry

    lax.fori_loop(0, blocks, outer, 0)

    def finish(ib, carry):
        i0 = pl.multiple_of(ib * BLK, BLK)
        for h in range(heads):
            dq = (dq_s[h, :, pl.ds(i0, BLK)] * scale).T.astype(BF)
            gp_ref[pl.ds(out_row(ib), BLK), 3 * h * hd : (3 * h + 1) * hd] = dq
        return carry

    lax.fori_loop(0, blocks, finish, 0)


def attend_back_call(lengths, hid, q, k, v, grads, outs, levels, chunk):
    heads, rows, hd = q.shape
    vm = pl.BlockSpec(memory_space=pltpu.VMEM)
    sm = pl.BlockSpec(memory_space=pltpu.SMEM)
    return pl.pallas_call(
        functools.partial(attend_back_kernel, chunk, 1.0 / math.sqrt(hd)),
        out_shape=jax.ShapeDtypeStruct((rows, heads * 3 * hd), BF),
        in_specs=[sm, sm] + [vm] * 11,
        out_specs=vm,
        scratch_shapes=[
            pltpu.VMEM((heads, rows, hd), BF),
            pltpu.VMEM((heads, rows, hd), BF),
            pltpu.VMEM((heads, hd, BLK), BF),
            pltpu.VMEM((8, rows), F32),
            pltpu.VMEM((8, rows), F32),
            pltpu.VMEM((8, rows), F32),
            pltpu.VMEM((heads, hd, rows), F32),
            pltpu.VMEM((heads, BLK, hd), F32),
            pltpu.VMEM((heads, BLK, hd), F32),
        ],
        cost_estimate=cost(heads * rows * rows * hd * 20, 30 * rows * heads * hd, heads * rows * rows // 2),
        name="attend_back",
    )(lengths, hid, q, k, v, *grads, *outs, *levels)


def feed_kernel(steps, ha_ref, hb_ref, ga_ref, gb_ref, up_ref, v_ref, down_ref, *rest):
    act_ref, gup_ref, gna_ref, gnb_ref, outa_ref, outb_ref = rest[-6:]
    early = pl.program_id(0) < steps // 2
    h2 = jnp.where(early, ha_ref[...], hb_ref[...])
    grad = jnp.where(early, ga_ref[...], gb_ref[...])
    u = dot_nn(h2, up_ref[...]) + v_ref[5:6, :]
    square = u * u
    tanh = jnp.tanh(u * (GELU_C + (GELU_C * GELU_A) * square))
    half = 0.5 * (1.0 + tanh)
    act = (u * half).astype(BF)
    slope = half + (0.5 * u) * (1.0 - tanh * tanh) * (GELU_C + (3.0 * GELU_C * GELU_A) * square)
    gup = (dot_nt(grad, down_ref[...]) * slope).astype(BF)
    act_ref[...] = act
    gup_ref[...] = gup
    gn = dot_nt(gup, up_ref[...]).astype(BF)
    out = dot_nn(act, down_ref[...]).astype(BF)

    @pl.when(early)
    def _():
        gna_ref[...] = gn
        outa_ref[...] = out

    @pl.when(jnp.logical_not(early))
    def _():
        gnb_ref[...] = gn
        outb_ref[...] = out


def feed_call(ha, hb, ga, gb, up, vectors, down, first, group_rows, before):
    rows, width = ha.shape
    hidden = up.shape[1]
    per = rows // BLK
    steps = 2 * per
    whole = lambda t: (0, 0)
    early = pl.BlockSpec((BLK, width), lambda t: (jnp.minimum(t, per - 1), 0))
    late = pl.BlockSpec((BLK, width), lambda t: (jnp.maximum(t - per, 0), 0))
    return pl.pallas_call(
        functools.partial(feed_kernel, steps),
        out_shape=(
            jax.ShapeDtypeStruct((group_rows, hidden), BF),
            jax.ShapeDtypeStruct((group_rows, hidden), BF),
        )
        + (jax.ShapeDtypeStruct((rows, width), BF),) * 4,
        grid=(steps,),
        in_specs=[
            early,
            late,
            early,
            late,
            pl.BlockSpec(up.shape, whole),
            pl.BlockSpec(vectors.shape, whole),
            pl.BlockSpec(down.shape, whole),
        ]
        + [pl.BlockSpec(memory_space=pl.ANY)] * len(before),
        out_specs=[
            pl.BlockSpec((BLK, hidden), lambda t: (first * per + t, 0)),
            pl.BlockSpec((BLK, hidden), lambda t: (first * per + t, 0)),
            early,
            late,
            early,
            late,
        ],
        input_output_aliases={7 + i: i for i in range(len(before))},
        cost_estimate=cost(16 * rows * width * hidden, 16 * rows * width, 2 * rows * hidden),
        name="feed",
    )(ha, hb, ga, gb, up, vectors, down, *before)


def spots(b_ref, pieces):
    return [b_ref[0] ^ (2 * (spot % 4) + spot // 4) for spot in range(pieces)]


def split_out(b_ref, acc, keep_ref, send_ref):
    piece = acc.shape[0] // 8
    for spot, block in enumerate(spots(b_ref, 8)):
        out = keep_ref if spot < 4 else send_ref
        value = acc[pl.ds(pl.multiple_of(block * piece, 8), piece), :]
        out[(spot % 4) * piece : (spot % 4 + 1) * piece, :] = value.astype(BF)


def weigh_kernel(tiles, b_ref, h0, h1, h2, h3, act_ref, up_ref, g0, g1, g2, g3, keep_ref, send_ref, bias_ref, acc):
    t = pl.program_id(0)
    tile = acc.shape[0] // (2 * tiles)
    chunk = h0.shape[0]
    at = pl.ds(pl.multiple_of(t * tile, tile), tile)

    @pl.when(t == 0)
    def _():
        bias_ref[...] = jnp.sum(up_ref[...].astype(F32), axis=0, keepdims=True)

    @pl.when(t < tiles)
    def _():
        total = dot_tn(h0[...], up_ref[:chunk, :])
        for k, h in enumerate((h1, h2, h3)):
            total = total + dot_tn(h[...], up_ref[(k + 1) * chunk : (k + 2) * chunk, :])
        acc[at, :] = total

    @pl.when(t >= tiles)
    def _():
        total = dot_tn(act_ref[:chunk, :], g0[...])
        for k, g in enumerate((g1, g2, g3)):
            total = total + dot_tn(act_ref[(k + 1) * chunk : (k + 2) * chunk, :], g[...])
        acc[at, :] = total

    @pl.when(t == 2 * tiles - 1)
    def _():
        split_out(b_ref, acc, keep_ref, send_ref)


def weigh_call(bid, hs, act, up, grads):
    chunk, width = hs[0].shape
    rows, hidden = act.shape
    tile = 256
    tiles = width // tile
    whole = lambda t, b: (0, 0)
    total = width + hidden
    half = jax.ShapeDtypeStruct((total // 2, width), BF)
    return pl.pallas_call(
        functools.partial(weigh_kernel, tiles),
        out_shape=(half, half, jax.ShapeDtypeStruct((1, hidden), F32)),
        grid_spec=pltpu.PrefetchScalarGridSpec(
            num_scalar_prefetch=1,
            grid=(2 * tiles,),
            in_specs=[pl.BlockSpec((chunk, tile), lambda t, b: (0, jnp.minimum(t, tiles - 1)))] * 4
            + [
                pl.BlockSpec((rows, tile), lambda t, b: (0, jnp.maximum(t - tiles, 0))),
                pl.BlockSpec((rows, hidden), whole),
            ]
            + [pl.BlockSpec((chunk, width), whole)] * 4,
            out_specs=[
                pl.BlockSpec(half.shape, whole),
                pl.BlockSpec(half.shape, whole),
                pl.BlockSpec((1, hidden), whole),
            ],
            scratch_shapes=[pltpu.VMEM((total, width), F32)],
        ),
        cost_estimate=cost(4 * rows * width * hidden, 12 * rows * width),
        name="weigh",
    )(bid, *hs, act, up, *grads)


def mix_kernel(m0, m1, m2, m3, p0, p1, p2, p3, x_ref, v_ref, resid_ref, h_ref):
    total = x_ref[...].astype(F32) + v_ref[2:3, :]
    for m, p in ((m0, p0), (m1, p1), (m2, p2), (m3, p3)):
        total = total + dot_nn(m[...], p[...])
    resid_ref[...] = total
    hat, _ = normalize(total)
    h_ref[...] = (hat * v_ref[3:4, :] + v_ref[4:5, :]).astype(BF)


def mix_call(parts, projs, x, vectors):
    rows, width = x.shape
    per = rows // BLK
    inner = parts[0].shape[1]
    low = pl.BlockSpec((BLK, inner), lambda t: (t, 0))
    high = pl.BlockSpec((BLK, inner), lambda t: (t + per, 0))
    whole = lambda t: (0, 0)
    return pl.pallas_call(
        mix_kernel,
        out_shape=(jax.ShapeDtypeStruct((rows, width), F32), jax.ShapeDtypeStruct((rows, width), BF)),
        grid=(per,),
        in_specs=[low, high, low, high]
        + [pl.BlockSpec(projs[0].shape, whole)] * 4
        + [pl.BlockSpec((BLK, width), lambda t: (t, 0)), pl.BlockSpec(vectors.shape, whole)],
        out_specs=[pl.BlockSpec((BLK, width), lambda t: (t, 0))] * 2,
        cost_estimate=cost(8 * rows * width * inner, 12 * rows * width),
        name="mix",
    )(*parts, *projs, x, vectors)


def turn_kernel(n_ref, s_ref, f_ref, resid_ref, cot_ref, v_ref, p0, p1, p2, p3, gr_ref, ga_ref, g0, g1, g2, g3, sum_ref):
    grad = n_ref[...].astype(F32) + s_ref[...].astype(F32) + f_ref[...].astype(F32)
    hat, rstd = normalize(resid_ref[...])
    cot = cot_ref[...].astype(F32)
    e = grad * v_ref[3:4, :]
    back = e - jnp.mean(e, axis=-1, keepdims=True) - hat * jnp.mean(e * hat, axis=-1, keepdims=True)
    grad_resid = cot + rstd * back
    gr_ref[...] = grad_resid
    att = grad_resid.astype(BF)
    ga_ref[...] = att
    for g, p in ((g0, p0), (g1, p1), (g2, p2), (g3, p3)):
        g[...] = dot_nt(att, p[...]).astype(BF)

    @pl.when(pl.program_id(0) == 0)
    def _():
        sum_ref[...] = jnp.zeros_like(sum_ref)

    for k, v in enumerate((grad_resid, grad * hat, grad, cot)):
        sum_ref[k + 4 : k + 5, :] += jnp.sum(v, axis=0, keepdims=True)


def turn_call(near, swapped, far, resid, cot, vectors, projs):
    rows, width = resid.shape
    per = rows // BLK
    inner = projs[0].shape[0]
    low = pl.BlockSpec((BLK, width), lambda t: (t, 0))
    whole = lambda t: (0, 0)
    return pl.pallas_call(
        turn_kernel,
        out_shape=(
            jax.ShapeDtypeStruct((rows, width), F32),
            jax.ShapeDtypeStruct((rows, width), BF),
        )
        + (jax.ShapeDtypeStruct((rows, inner), BF),) * 4
        + (jax.ShapeDtypeStruct((8, width), F32),),
        grid=(per,),
        in_specs=[low] * 5
        + [pl.BlockSpec(vectors.shape, whole)]
        + [pl.BlockSpec(projs[0].shape, whole)] * 4,
        out_specs=[low, low]
        + [pl.BlockSpec((BLK, inner), lambda t: (t, 0))] * 4
        + [pl.BlockSpec((8, width), whole)],
        cost_estimate=cost(rows, width),
        name="turn",
    )(near, swapped, far, resid, cot, vectors, *projs)


def tally_kernel(steps, b_ref, gp_ref, hat_ref, w_ref, v_ref, pw_ref, up_ref, s_ref, keep_ref, send_ref, acc, col):
    t = pl.program_id(0)
    gp = gp_ref[...]
    cols = gp.shape[1]
    half = acc.shape[0] // 2

    @pl.when(t == 0)
    def _():
        acc[:cols, :] = jnp.zeros((cols, acc.shape[1]), F32)
        acc[cols:, :] = pw_ref[...]
        col[...] = jnp.zeros_like(col)

    acc[:cols, :] += dot_tn(gp, hat_ref[...])
    col[...] += dot_tn(gp, jnp.ones((gp.shape[0], 128), BF))

    @pl.when(t == steps - 1)
    def _():
        total = col[:, 0:1]
        moment = acc[:cols, :]
        w = w_ref[...].astype(F32)
        small = s_ref[...]
        row = lax.broadcasted_iota(jnp.int32, small.shape, 0)
        small = jnp.where(row == 0, jnp.sum(w * moment, axis=0, keepdims=True), small)
        small = jnp.where(row == 1, jnp.sum(w * total, axis=0, keepdims=True), small)
        bias = jnp.concatenate((col[...].T[0:1, :], jnp.zeros((1, small.shape[1] - cols), F32)), axis=1)
        small = jnp.where(row == 2, bias, small)
        small = jnp.where(row == 3, up_ref[...], small).astype(BF)
        acc[:cols, :] = moment * v_ref[0:1, :] + total * v_ref[1:2, :]
        split_out(b_ref, acc, keep_ref, send_ref)
        keep_ref[half:, :] = small
        send_ref[half:, :] = small


def tally_call(bid, gp, hat, w, vectors, proj_grad, up_grad, sums):
    rows, width = hat.shape
    cols = gp.shape[1]
    total = cols + proj_grad.shape[0]
    block = 2 * BLK
    steps = rows // block
    whole = lambda t, b: (0, 0)
    half = jax.ShapeDtypeStruct((total // 2 + sums.shape[0], width), BF)
    return pl.pallas_call(
        functools.partial(tally_kernel, steps),
        out_shape=(half, half),
        grid_spec=pltpu.PrefetchScalarGridSpec(
            num_scalar_prefetch=1,
            grid=(steps,),
            in_specs=[
                pl.BlockSpec((block, cols), lambda t, b: (t, 0)),
                pl.BlockSpec((block, width), lambda t, b: (t, 0)),
            ]
            + [pl.BlockSpec(v.shape, whole) for v in (w, vectors, proj_grad, up_grad, sums)],
            out_specs=[pl.BlockSpec(half.shape, whole)] * 2,
            scratch_shapes=[pltpu.VMEM((total, width), F32), pltpu.VMEM((cols, 128), F32)],
        ),
        cost_estimate=cost(cols, width),
        name="tally",
    )(bid, gp, hat, w, vectors, proj_grad, up_grad, sums)


def spread_kernel(gp_ref, w_ref, *outs):
    e = dot_nn(gp_ref[...], w_ref[...]).astype(BF)
    for k, out in enumerate(outs):

        @pl.when(pl.program_id(0) == k)
        def _(out=out):
            out[...] = e


def spread_call(gp, w, chunk):
    cols, width = w.shape
    whole = lambda t: (0, 0)
    return pl.pallas_call(
        spread_kernel,
        out_shape=(jax.ShapeDtypeStruct((chunk, width), BF),) * 4,
        grid=(4,),
        in_specs=[pl.BlockSpec((chunk, cols), lambda t: (t, 0)), pl.BlockSpec(w.shape, whole)],
        out_specs=[pl.BlockSpec((chunk, width), whole)] * 4,
        cost_estimate=cost(cols, width),
        name="spread",
    )(gp, w)


def unpack_kernel(counts, parts, b_ref, *rest):
    acc = rest[-1]
    piece = acc.shape[0] // 8
    per = 8 // parts
    for spot, block in enumerate(spots(b_ref, 8)):
        at = spot % per * piece
        value = rest[spot // per][at : at + piece, :].astype(F32)
        acc[pl.ds(pl.multiple_of(block * piece, 8), piece), :] = value
    start = 0
    for out, count in zip(rest[parts:-1], counts, strict=True):
        out[...] = acc[start : start + count, :]
        start += count


def unpack_call(bid, parts, counts):
    total = sum(part.shape[0] for part in parts)
    width = parts[0].shape[1]
    vm = pl.BlockSpec(memory_space=pltpu.VMEM)
    return pl.pallas_call(
        functools.partial(unpack_kernel, counts, len(parts)),
        out_shape=tuple(jax.ShapeDtypeStruct((n, width), F32) for n in counts),
        in_specs=[pl.BlockSpec(memory_space=pltpu.SMEM)] + [vm] * len(parts),
        out_specs=[vm] * len(counts),
        scratch_shapes=[pltpu.VMEM((total, width), F32)],
        cost_estimate=cost(total, width),
        name="unpack",
    )(bid, *parts)


def tie(x, *needed):
    return lax.optimization_barrier((x,) + needed)[0]


def across(pieces):
    return [swap(piece, "batch", 2 * d) for d, piece in enumerate(pieces, 1)]


def sum_rest(x):
    for level in range(3, lax.axis_size("batch").bit_length() - 1):
        x = (x.astype(F32) + swap(x, "batch", 1 << level).astype(F32)).astype(x.dtype)
    return x


def fold(kept, got):
    piece = kept.shape[0] // 4
    total = kept[:piece].astype(F32)
    for g in got:
        total = total + g[:piece].astype(F32)
    return sum_rest(total.astype(BF))


def quarters(x):
    piece = x.shape[0] // 4
    return [x[d * piece : (d + 1) * piece] for d in range(1, 4)]


def sum_group(x):
    x = x + swap(x, "head", 1)
    return x + swap(x, "head", 2)


def per_device(
    inputs,
    lengths,
    cotangent,
    gain_attn,
    shift_attn,
    weight_qkv,
    bias_qkv,
    weight_proj,
    bias_proj,
    gain_mlp,
    shift_mlp,
    weight_up,
    bias_up,
    weight_down,
    bias_down,
):
    chunk, width = inputs.shape
    group_rows = chunk * lax.axis_size("head")
    heads, triple = weight_qkv.shape[1:]
    cols = heads * triple
    inner = cols // 3
    own = lax.axis_index("head")
    hid = own.astype(jnp.int32).reshape(1)
    bid = (lax.axis_index("batch") % 8).astype(jnp.int32).reshape(1)
    lens = lengths[0]
    live_rows = jnp.sum(lens[:-1])
    places = own * chunk + jnp.arange(chunk, dtype=jnp.int32)
    live = (places < live_rows)[:, None]
    qkv_t = weight_qkv.transpose(1, 2, 0).reshape(cols, width)
    proj = weight_proj.reshape(inner, width)
    zero = jnp.zeros((width,), F32)
    vectors = jnp.stack(
        (gain_attn, shift_attn, bias_proj, gain_mlp, shift_mlp, bias_up, bias_down, zero)
    )

    x_far = swap(inputs, "head", 2)
    x_near = swap(inputs, "head", 1)
    begun = qkv_call(hid, inputs, x_near, vectors, qkv_t, bias_qkv, 0, group_rows, ())
    x_far = tie(x_far, begun[0])
    x_last = swap(x_far, "head", 1)
    queries, keys, values, values_t, hats = qkv_call(
        hid, x_far, x_last, vectors, qkv_t, bias_qkv, 2, group_rows, begun
    )
    grad_own = jnp.where(live, cotangent, jnp.zeros_like(cotangent))
    grad_far = swap(tie(grad_own, x_far), "head", 2)
    proj_far = swap(tie(proj, x_far), "head", 2)
    projs = (proj, swap(proj, "head", 1), proj_far, swap(proj_far, "head", 1))

    merged_far, level_far = attend_call(lens, hid, queries, keys, values_t, 2, chunk)
    from_far = swap(merged_far, "head", 2)
    merged_near, level_near = attend_call(
        lens, hid, tie(queries, merged_far, grad_far), keys, values_t, 0, chunk
    )
    grads = (grad_own, swap(grad_own, "head", 1), grad_far, swap(grad_far, "head", 1))
    parts = (merged_near, swap(merged_near, "head", 1), from_far, swap(from_far, "head", 1))
    resid, h_own = mix_call(parts, projs, inputs, vectors)
    h_far = swap(h_own, "head", 2)
    h_near = swap(h_own, "head", 1)

    near = feed_call(h_own, h_near, grads[0], grads[1], weight_up, vectors, weight_down, 0, group_rows, ())
    h_far = tie(h_far, near[0])
    h_last = swap(h_far, "head", 1)
    act, grad_up, norm_far, norm_last, down_far, down_last = feed_call(
        h_far, h_last, grads[2], grads[3], weight_up, vectors, weight_down, 2, group_rows, near[:2]
    )
    far_sum = (norm_far.astype(F32) + swap(norm_last, "head", 1).astype(F32)).astype(BF)
    grad_far_sum = swap(far_sum, "head", 2)
    near_swapped = swap(near[3], "head", 1)
    down_swapped = swap(tie(down_last, far_sum), "head", 1)
    near_down = swap(tie(near[5], far_sum), "head", 1)

    keep_feed, send_feed, grad_bup = weigh_call(
        bid, (h_own, h_near, h_far, h_last), tie(act, far_sum), grad_up, grads
    )
    other_feed = swap(send_feed, "batch", 1)
    grad_resid, grad_att, grad_near, grad_mate, grad_cross, grad_last, sums = turn_call(
        near[2],
        near_swapped,
        tie(grad_far_sum, grad_bup, down_swapped, near_down),
        resid,
        grad_own,
        vectors,
        projs,
    )
    got_last = swap(grad_last, "head", 2)
    got = swap(grad_cross, "head", 2)
    grad_mate = swap(grad_mate, "head", 1)
    grad_att = tie(grad_att, grad_mate)
    low = slice(0, chunk)
    high = slice(chunk, 2 * chunk)
    grad_proj = [
        dot_tn(p[at], grad_att) for p, at in zip(parts, (low, high, low, high), strict=True)
    ]
    near_sent, far_sent = grad_proj[1].astype(BF), grad_proj[3].astype(BF)
    down_far = tie(down_far, grad_att)
    down_sum = (down_far.astype(F32) + down_swapped.astype(F32)).astype(BF)
    got_last = tie(got_last, near_sent, far_sent, down_sum)
    merged_grads = (grad_near, grad_mate, got, swap(got_last, "head", 1))
    grad_near_proj = grad_proj[0] + swap(near_sent, "head", 1).astype(F32)
    far_proj = (grad_proj[2] + swap(far_sent, "head", 1).astype(F32)).astype(BF)
    far_proj = swap(far_proj, "head", 2)

    kept_feed = (keep_feed.astype(F32) + tie(other_feed, got).astype(F32)).astype(BF)
    got_feed = across(quarters(kept_feed))
    down_other = swap(tie(down_sum, kept_feed), "head", 2)

    grad_packed = attend_back_call(
        lens,
        hid,
        tie(queries, kept_feed, grad_near_proj),
        keys,
        values,
        merged_grads,
        (merged_near, merged_far),
        (level_near, level_far),
        chunk,
    )
    got_feed = [tie(g, grad_packed) for g in got_feed]
    grad_wproj = grad_near_proj + tie(far_proj, grad_packed).astype(F32)
    total_feed = fold(kept_feed, got_feed)
    gathered_feed = across([total_feed] * 3)
    keep, send = tally_call(
        bid, tie(grad_packed, total_feed, down_other), hats, qkv_t, vectors, grad_wproj, grad_bup, sums
    )
    other = swap(send, "batch", 1)
    spread = spread_call(tie(grad_packed, keep), qkv_t, chunk)
    gathered_feed, spread = lax.optimization_barrier((gathered_feed, spread))
    e_own, e_near, e_far, e_last = spread

    feed_a = jnp.concatenate((total_feed, gathered_feed[0]), axis=0)
    feed_b = jnp.concatenate(gathered_feed[1:], axis=0)
    last_a = swap(feed_a, "batch", 1)
    summed = (keep.astype(F32) + tie(other, feed_a, feed_b).astype(F32)).astype(BF)
    kept, small = summed[:-8], summed[-8:]
    pieces = [jnp.concatenate((q, small), axis=0) for q in quarters(kept)]
    e_swapped = swap(tie(e_last, *pieces), "head", 1)
    e_sum = (e_far.astype(F32) + e_swapped.astype(F32)).astype(BF)
    got_attn = [tie(g, last_a, e_sum) for g in across(pieces)]

    tiny = [small.astype(F32)] + [g[-8:].astype(F32) for g in got_attn]
    small = sum_rest((tiny[0] + tiny[1]) + (tiny[2] + tiny[3]))
    total_attn = fold(kept, got_attn)
    gathered_attn = across([total_attn] * 3)
    last_b = swap(tie(feed_b, total_attn), "batch", 1)
    e_other = swap(tie(e_sum, total_attn), "head", 2)
    half = jnp.concatenate([total_attn] + [tie(g, last_b) for g in gathered_attn], axis=0)
    e_mate = swap(tie(e_near, half), "head", 1)
    last = swap(half, "batch", 1)
    biases = small[2:4]
    small = sum_group(tie(small, half))
    e_own = e_own.astype(F32) + e_mate.astype(F32) + tie(e_other, half).astype(F32)

    near_down = near[4].astype(F32) + near_down.astype(F32)
    output = (resid + near_down + tie(down_other, half).astype(F32) + bias_down).astype(BF)
    x_hat, x_rstd = normalize(tie(inputs, half).astype(F32))
    e_own = e_own * gain_attn
    grad_inputs = (
        grad_resid
        + x_rstd
        * (
            e_own
            - jnp.mean(e_own, axis=-1, keepdims=True)
            - x_hat * jnp.mean(e_own * x_hat, axis=-1, keepdims=True)
        )
    ).astype(BF)
    sum_wup, sum_wdown = unpack_call(bid, (feed_a, feed_b, last_a, tie(last_b, half)), (width, width))
    sum_wqkv, sum_wproj = unpack_call(bid, (half, tie(last, sum_wup, grad_inputs)), (cols, inner))
    return (
        output,
        grad_inputs,
        small[0],
        small[1],
        sum_wqkv.reshape(heads, triple, width).transpose(2, 0, 1),
        biases[0, :cols].reshape(heads, triple),
        sum_wproj.reshape(heads, inner // heads, width),
        small[4],
        small[5],
        small[6],
        sum_wup,
        biases[1],
        sum_wdown,
        small[7],
    )


def solution(mesh):
    rows = P(("batch", "head"), None)
    in_specs = (
        rows,
        P("batch", None),
        rows,
        P(),
        P(),
        P(None, "head", None),
        P("head", None),
        P("head", None, None),
        P(),
        P(),
        P(),
        P(None, "head"),
        P("head"),
        P("head", None),
        P(),
    )
    out_specs = (
        rows,
        rows,
        P(),
        P(),
        P(None, "head", None),
        P("head", None),
        P("head", None, None),
        P(),
        P(),
        P(),
        P(None, "head"),
        P("head"),
        P("head", None),
        P(),
    )
    return jax.shard_map(
        per_device, mesh=mesh, in_specs=in_specs, out_specs=out_specs, check_vma=False
    )
```

```python
import functools
import math

import jax
import jax.numpy as jnp
from jax import lax
from jax.experimental import pallas as pl
from jax.experimental.pallas import tpu as pltpu
from jax.sharding import PartitionSpec as P

F32 = jnp.float32
BF = jnp.bfloat16
BLK = 256
NEG = -1e30
EPS = 1e-05
GELU_C = math.sqrt(2.0 / math.pi)
GELU_A = 0.044715


def dot_nn(a, b):
    return lax.dot_general(a, b, (((1,), (0,)), ((), ())), preferred_element_type=F32)


def dot_nt(a, b):
    return lax.dot_general(a, b, (((1,), (1,)), ((), ())), preferred_element_type=F32)


def dot_tn(a, b):
    return lax.dot_general(a, b, (((0,), (0,)), ((), ())), preferred_element_type=F32)


def cost(flops, nbytes, trans=0):
    return pl.CostEstimate(flops=int(flops), bytes_accessed=int(nbytes), transcendentals=int(trans))


def swap(x, axis, bits):
    size = lax.axis_size(axis)
    return lax.ppermute(x, axis, [(i, i ^ bits) for i in range(size)])


def normalize(v):
    center = v - jnp.mean(v, axis=-1, keepdims=True)
    rstd = lax.rsqrt(jnp.mean(center * center, axis=-1, keepdims=True) + EPS)
    return center * rstd, rstd


def qkv_kernel(heads, hd, steps, h_ref, a_ref, b_ref, v_ref, w_ref, bias_ref, *rest):
    q_out, k_out, v_out, vt_out, hat_out = rest[-5:]
    t = pl.program_id(0)
    x = jnp.where(t < steps // 2, a_ref[...], b_ref[...]).astype(F32)
    xhat, _ = normalize(x)
    hat_out[...] = xhat.astype(BF)
    h1 = (xhat * v_ref[0:1, :] + v_ref[1:2, :]).astype(BF)
    bias = jnp.concatenate([bias_ref[h : h + 1, :] for h in range(heads)], axis=1)
    packed = (dot_nt(h1, w_ref[...]) + bias).astype(BF)
    for h in range(heads):
        o = 3 * hd * h
        q_out[h] = packed[:, o : o + hd]
        k_out[h] = packed[:, o + hd : o + 2 * hd]
        v = packed[:, o + 2 * hd : o + 3 * hd]
        v_out[h] = v
        vt_out[h] = v.T


def qkv_call(hid, a, b, vectors, w, bias, first, group_rows, before):
    rows, width = a.shape
    heads, triple = bias.shape
    hd = triple // 3
    per = rows // BLK
    steps = 2 * per
    place = lambda t, h: (h[0] ^ (first + t // per)) * per + t % per
    whole = lambda t, h: (0, 0)
    out_shape = tuple(
        jax.ShapeDtypeStruct(s, BF)
        for s in ((heads, group_rows, hd),) * 3 + ((heads, hd, group_rows), (group_rows, width))
    )
    in_specs = [
        pl.BlockSpec((BLK, width), lambda t, h: (jnp.minimum(t, per - 1), 0)),
        pl.BlockSpec((BLK, width), lambda t, h: (jnp.maximum(t - per, 0), 0)),
        pl.BlockSpec(vectors.shape, whole),
        pl.BlockSpec(w.shape, whole),
        pl.BlockSpec(bias.shape, whole),
    ] + [pl.BlockSpec(memory_space=pl.ANY)] * len(before)
    return pl.pallas_call(
        functools.partial(qkv_kernel, heads, hd, steps),
        out_shape=out_shape,
        grid_spec=pltpu.PrefetchScalarGridSpec(
            num_scalar_prefetch=1,
            grid=(steps,),
            in_specs=in_specs,
            out_specs=[pl.BlockSpec((heads, BLK, hd), lambda t, h: (0, place(t, h), 0))] * 3
            + [
                pl.BlockSpec((heads, hd, BLK), lambda t, h: (0, 0, place(t, h))),
                pl.BlockSpec((BLK, width), lambda t, h: (first * per + t, 0)),
            ],
        ),
        input_output_aliases={6 + i: i for i in range(len(before))},
        cost_estimate=cost(4 * rows * width * w.shape[0], 12 * rows * width),
        name="qkv",
    )(hid, a, b, vectors, w, bias, *before)


def row_segment(len_ref, row):
    low = row
    high = row + 1
    start = jnp.int32(0)
    for k in range(len_ref.shape[0] - 1):
        stop = start + len_ref[k]
        inside = (row >= start) & (row < stop)
        low = jnp.where(inside, start, low)
        high = jnp.where(inside, stop, high)
        start = stop
    return low, high


def lane_starts(len_ref, row, width):
    i = row + lax.broadcasted_iota(jnp.int32, (1, width), 1)
    start = jnp.zeros((1, width), jnp.int32)
    stop = jnp.int32(0)
    for k in range(len_ref.shape[0] - 1):
        stop = stop + len_ref[k]
        start = jnp.where(i >= stop, stop, start)
    return jnp.where(i >= stop, i, start), i


def attend_kernel(heads, first, per, scale, len_ref, h_ref, q_ref, k_ref, vt_ref, oa_ref, ob_ref, la_ref, lb_ref, s_s, m_s, z_s, acc_s):
    t = pl.program_id(0)
    row = ((h_ref[0] ^ (first + t // per)) * per + t % per) * BLK
    start, i = lane_starts(len_ref, row, BLK)
    low, _ = row_segment(len_ref, row)
    m_s[...] = jnp.zeros_like(m_s)
    z_s[...] = jnp.zeros_like(z_s)
    acc_s[...] = jnp.zeros_like(acc_s)
    qs = [q_ref[h] * jnp.asarray(scale, BF) for h in range(heads)]
    blocks = (low // BLK, row // BLK + 1)

    def measure(jb, carry):
        j0 = pl.multiple_of(jb * BLK, BLK)
        j = j0 + lax.broadcasted_iota(jnp.int32, (BLK, BLK), 0)
        mask = (j >= start) & (j <= i)
        scores = [dot_nt(k_ref[h, pl.ds(j0, BLK), :], qs[h]) for h in range(heads)]
        tops = [m_s[h : h + 1, :] for h in range(heads)]
        for h in range(heads):
            s = jnp.where(mask, scores[h], 0.0)
            s_s[h, pl.ds(j0, BLK), :] = s
            tops[h] = jnp.maximum(tops[h], jnp.max(jnp.abs(s), axis=0, keepdims=True))
        for h in range(heads):
            m_s[h : h + 1, :] = tops[h]
        return carry

    lax.fori_loop(*blocks, measure, 0)
    tops = [m_s[h : h + 1, :] for h in range(heads)]
    offsets = [jnp.exp(-top) for top in tops]

    def gather(jb, carry):
        j0 = pl.multiple_of(jb * BLK, BLK)
        sums, weights = [], []
        for h in range(heads):
            s = s_s[h, pl.ds(j0, BLK), :]
            u = jnp.exp(jnp.abs(s) - tops[h]) - offsets[h]
            sums.append(jnp.sum(u, axis=0, keepdims=True))
            weights.append(jnp.where(s < 0, -u, u).astype(BF))
        adds = [dot_nn(vt_ref[h, :, pl.ds(j0, BLK)], weights[h]) for h in range(heads)]
        for h in range(heads):
            z_s[h : h + 1, :] += sums[h]
            acc_s[h] += adds[h]
        return carry

    lax.fori_loop(*blocks, gather, 0)
    count = (i - start + 1).astype(F32)
    outs, levels = [], []
    for h in range(heads):
        z = z_s[h : h + 1, :] + count * offsets[h]
        outs.append((acc_s[h] / z).T)
        levels.append(tops[h] + jnp.log(z))
    out = jnp.concatenate(outs, axis=1).astype(BF)

    def store(o_ref, l_ref):
        o_ref[...] = out
        for h in range(heads):
            l_ref[h : h + 1, :] = levels[h]

    @pl.when(t < per)
    def _():
        store(oa_ref, la_ref)

    @pl.when(t >= per)
    def _():
        store(ob_ref, lb_ref)


def attend_call(lengths, hid, q, k, vt, first, chunk):
    heads, rows, hd = q.shape
    per = chunk // BLK
    steps = 2 * per
    place = lambda t, n, h: (0, (h[0] ^ (first + t // per)) * per + t % per, 0)
    whole = lambda t, n, h: (0, 0, 0)
    return pl.pallas_call(
        functools.partial(attend_kernel, heads, first, per, 1.0 / math.sqrt(hd)),
        out_shape=(jax.ShapeDtypeStruct((chunk, heads * hd), BF),) * 2
        + (jax.ShapeDtypeStruct((8, chunk), F32),) * 2,
        grid_spec=pltpu.PrefetchScalarGridSpec(
            num_scalar_prefetch=2,
            grid=(steps,),
            in_specs=[
                pl.BlockSpec((heads, BLK, hd), place),
                pl.BlockSpec((heads, rows, hd), whole),
                pl.BlockSpec((heads, hd, rows), whole),
            ],
            out_specs=[
                pl.BlockSpec((BLK, heads * hd), lambda t, n, h: (jnp.minimum(t, per - 1), 0)),
                pl.BlockSpec((BLK, heads * hd), lambda t, n, h: (jnp.maximum(t - per, 0), 0)),
                pl.BlockSpec((8, BLK), lambda t, n, h: (0, jnp.minimum(t, per - 1))),
                pl.BlockSpec((8, BLK), lambda t, n, h: (0, jnp.maximum(t - per, 0))),
            ],
            scratch_shapes=[
                pltpu.VMEM((heads, rows, BLK), F32),
                pltpu.VMEM((8, BLK), F32),
                pltpu.VMEM((8, BLK), F32),
                pltpu.VMEM((heads, hd, BLK), F32),
            ],
        ),
        cost_estimate=cost(heads * rows * rows * hd * 4, 12 * rows * heads * hd, heads * rows * rows // 4),
        name="attend",
    )(lengths, hid, q, k, vt)


def attend_back_kernel(chunk, scale, len_ref, h_ref, q_ref, k_ref, v_ref, *rest):
    g_refs, o_refs, l_refs = rest[0:4], rest[4:8], rest[8:12]
    gp_ref, q_s, g_s, kt_s, l_s, c_s, d_s, dq_s, dk_s, dv_s = rest[12:]
    heads, rows, hd = q_ref.shape
    blocks = rows // BLK
    per = chunk // BLK
    own = h_ref[0]
    for c in range(4):
        r0 = pl.multiple_of((own ^ c) * chunk, chunk)
        g = g_refs[c][...]
        o = o_refs[c][...]
        for h in range(heads):
            gh = g[:, h * hd : (h + 1) * hd]
            g_s[h, pl.ds(r0, chunk), :] = gh
            both = gh.astype(F32) * o[:, h * hd : (h + 1) * hd].astype(F32)
            d_s[h : h + 1, pl.ds(r0, chunk)] = jnp.sum(both.T, axis=0, keepdims=True)
        level = l_refs[c][...]
        l_s[:, pl.ds(r0, chunk)] = level
        c_s[:, pl.ds(r0, chunk)] = jnp.exp(-level)
    for h in range(heads):
        q_s[h] = q_ref[h] * jnp.asarray(scale, BF)
    dq_s[...] = jnp.zeros_like(dq_s)

    def out_row(block):
        return pl.multiple_of(((own ^ (block // per)) * per + block % per) * BLK, BLK)

    def outer(jb, carry):
        j0 = pl.multiple_of(jb * BLK, BLK)
        dk_s[...] = jnp.zeros_like(dk_s)
        dv_s[...] = jnp.zeros_like(dv_s)
        for h in range(heads):
            kt_s[h] = k_ref[h, pl.ds(j0, BLK), :].T
        _, stop = row_segment(len_ref, j0 + BLK - 1)
        j = j0 + lax.broadcasted_iota(jnp.int32, (BLK, BLK), 0)

        def inner(ib, carry):
            i0 = pl.multiple_of(ib * BLK, BLK)
            start, i = lane_starts(len_ref, i0, BLK)
            mask = (j >= start) & (j <= i)
            at = pl.ds(i0, BLK)
            qh = [q_s[h, at, :] for h in range(heads)]
            gh = [g_s[h, at, :] for h in range(heads)]
            scores = [dot_nt(k_ref[h, pl.ds(j0, BLK), :], qh[h]) for h in range(heads)]
            gws = [dot_nt(v_ref[h, pl.ds(j0, BLK), :], gh[h]) for h in range(heads)]
            ws, gss = [], []
            for h in range(heads):
                s, gw = scores[h], gws[h]
                level = l_s[h : h + 1, at]
                offset = c_s[h : h + 1, at]
                d = d_s[h : h + 1, at]
                p = jnp.exp(jnp.where(mask, jnp.abs(s), NEG) - level)
                u = p - jnp.where(mask, offset, 0.0)
                sign = jnp.clip(s * 1e38, -1.0, 1.0)
                w = (sign * u).astype(BF)
                gs = (p * (gw - sign * d)).astype(BF)
                ws.append(w)
                gss.append(gs)
            dvs = [dot_nn(ws[h], gh[h]) for h in range(heads)]
            dks = [dot_nn(gss[h], qh[h]) for h in range(heads)]
            dqs = [dot_nn(kt_s[h], gss[h]) for h in range(heads)]
            for h in range(heads):
                dv_s[h] += dvs[h]
                dk_s[h] += dks[h]
                dq_s[h, :, at] += dqs[h]
            return carry

        lax.fori_loop(jb, (stop - 1) // BLK + 1, inner, 0)
        for h in range(heads):
            at = pl.ds(out_row(jb), BLK)
            gp_ref[at, (3 * h + 1) * hd : (3 * h + 2) * hd] = dk_s[h].astype(BF)
            gp_ref[at, (3 * h + 2) * hd : (3 * h + 3) * hd] = dv_s[h].astype(BF)
        return carry

    lax.fori_loop(0, blocks, outer, 0)

    def finish(ib, carry):
        i0 = pl.multiple_of(ib * BLK, BLK)
        for h in range(heads):
            dq = (dq_s[h, :, pl.ds(i0, BLK)] * scale).T.astype(BF)
            gp_ref[pl.ds(out_row(ib), BLK), 3 * h * hd : (3 * h + 1) * hd] = dq
        return carry

    lax.fori_loop(0, blocks, finish, 0)


def attend_back_call(lengths, hid, q, k, v, grads, outs, levels, chunk):
    heads, rows, hd = q.shape
    vm = pl.BlockSpec(memory_space=pltpu.VMEM)
    sm = pl.BlockSpec(memory_space=pltpu.SMEM)
    return pl.pallas_call(
        functools.partial(attend_back_kernel, chunk, 1.0 / math.sqrt(hd)),
        out_shape=jax.ShapeDtypeStruct((rows, heads * 3 * hd), BF),
        in_specs=[sm, sm] + [vm] * 15,
        out_specs=vm,
        scratch_shapes=[
            pltpu.VMEM((heads, rows, hd), BF),
            pltpu.VMEM((heads, rows, hd), BF),
            pltpu.VMEM((heads, hd, BLK), BF),
            pltpu.VMEM((8, rows), F32),
            pltpu.VMEM((8, rows), F32),
            pltpu.VMEM((8, rows), F32),
            pltpu.VMEM((heads, hd, rows), F32),
            pltpu.VMEM((heads, BLK, hd), F32),
            pltpu.VMEM((heads, BLK, hd), F32),
        ],
        cost_estimate=cost(heads * rows * rows * hd * 20, 30 * rows * heads * hd, heads * rows * rows // 2),
        name="attend_back",
    )(lengths, hid, q, k, v, *grads, *outs, *levels)


def feed_kernel(steps, ha_ref, hb_ref, ga_ref, gb_ref, up_ref, v_ref, down_ref, *rest):
    act_ref, gup_ref, gna_ref, gnb_ref, outa_ref, outb_ref = rest[-6:]
    early = pl.program_id(0) < steps // 2
    h2 = jnp.where(early, ha_ref[...], hb_ref[...])
    grad = jnp.where(early, ga_ref[...], gb_ref[...])
    u = dot_nn(h2, up_ref[...]) + v_ref[5:6, :]
    square = u * u
    tanh = jnp.tanh(u * (GELU_C + (GELU_C * GELU_A) * square))
    half = 0.5 * (1.0 + tanh)
    act = (u * half).astype(BF)
    slope = half + (0.5 * u) * (1.0 - tanh * tanh) * (GELU_C + (3.0 * GELU_C * GELU_A) * square)
    gup = (dot_nt(grad, down_ref[...]) * slope).astype(BF)
    act_ref[...] = act
    gup_ref[...] = gup
    gn = dot_nt(gup, up_ref[...]).astype(BF)
    out = dot_nn(act, down_ref[...]).astype(BF)

    @pl.when(early)
    def _():
        gna_ref[...] = gn
        outa_ref[...] = out

    @pl.when(jnp.logical_not(early))
    def _():
        gnb_ref[...] = gn
        outb_ref[...] = out


def feed_call(ha, hb, ga, gb, up, vectors, down, first, group_rows, before):
    rows, width = ha.shape
    hidden = up.shape[1]
    per = rows // BLK
    steps = 2 * per
    whole = lambda t: (0, 0)
    early = pl.BlockSpec((BLK, width), lambda t: (jnp.minimum(t, per - 1), 0))
    late = pl.BlockSpec((BLK, width), lambda t: (jnp.maximum(t - per, 0), 0))
    return pl.pallas_call(
        functools.partial(feed_kernel, steps),
        out_shape=(
            jax.ShapeDtypeStruct((group_rows, hidden), BF),
            jax.ShapeDtypeStruct((group_rows, hidden), BF),
        )
        + (jax.ShapeDtypeStruct((rows, width), BF),) * 4,
        grid=(steps,),
        in_specs=[
            early,
            late,
            early,
            late,
            pl.BlockSpec(up.shape, whole),
            pl.BlockSpec(vectors.shape, whole),
            pl.BlockSpec(down.shape, whole),
        ]
        + [pl.BlockSpec(memory_space=pl.ANY)] * len(before),
        out_specs=[
            pl.BlockSpec((BLK, hidden), lambda t: (first * per + t, 0)),
            pl.BlockSpec((BLK, hidden), lambda t: (first * per + t, 0)),
            early,
            late,
            early,
            late,
        ],
        input_output_aliases={7 + i: i for i in range(len(before))},
        cost_estimate=cost(16 * rows * width * hidden, 16 * rows * width, 2 * rows * hidden),
        name="feed",
    )(ha, hb, ga, gb, up, vectors, down, *before)


def spots(b_ref, pieces):
    return [b_ref[0] ^ (2 * (spot % 4) + spot // 4) for spot in range(pieces)]


def split_out(b_ref, acc, keep_ref, send_ref):
    piece = acc.shape[0] // 8
    for spot, block in enumerate(spots(b_ref, 8)):
        out = keep_ref if spot < 4 else send_ref
        value = acc[pl.ds(pl.multiple_of(block * piece, 8), piece), :]
        out[(spot % 4) * piece : (spot % 4 + 1) * piece, :] = value.astype(BF)


def weigh_kernel(tiles, b_ref, h0, h1, h2, h3, act_ref, up_ref, g0, g1, g2, g3, keep_ref, send_ref, bias_ref, acc):
    t = pl.program_id(0)
    tile = acc.shape[0] // (2 * tiles)
    chunk = h0.shape[0]
    at = pl.ds(pl.multiple_of(t * tile, tile), tile)

    @pl.when(t == 0)
    def _():
        bias_ref[...] = jnp.sum(up_ref[...].astype(F32), axis=0, keepdims=True)

    @pl.when(t < tiles)
    def _():
        total = dot_tn(h0[...], up_ref[:chunk, :])
        for k, h in enumerate((h1, h2, h3)):
            total = total + dot_tn(h[...], up_ref[(k + 1) * chunk : (k + 2) * chunk, :])
        acc[at, :] = total

    @pl.when(t >= tiles)
    def _():
        total = dot_tn(act_ref[:chunk, :], g0[...])
        for k, g in enumerate((g1, g2, g3)):
            total = total + dot_tn(act_ref[(k + 1) * chunk : (k + 2) * chunk, :], g[...])
        acc[at, :] = total

    @pl.when(t == 2 * tiles - 1)
    def _():
        split_out(b_ref, acc, keep_ref, send_ref)


def weigh_call(bid, hs, act, up, grads):
    chunk, width = hs[0].shape
    rows, hidden = act.shape
    tile = 256
    tiles = width // tile
    whole = lambda t, b: (0, 0)
    total = width + hidden
    half = jax.ShapeDtypeStruct((total // 2, width), BF)
    return pl.pallas_call(
        functools.partial(weigh_kernel, tiles),
        out_shape=(half, half, jax.ShapeDtypeStruct((1, hidden), F32)),
        grid_spec=pltpu.PrefetchScalarGridSpec(
            num_scalar_prefetch=1,
            grid=(2 * tiles,),
            in_specs=[pl.BlockSpec((chunk, tile), lambda t, b: (0, jnp.minimum(t, tiles - 1)))] * 4
            + [
                pl.BlockSpec((rows, tile), lambda t, b: (0, jnp.maximum(t - tiles, 0))),
                pl.BlockSpec((rows, hidden), whole),
            ]
            + [pl.BlockSpec((chunk, width), whole)] * 4,
            out_specs=[
                pl.BlockSpec(half.shape, whole),
                pl.BlockSpec(half.shape, whole),
                pl.BlockSpec((1, hidden), whole),
            ],
            scratch_shapes=[pltpu.VMEM((total, width), F32)],
        ),
        cost_estimate=cost(4 * rows * width * hidden, 12 * rows * width),
        name="weigh",
    )(bid, *hs, act, up, *grads)


def mix_kernel(m0, m1, m2, m3, p0, p1, p2, p3, x_ref, v_ref, resid_ref, h_ref):
    total = x_ref[...].astype(F32) + v_ref[2:3, :]
    for m, p in ((m0, p0), (m1, p1), (m2, p2), (m3, p3)):
        total = total + dot_nn(m[...], p[...])
    resid_ref[...] = total
    hat, _ = normalize(total)
    h_ref[...] = (hat * v_ref[3:4, :] + v_ref[4:5, :]).astype(BF)


def mix_call(parts, projs, x, vectors):
    rows, width = x.shape
    per = rows // BLK
    inner = parts[0].shape[1]
    low = pl.BlockSpec((BLK, inner), lambda t: (t, 0))
    whole = lambda t: (0, 0)
    return pl.pallas_call(
        mix_kernel,
        out_shape=(jax.ShapeDtypeStruct((rows, width), F32), jax.ShapeDtypeStruct((rows, width), BF)),
        grid=(per,),
        in_specs=[low] * 4
        + [pl.BlockSpec(projs[0].shape, whole)] * 4
        + [pl.BlockSpec((BLK, width), lambda t: (t, 0)), pl.BlockSpec(vectors.shape, whole)],
        out_specs=[pl.BlockSpec((BLK, width), lambda t: (t, 0))] * 2,
        cost_estimate=cost(8 * rows * width * inner, 12 * rows * width),
        name="mix",
    )(*parts, *projs, x, vectors)


def turn_kernel(n_ref, s_ref, f_ref, resid_ref, cot_ref, v_ref, p0, p1, p2, p3, gr_ref, ga_ref, g0, g1, g2, g3, sum_ref):
    grad = n_ref[...].astype(F32) + s_ref[...].astype(F32) + f_ref[...].astype(F32)
    hat, rstd = normalize(resid_ref[...])
    cot = cot_ref[...].astype(F32)
    e = grad * v_ref[3:4, :]
    back = e - jnp.mean(e, axis=-1, keepdims=True) - hat * jnp.mean(e * hat, axis=-1, keepdims=True)
    grad_resid = cot + rstd * back
    gr_ref[...] = grad_resid
    att = grad_resid.astype(BF)
    ga_ref[...] = att
    for g, p in ((g0, p0), (g1, p1), (g2, p2), (g3, p3)):
        g[...] = dot_nt(att, p[...]).astype(BF)

    @pl.when(pl.program_id(0) == 0)
    def _():
        sum_ref[...] = jnp.zeros_like(sum_ref)

    for k, v in enumerate((grad_resid, grad * hat, grad, cot)):
        sum_ref[k + 4 : k + 5, :] += jnp.sum(v, axis=0, keepdims=True)


def turn_call(near, swapped, far, resid, cot, vectors, projs):
    rows, width = resid.shape
    per = rows // BLK
    inner = projs[0].shape[0]
    low = pl.BlockSpec((BLK, width), lambda t: (t, 0))
    whole = lambda t: (0, 0)
    return pl.pallas_call(
        turn_kernel,
        out_shape=(
            jax.ShapeDtypeStruct((rows, width), F32),
            jax.ShapeDtypeStruct((rows, width), BF),
        )
        + (jax.ShapeDtypeStruct((rows, inner), BF),) * 4
        + (jax.ShapeDtypeStruct((8, width), F32),),
        grid=(per,),
        in_specs=[low] * 5
        + [pl.BlockSpec(vectors.shape, whole)]
        + [pl.BlockSpec(projs[0].shape, whole)] * 4,
        out_specs=[low, low]
        + [pl.BlockSpec((BLK, inner), lambda t: (t, 0))] * 4
        + [pl.BlockSpec((8, width), whole)],
        cost_estimate=cost(rows, width),
        name="turn",
    )(near, swapped, far, resid, cot, vectors, *projs)


def tally_kernel(steps, b_ref, gp_ref, hat_ref, w_ref, v_ref, pw_ref, up_ref, s_ref, keep_ref, send_ref, acc, col):
    t = pl.program_id(0)
    gp = gp_ref[...]
    cols = gp.shape[1]
    half = acc.shape[0] // 2

    @pl.when(t == 0)
    def _():
        acc[:cols, :] = jnp.zeros((cols, acc.shape[1]), F32)
        acc[cols:, :] = pw_ref[...]
        col[...] = jnp.zeros_like(col)

    acc[:cols, :] += dot_tn(gp, hat_ref[...])
    col[...] += dot_tn(gp, jnp.ones((gp.shape[0], 128), BF))

    @pl.when(t == steps - 1)
    def _():
        total = col[:, 0:1]
        moment = acc[:cols, :]
        w = w_ref[...].astype(F32)
        small = s_ref[...]
        row = lax.broadcasted_iota(jnp.int32, small.shape, 0)
        small = jnp.where(row == 0, jnp.sum(w * moment, axis=0, keepdims=True), small)
        small = jnp.where(row == 1, jnp.sum(w * total, axis=0, keepdims=True), small)
        bias = jnp.concatenate((col[...].T[0:1, :], jnp.zeros((1, small.shape[1] - cols), F32)), axis=1)
        small = jnp.where(row == 2, bias, small)
        small = jnp.where(row == 3, up_ref[...], small).astype(BF)
        acc[:cols, :] = moment * v_ref[0:1, :] + total * v_ref[1:2, :]
        split_out(b_ref, acc, keep_ref, send_ref)
        keep_ref[half:, :] = small
        send_ref[half:, :] = small


def tally_call(bid, gp, hat, w, vectors, proj_grad, up_grad, sums):
    rows, width = hat.shape
    cols = gp.shape[1]
    total = cols + proj_grad.shape[0]
    block = 2 * BLK
    steps = rows // block
    whole = lambda t, b: (0, 0)
    half = jax.ShapeDtypeStruct((total // 2 + sums.shape[0], width), BF)
    return pl.pallas_call(
        functools.partial(tally_kernel, steps),
        out_shape=(half, half),
        grid_spec=pltpu.PrefetchScalarGridSpec(
            num_scalar_prefetch=1,
            grid=(steps,),
            in_specs=[
                pl.BlockSpec((block, cols), lambda t, b: (t, 0)),
                pl.BlockSpec((block, width), lambda t, b: (t, 0)),
            ]
            + [pl.BlockSpec(v.shape, whole) for v in (w, vectors, proj_grad, up_grad, sums)],
            out_specs=[pl.BlockSpec(half.shape, whole)] * 2,
            scratch_shapes=[pltpu.VMEM((total, width), F32), pltpu.VMEM((cols, 128), F32)],
        ),
        cost_estimate=cost(cols, width),
        name="tally",
    )(bid, gp, hat, w, vectors, proj_grad, up_grad, sums)


def spread_kernel(gp_ref, w_ref, *outs):
    e = dot_nn(gp_ref[...], w_ref[...]).astype(BF)
    for k, out in enumerate(outs):

        @pl.when(pl.program_id(0) == k)
        def _(out=out):
            out[...] = e


def spread_call(gp, w, chunk):
    cols, width = w.shape
    whole = lambda t: (0, 0)
    return pl.pallas_call(
        spread_kernel,
        out_shape=(jax.ShapeDtypeStruct((chunk, width), BF),) * 4,
        grid=(4,),
        in_specs=[pl.BlockSpec((chunk, cols), lambda t: (t, 0)), pl.BlockSpec(w.shape, whole)],
        out_specs=[pl.BlockSpec((chunk, width), whole)] * 4,
        cost_estimate=cost(cols, width),
        name="spread",
    )(gp, w)


def unpack_kernel(counts, places, b_ref, *rest):
    acc = rest[-1]
    piece = acc.shape[0] // 8
    for (part, at), block in zip(places, spots(b_ref, 8), strict=True):
        value = rest[part][at : at + piece, :].astype(F32)
        acc[pl.ds(pl.multiple_of(block * piece, 8), piece), :] = value
    start = 0
    for out, count in zip(rest[-1 - len(counts) : -1], counts, strict=True):
        out[...] = acc[start : start + count, :]
        start += count


def unpack_call(bid, parts, places, counts):
    total = sum(counts)
    width = parts[0].shape[1]
    vm = pl.BlockSpec(memory_space=pltpu.VMEM)
    return pl.pallas_call(
        functools.partial(unpack_kernel, counts, places),
        out_shape=tuple(jax.ShapeDtypeStruct((n, width), F32) for n in counts),
        in_specs=[pl.BlockSpec(memory_space=pltpu.SMEM)] + [vm] * len(parts),
        out_specs=[vm] * len(counts),
        scratch_shapes=[pltpu.VMEM((total, width), F32)],
        cost_estimate=cost(total, width),
        name="unpack",
    )(bid, *parts)


def tie(x, *needed):
    return lax.optimization_barrier((x,) + needed)[0]


def across(pieces):
    return [swap(piece, "batch", 2 * d) for d, piece in enumerate(pieces, 1)]


def sum_rest(x):
    for level in range(3, lax.axis_size("batch").bit_length() - 1):
        x = (x.astype(F32) + swap(x, "batch", 1 << level).astype(F32)).astype(x.dtype)
    return x


def fold(kept, got):
    piece = kept.shape[0] // 4
    total = kept[:piece].astype(F32)
    for g in got:
        total = total + g[:piece].astype(F32)
    return sum_rest(total.astype(BF))


def quarters(x):
    piece = x.shape[0] // 4
    return [x[d * piece : (d + 1) * piece] for d in range(1, 4)]


def sum_group(x):
    x = x + swap(x, "head", 1)
    return x + swap(x, "head", 2)


def per_device(
    inputs,
    lengths,
    cotangent,
    gain_attn,
    shift_attn,
    weight_qkv,
    bias_qkv,
    weight_proj,
    bias_proj,
    gain_mlp,
    shift_mlp,
    weight_up,
    bias_up,
    weight_down,
    bias_down,
):
    chunk, width = inputs.shape
    group_rows = chunk * lax.axis_size("head")
    heads, triple = weight_qkv.shape[1:]
    cols = heads * triple
    inner = cols // 3
    own = lax.axis_index("head")
    hid = own.astype(jnp.int32).reshape(1)
    bid = (lax.axis_index("batch") % 8).astype(jnp.int32).reshape(1)
    lens = lengths[0]
    live_rows = jnp.sum(lens[:-1])
    places = own * chunk + jnp.arange(chunk, dtype=jnp.int32)
    live = (places < live_rows)[:, None]
    qkv_t = weight_qkv.transpose(1, 2, 0).reshape(cols, width)
    proj = weight_proj.reshape(inner, width)
    zero = jnp.zeros((width,), F32)
    vectors = jnp.stack(
        (gain_attn, shift_attn, bias_proj, gain_mlp, shift_mlp, bias_up, bias_down, zero)
    )

    x_far = swap(inputs, "head", 2)
    x_near = swap(inputs, "head", 1)
    begun = qkv_call(hid, inputs, x_near, vectors, qkv_t, bias_qkv, 0, group_rows, ())
    x_far = tie(x_far, begun[0])
    x_last = swap(x_far, "head", 1)
    queries, keys, values, values_t, hats = qkv_call(
        hid, x_far, x_last, vectors, qkv_t, bias_qkv, 2, group_rows, begun
    )
    grad_own = jnp.where(live, cotangent, jnp.zeros_like(cotangent))
    grad_far = swap(tie(grad_own, x_far), "head", 2)
    proj_far = swap(tie(proj, x_far), "head", 2)
    out_far, out_last, level_far, level_last = attend_call(
        lens, hid, queries, keys, values_t, 2, chunk
    )
    from_last = swap(out_last, "head", 2)
    from_far = swap(out_far, "head", 2)
    out_own, out_mate, level_own, level_mate = attend_call(
        lens, hid, tie(queries, out_far, grad_far, proj_far), keys, values_t, 0, chunk
    )
    grads = (grad_own, swap(grad_own, "head", 1), grad_far, swap(grad_far, "head", 1))
    from_last = swap(tie(from_last, out_own, from_far), "head", 1)
    parts = (out_own, swap(out_mate, "head", 1), from_far, from_last)
    proj_last = swap(tie(proj_far, out_own), "head", 1)
    projs = (proj, swap(tie(proj, out_far), "head", 1), proj_far, proj_last)
    resid, h_own = mix_call(parts, projs, inputs, vectors)
    h_far = swap(h_own, "head", 2)
    h_near = swap(h_own, "head", 1)

    near = feed_call(h_own, h_near, grads[0], grads[1], weight_up, vectors, weight_down, 0, group_rows, ())
    h_far = tie(h_far, near[0])
    h_last = swap(h_far, "head", 1)
    act, grad_up, norm_far, norm_last, down_far, down_last = feed_call(
        h_far, h_last, grads[2], grads[3], weight_up, vectors, weight_down, 2, group_rows, near[:2]
    )
    far_sum = (norm_far.astype(F32) + swap(norm_last, "head", 1).astype(F32)).astype(BF)
    grad_far_sum = swap(far_sum, "head", 2)
    near_swapped = swap(near[3], "head", 1)
    down_swapped = swap(tie(down_last, far_sum), "head", 1)
    near_down = swap(tie(near[5], far_sum), "head", 1)

    keep_feed, send_feed, grad_bup = weigh_call(
        bid, (h_own, h_near, h_far, h_last), tie(act, far_sum), grad_up, grads
    )
    other_feed = swap(send_feed, "batch", 1)
    grad_resid, grad_att, grad_near, grad_mate, grad_cross, grad_last, sums = turn_call(
        near[2],
        near_swapped,
        tie(grad_far_sum, grad_bup, down_swapped, near_down),
        resid,
        grad_own,
        vectors,
        projs,
    )
    got_last = swap(grad_last, "head", 2)
    got = swap(grad_cross, "head", 2)
    grad_mate = swap(grad_mate, "head", 1)
    grad_att = tie(grad_att, grad_mate)
    grad_proj = [dot_tn(p, grad_att) for p in parts]
    near_sent, far_sent = grad_proj[1].astype(BF), grad_proj[3].astype(BF)
    down_far = tie(down_far, grad_att)
    down_sum = (down_far.astype(F32) + down_swapped.astype(F32)).astype(BF)
    got_last = tie(got_last, near_sent, far_sent, down_sum)
    merged_grads = (grad_near, grad_mate, got, swap(got_last, "head", 1))
    grad_near_proj = grad_proj[0] + swap(near_sent, "head", 1).astype(F32)
    far_proj = (grad_proj[2] + swap(far_sent, "head", 1).astype(F32)).astype(BF)
    far_proj = swap(far_proj, "head", 2)

    kept_feed = (keep_feed.astype(F32) + tie(other_feed, got).astype(F32)).astype(BF)
    got_feed = across(quarters(kept_feed))
    down_other = swap(tie(down_sum, kept_feed), "head", 2)

    grad_packed = attend_back_call(
        lens,
        hid,
        tie(queries, kept_feed, grad_near_proj),
        keys,
        values,
        merged_grads,
        (out_own, out_mate, out_far, out_last),
        (level_own, level_mate, level_far, level_last),
        chunk,
    )
    got_feed = [tie(g, grad_packed) for g in got_feed]
    grad_wproj = grad_near_proj + tie(far_proj, grad_packed).astype(F32)
    total_feed = fold(kept_feed, got_feed)
    gathered_feed = across([total_feed] * 3)
    keep, send = tally_call(
        bid, tie(grad_packed, total_feed, down_other), hats, qkv_t, vectors, grad_wproj, grad_bup, sums
    )
    other = swap(send, "batch", 1)
    spread = spread_call(tie(grad_packed, keep), qkv_t, chunk)
    gathered_feed, spread = lax.optimization_barrier((gathered_feed, spread))
    e_own, e_near, e_far, e_last = spread

    feed_first = jnp.concatenate((total_feed, gathered_feed[0]), axis=0)
    feed_second = jnp.concatenate(gathered_feed[1:], axis=0)
    feed_got = swap(feed_first, "batch", 1)
    summed = (keep.astype(F32) + tie(other, feed_first, feed_second).astype(F32)).astype(BF)
    kept, small = summed[:-8], summed[-8:]
    pieces = [jnp.concatenate((q, small), axis=0) for q in quarters(kept)]
    e_swapped = swap(tie(e_last, *pieces), "head", 1)
    e_sum = (e_far.astype(F32) + e_swapped.astype(F32)).astype(BF)
    output = resid + near[4].astype(F32) + near_down.astype(F32) + tie(down_other, e_sum).astype(F32)
    output = (output + bias_down).astype(BF)
    got_attn = [tie(g, feed_got, output) for g in across(pieces)]

    tiny = [small.astype(F32)] + [g[-8:].astype(F32) for g in got_attn]
    small = sum_rest((tiny[0] + tiny[1]) + (tiny[2] + tiny[3]))
    total_attn = fold(kept, got_attn)
    gathered_attn = across([total_attn] * 3)
    second_got = swap(tie(feed_second, total_attn), "batch", 1)
    e_other = swap(tie(e_sum, total_attn), "head", 2)
    half = jnp.concatenate([total_attn] + [tie(g, second_got) for g in gathered_attn], axis=0)
    e_mate = swap(tie(e_near, half), "head", 1)
    last = swap(half, "batch", 1)
    biases = small[2:4]
    small = sum_group(tie(small, half))
    e_own = e_own.astype(F32) + e_mate.astype(F32) + tie(e_other, half).astype(F32)

    x_hat, x_rstd = normalize(tie(inputs, half).astype(F32))
    e_own = e_own * gain_attn
    grad_inputs = (
        grad_resid
        + x_rstd
        * (
            e_own
            - jnp.mean(e_own, axis=-1, keepdims=True)
            - x_hat * jnp.mean(e_own * x_hat, axis=-1, keepdims=True)
        )
    ).astype(BF)
    pair = tuple(k * total_feed.shape[0] for k in range(2))
    places = tuple((k, at) for k in range(4) for at in pair)
    parts = (feed_first, feed_second, feed_got, tie(second_got, half))
    sum_wup, sum_wdown = unpack_call(bid, parts, places, (width, width))
    places = tuple((k, at * total_attn.shape[0]) for k in range(2) for at in range(4))
    parts = (half, tie(last, sum_wup, grad_inputs))
    sum_wqkv, sum_wproj = unpack_call(bid, parts, places, (cols, inner))
    return (
        output,
        grad_inputs,
        small[0],
        small[1],
        sum_wqkv.reshape(heads, triple, width).transpose(2, 0, 1),
        biases[0, :cols].reshape(heads, triple),
        sum_wproj.reshape(heads, inner // heads, width),
        small[4],
        small[5],
        small[6],
        sum_wup,
        biases[1],
        sum_wdown,
        small[7],
    )


def solution(mesh):
    rows = P(("batch", "head"), None)
    in_specs = (
        rows,
        P("batch", None),
        rows,
        P(),
        P(),
        P(None, "head", None),
        P("head", None),
        P("head", None, None),
        P(),
        P(),
        P(),
        P(None, "head"),
        P("head"),
        P("head", None),
        P(),
    )
    out_specs = (
        rows,
        rows,
        P(),
        P(),
        P(None, "head", None),
        P("head", None),
        P("head", None, None),
        P(),
        P(),
        P(),
        P(None, "head"),
        P("head"),
        P("head", None),
        P(),
    )
    return jax.shard_map(
        per_device, mesh=mesh, in_specs=in_specs, out_specs=out_specs, check_vma=False
    )
```

```python
import functools
import math

import jax
import jax.numpy as jnp
from jax import lax
from jax.experimental import pallas as pl
from jax.experimental.pallas import tpu as pltpu
from jax.sharding import PartitionSpec as P

F32 = jnp.float32
BF = jnp.bfloat16
BLK = 256
NEG = -1e30
EPS = 1e-05
GELU_C = math.sqrt(2.0 / math.pi)
GELU_A = 0.044715


def dot_nn(a, b):
    return lax.dot_general(a, b, (((1,), (0,)), ((), ())), preferred_element_type=F32)


def dot_nt(a, b):
    return lax.dot_general(a, b, (((1,), (1,)), ((), ())), preferred_element_type=F32)


def dot_tn(a, b):
    return lax.dot_general(a, b, (((0,), (0,)), ((), ())), preferred_element_type=F32)


def cost(flops, nbytes, trans=0):
    return pl.CostEstimate(flops=int(flops), bytes_accessed=int(nbytes), transcendentals=int(trans))


def swap(x, axis, bits):
    size = lax.axis_size(axis)
    return lax.ppermute(x, axis, [(i, i ^ bits) for i in range(size)])


def normalize(v):
    center = v - jnp.mean(v, axis=-1, keepdims=True)
    rstd = lax.rsqrt(jnp.mean(center * center, axis=-1, keepdims=True) + EPS)
    return center * rstd, rstd


def qkv_kernel(heads, hd, steps, h_ref, a_ref, b_ref, v_ref, w_ref, bias_ref, *rest):
    q_out, k_out, v_out, vt_out, hat_out = rest[-5:]
    t = pl.program_id(0)
    x = jnp.where(t < steps // 2, a_ref[...], b_ref[...]).astype(F32)
    xhat, _ = normalize(x)
    hat_out[...] = xhat.astype(BF)
    h1 = (xhat * v_ref[0:1, :] + v_ref[1:2, :]).astype(BF)
    bias = jnp.concatenate([bias_ref[h : h + 1, :] for h in range(heads)], axis=1)
    packed = (dot_nt(h1, w_ref[...]) + bias).astype(BF)
    for h in range(heads):
        o = 3 * hd * h
        q_out[h] = packed[:, o : o + hd]
        k_out[h] = packed[:, o + hd : o + 2 * hd]
        v = packed[:, o + 2 * hd : o + 3 * hd]
        v_out[h] = v
        vt_out[h] = v.T


def qkv_call(hid, a, b, vectors, w, bias, first, group_rows, before):
    rows, width = a.shape
    heads, triple = bias.shape
    hd = triple // 3
    per = rows // BLK
    steps = 2 * per
    place = lambda t, h: (h[0] ^ (first + t // per)) * per + t % per
    whole = lambda t, h: (0, 0)
    out_shape = tuple(
        jax.ShapeDtypeStruct(s, BF)
        for s in ((heads, group_rows, hd),) * 3 + ((heads, hd, group_rows), (group_rows, width))
    )
    in_specs = [
        pl.BlockSpec((BLK, width), lambda t, h: (jnp.minimum(t, per - 1), 0)),
        pl.BlockSpec((BLK, width), lambda t, h: (jnp.maximum(t - per, 0), 0)),
        pl.BlockSpec(vectors.shape, whole),
        pl.BlockSpec(w.shape, whole),
        pl.BlockSpec(bias.shape, whole),
    ] + [pl.BlockSpec(memory_space=pl.ANY)] * len(before)
    return pl.pallas_call(
        functools.partial(qkv_kernel, heads, hd, steps),
        out_shape=out_shape,
        grid_spec=pltpu.PrefetchScalarGridSpec(
            num_scalar_prefetch=1,
            grid=(steps,),
            in_specs=in_specs,
            out_specs=[pl.BlockSpec((heads, BLK, hd), lambda t, h: (0, place(t, h), 0))] * 3
            + [
                pl.BlockSpec((heads, hd, BLK), lambda t, h: (0, 0, place(t, h))),
                pl.BlockSpec((BLK, width), lambda t, h: (first * per + t, 0)),
            ],
        ),
        input_output_aliases={6 + i: i for i in range(len(before))},
        cost_estimate=cost(4 * rows * width * w.shape[0], 12 * rows * width),
        name="qkv",
    )(hid, a, b, vectors, w, bias, *before)


def row_segment(len_ref, row):
    low = row
    high = row + 1
    start = jnp.int32(0)
    for k in range(len_ref.shape[0] - 1):
        stop = start + len_ref[k]
        inside = (row >= start) & (row < stop)
        low = jnp.where(inside, start, low)
        high = jnp.where(inside, stop, high)
        start = stop
    return low, high


def lane_starts(len_ref, row, width):
    i = row + lax.broadcasted_iota(jnp.int32, (1, width), 1)
    start = jnp.zeros((1, width), jnp.int32)
    stop = jnp.int32(0)
    for k in range(len_ref.shape[0] - 1):
        stop = stop + len_ref[k]
        start = jnp.where(i >= stop, stop, start)
    return jnp.where(i >= stop, i, start), i


def attend_kernel(heads, first, per, scale, len_ref, h_ref, q_ref, k_ref, vt_ref, oa_ref, ob_ref, la_ref, lb_ref, s_s, m_s, z_s, acc_s):
    t = pl.program_id(0)
    row = ((h_ref[0] ^ (first + t // per)) * per + t % per) * BLK
    start, i = lane_starts(len_ref, row, BLK)
    low, _ = row_segment(len_ref, row)
    m_s[...] = jnp.zeros_like(m_s)
    z_s[...] = jnp.zeros_like(z_s)
    acc_s[...] = jnp.zeros_like(acc_s)
    qs = [q_ref[h] * jnp.asarray(scale, BF) for h in range(heads)]
    blocks = (low // BLK, row // BLK + 1)

    def measure(jb, carry):
        j0 = pl.multiple_of(jb * BLK, BLK)
        j = j0 + lax.broadcasted_iota(jnp.int32, (BLK, BLK), 0)
        mask = (j >= start) & (j <= i)
        scores = [dot_nt(k_ref[h, pl.ds(j0, BLK), :], qs[h]) for h in range(heads)]
        tops = [m_s[h : h + 1, :] for h in range(heads)]
        for h in range(heads):
            s = jnp.where(mask, scores[h], 0.0)
            s_s[h, pl.ds(j0, BLK), :] = s
            tops[h] = jnp.maximum(tops[h], jnp.max(jnp.abs(s), axis=0, keepdims=True))
        for h in range(heads):
            m_s[h : h + 1, :] = tops[h]
        return carry

    lax.fori_loop(*blocks, measure, 0)
    tops = [m_s[h : h + 1, :] for h in range(heads)]
    offsets = [jnp.exp(-top) for top in tops]

    def gather(jb, carry):
        j0 = pl.multiple_of(jb * BLK, BLK)
        sums, weights = [], []
        for h in range(heads):
            s = s_s[h, pl.ds(j0, BLK), :]
            u = jnp.exp(jnp.abs(s) - tops[h]) - offsets[h]
            sums.append(jnp.sum(u, axis=0, keepdims=True))
            weights.append(jnp.where(s < 0, -u, u).astype(BF))
        adds = [dot_nn(vt_ref[h, :, pl.ds(j0, BLK)], weights[h]) for h in range(heads)]
        for h in range(heads):
            z_s[h : h + 1, :] += sums[h]
            acc_s[h] += adds[h]
        return carry

    lax.fori_loop(*blocks, gather, 0)
    count = (i - start + 1).astype(F32)
    outs, levels = [], []
    for h in range(heads):
        z = z_s[h : h + 1, :] + count * offsets[h]
        outs.append((acc_s[h] / z).T)
        levels.append(tops[h] + jnp.log(z))
    out = jnp.concatenate(outs, axis=1).astype(BF)

    def store(o_ref, l_ref):
        o_ref[...] = out
        for h in range(heads):
            l_ref[h : h + 1, :] = levels[h]

    @pl.when(t < per)
    def _():
        store(oa_ref, la_ref)

    @pl.when(t >= per)
    def _():
        store(ob_ref, lb_ref)


def attend_call(lengths, hid, q, k, vt, first, chunk):
    heads, rows, hd = q.shape
    per = chunk // BLK
    steps = 2 * per
    place = lambda t, n, h: (0, (h[0] ^ (first + t // per)) * per + t % per, 0)
    whole = lambda t, n, h: (0, 0, 0)
    return pl.pallas_call(
        functools.partial(attend_kernel, heads, first, per, 1.0 / math.sqrt(hd)),
        out_shape=(jax.ShapeDtypeStruct((chunk, heads * hd), BF),) * 2
        + (jax.ShapeDtypeStruct((8, chunk), F32),) * 2,
        grid_spec=pltpu.PrefetchScalarGridSpec(
            num_scalar_prefetch=2,
            grid=(steps,),
            in_specs=[
                pl.BlockSpec((heads, BLK, hd), place),
                pl.BlockSpec((heads, rows, hd), whole),
                pl.BlockSpec((heads, hd, rows), whole),
            ],
            out_specs=[
                pl.BlockSpec((BLK, heads * hd), lambda t, n, h: (jnp.minimum(t, per - 1), 0)),
                pl.BlockSpec((BLK, heads * hd), lambda t, n, h: (jnp.maximum(t - per, 0), 0)),
                pl.BlockSpec((8, BLK), lambda t, n, h: (0, jnp.minimum(t, per - 1))),
                pl.BlockSpec((8, BLK), lambda t, n, h: (0, jnp.maximum(t - per, 0))),
            ],
            scratch_shapes=[
                pltpu.VMEM((heads, rows, BLK), F32),
                pltpu.VMEM((8, BLK), F32),
                pltpu.VMEM((8, BLK), F32),
                pltpu.VMEM((heads, hd, BLK), F32),
            ],
        ),
        cost_estimate=cost(rows, hd),
        name="attend",
    )(lengths, hid, q, k, vt)


def attend_back_kernel(chunk, scale, len_ref, h_ref, q_ref, k_ref, v_ref, *rest):
    g_refs, o_refs, l_refs = rest[0:4], rest[4:8], rest[8:12]
    gp_ref, q_s, g_s, kt_s, l_s, c_s, d_s, dq_s, dk_s, dv_s = rest[12:]
    heads, rows, hd = q_ref.shape
    blocks = rows // BLK
    per = chunk // BLK
    own = h_ref[0]
    for c in range(4):
        r0 = pl.multiple_of((own ^ c) * chunk, chunk)
        g = g_refs[c][...]
        o = o_refs[c][...]
        for h in range(heads):
            gh = g[:, h * hd : (h + 1) * hd]
            g_s[h, pl.ds(r0, chunk), :] = gh
            both = gh.astype(F32) * o[:, h * hd : (h + 1) * hd].astype(F32)
            d_s[h : h + 1, pl.ds(r0, chunk)] = jnp.sum(both.T, axis=0, keepdims=True)
        level = l_refs[c][...]
        l_s[:, pl.ds(r0, chunk)] = level
        c_s[:, pl.ds(r0, chunk)] = jnp.exp(-level)
    for h in range(heads):
        q_s[h] = q_ref[h] * jnp.asarray(scale, BF)
    dq_s[...] = jnp.zeros_like(dq_s)

    def out_row(block):
        return pl.multiple_of(((own ^ (block // per)) * per + block % per) * BLK, BLK)

    def outer(jb, carry):
        j0 = pl.multiple_of(jb * BLK, BLK)
        dk_s[...] = jnp.zeros_like(dk_s)
        dv_s[...] = jnp.zeros_like(dv_s)
        for h in range(heads):
            kt_s[h] = k_ref[h, pl.ds(j0, BLK), :].T
        _, stop = row_segment(len_ref, j0 + BLK - 1)
        j = j0 + lax.broadcasted_iota(jnp.int32, (BLK, BLK), 0)

        def inner(ib, carry):
            i0 = pl.multiple_of(ib * BLK, BLK)
            start, i = lane_starts(len_ref, i0, BLK)
            mask = (j >= start) & (j <= i)
            at = pl.ds(i0, BLK)
            qh = [q_s[h, at, :] for h in range(heads)]
            gh = [g_s[h, at, :] for h in range(heads)]
            scores = [dot_nt(k_ref[h, pl.ds(j0, BLK), :], qh[h]) for h in range(heads)]
            gws = [dot_nt(v_ref[h, pl.ds(j0, BLK), :], gh[h]) for h in range(heads)]
            ws, gss = [], []
            for h in range(heads):
                s, gw = scores[h], gws[h]
                level = l_s[h : h + 1, at]
                offset = c_s[h : h + 1, at]
                d = d_s[h : h + 1, at]
                p = jnp.exp(jnp.where(mask, jnp.abs(s), NEG) - level)
                u = p - jnp.where(mask, offset, 0.0)
                sign = jnp.clip(s * 1e38, -1.0, 1.0)
                w = (sign * u).astype(BF)
                gs = (p * (gw - sign * d)).astype(BF)
                ws.append(w)
                gss.append(gs)
            dvs = [dot_nn(ws[h], gh[h]) for h in range(heads)]
            dks = [dot_nn(gss[h], qh[h]) for h in range(heads)]
            dqs = [dot_nn(kt_s[h], gss[h]) for h in range(heads)]
            for h in range(heads):
                dv_s[h] += dvs[h]
                dk_s[h] += dks[h]
                dq_s[h, :, at] += dqs[h]
            return carry

        lax.fori_loop(jb, (stop - 1) // BLK + 1, inner, 0)
        for h in range(heads):
            at = pl.ds(out_row(jb), BLK)
            gp_ref[at, (3 * h + 1) * hd : (3 * h + 2) * hd] = dk_s[h].astype(BF)
            gp_ref[at, (3 * h + 2) * hd : (3 * h + 3) * hd] = dv_s[h].astype(BF)
        return carry

    lax.fori_loop(0, blocks, outer, 0)

    def finish(ib, carry):
        i0 = pl.multiple_of(ib * BLK, BLK)
        for h in range(heads):
            dq = (dq_s[h, :, pl.ds(i0, BLK)] * scale).T.astype(BF)
            gp_ref[pl.ds(out_row(ib), BLK), 3 * h * hd : (3 * h + 1) * hd] = dq
        return carry

    lax.fori_loop(0, blocks, finish, 0)


def attend_back_call(lengths, hid, q, k, v, grads, outs, levels, chunk):
    heads, rows, hd = q.shape
    vm = pl.BlockSpec(memory_space=pltpu.VMEM)
    sm = pl.BlockSpec(memory_space=pltpu.SMEM)
    return pl.pallas_call(
        functools.partial(attend_back_kernel, chunk, 1.0 / math.sqrt(hd)),
        out_shape=jax.ShapeDtypeStruct((rows, heads * 3 * hd), BF),
        in_specs=[sm, sm] + [vm] * 15,
        out_specs=vm,
        scratch_shapes=[
            pltpu.VMEM((heads, rows, hd), BF),
            pltpu.VMEM((heads, rows, hd), BF),
            pltpu.VMEM((heads, hd, BLK), BF),
            pltpu.VMEM((8, rows), F32),
            pltpu.VMEM((8, rows), F32),
            pltpu.VMEM((8, rows), F32),
            pltpu.VMEM((heads, hd, rows), F32),
            pltpu.VMEM((heads, BLK, hd), F32),
            pltpu.VMEM((heads, BLK, hd), F32),
        ],
        cost_estimate=cost(heads * rows * rows * hd * 20, 30 * rows * heads * hd, heads * rows * rows // 2),
        name="attend_back",
    )(lengths, hid, q, k, v, *grads, *outs, *levels)


def feed_kernel(steps, ha_ref, hb_ref, ga_ref, gb_ref, up_ref, v_ref, down_ref, *rest):
    act_ref, gup_ref, gna_ref, gnb_ref, outa_ref, outb_ref = rest[-6:]
    early = pl.program_id(0) < steps // 2
    h2 = jnp.where(early, ha_ref[...], hb_ref[...])
    grad = jnp.where(early, ga_ref[...], gb_ref[...])
    u = dot_nn(h2, up_ref[...]) + v_ref[5:6, :]
    square = u * u
    tanh = jnp.tanh(u * (GELU_C + (GELU_C * GELU_A) * square))
    half = 0.5 * (1.0 + tanh)
    act = (u * half).astype(BF)
    slope = half + (0.5 * u) * (1.0 - tanh * tanh) * (GELU_C + (3.0 * GELU_C * GELU_A) * square)
    gup = (dot_nt(grad, down_ref[...]) * slope).astype(BF)
    act_ref[...] = act
    gup_ref[...] = gup
    gn = dot_nt(gup, up_ref[...]).astype(BF)
    out = dot_nn(act, down_ref[...]).astype(BF)

    @pl.when(early)
    def _():
        gna_ref[...] = gn
        outa_ref[...] = out

    @pl.when(jnp.logical_not(early))
    def _():
        gnb_ref[...] = gn
        outb_ref[...] = out


def feed_call(ha, hb, ga, gb, up, vectors, down, first, group_rows, before):
    rows, width = ha.shape
    hidden = up.shape[1]
    per = rows // BLK
    steps = 2 * per
    whole = lambda t: (0, 0)
    early = pl.BlockSpec((BLK, width), lambda t: (jnp.minimum(t, per - 1), 0))
    late = pl.BlockSpec((BLK, width), lambda t: (jnp.maximum(t - per, 0), 0))
    return pl.pallas_call(
        functools.partial(feed_kernel, steps),
        out_shape=(
            jax.ShapeDtypeStruct((group_rows, hidden), BF),
            jax.ShapeDtypeStruct((group_rows, hidden), BF),
        )
        + (jax.ShapeDtypeStruct((rows, width), BF),) * 4,
        grid=(steps,),
        in_specs=[
            early,
            late,
            early,
            late,
            pl.BlockSpec(up.shape, whole),
            pl.BlockSpec(vectors.shape, whole),
            pl.BlockSpec(down.shape, whole),
        ]
        + [pl.BlockSpec(memory_space=pl.ANY)] * len(before),
        out_specs=[
            pl.BlockSpec((BLK, hidden), lambda t: (first * per + t, 0)),
            pl.BlockSpec((BLK, hidden), lambda t: (first * per + t, 0)),
            early,
            late,
            early,
            late,
        ],
        input_output_aliases={7 + i: i for i in range(len(before))},
        cost_estimate=cost(16 * rows * width * hidden, 16 * rows * width, 2 * rows * hidden),
        name="feed",
    )(ha, hb, ga, gb, up, vectors, down, *before)


def spots(b_ref, pieces):
    return [b_ref[0] ^ (2 * (spot % 4) + spot // 4) for spot in range(pieces)]


def split_out(b_ref, acc, keep_ref, send_ref):
    piece = acc.shape[0] // 8
    for spot, block in enumerate(spots(b_ref, 8)):
        out = keep_ref if spot < 4 else send_ref
        value = acc[pl.ds(pl.multiple_of(block * piece, 8), piece), :]
        out[(spot % 4) * piece : (spot % 4 + 1) * piece, :] = value.astype(BF)


def weigh_kernel(tiles, b_ref, h0, h1, h2, h3, act_ref, up_ref, g0, g1, g2, g3, keep_ref, send_ref, bias_ref, acc):
    t = pl.program_id(0)
    tile = acc.shape[0] // (2 * tiles)
    chunk = h0.shape[0]
    at = pl.ds(pl.multiple_of(t * tile, tile), tile)

    @pl.when(t == 0)
    def _():
        bias_ref[...] = jnp.sum(up_ref[...].astype(F32), axis=0, keepdims=True)

    @pl.when(t < tiles)
    def _():
        total = dot_tn(h0[...], up_ref[:chunk, :])
        for k, h in enumerate((h1, h2, h3)):
            total = total + dot_tn(h[...], up_ref[(k + 1) * chunk : (k + 2) * chunk, :])
        acc[at, :] = total

    @pl.when(t >= tiles)
    def _():
        total = dot_tn(act_ref[:chunk, :], g0[...])
        for k, g in enumerate((g1, g2, g3)):
            total = total + dot_tn(act_ref[(k + 1) * chunk : (k + 2) * chunk, :], g[...])
        acc[at, :] = total

    @pl.when(t == 2 * tiles - 1)
    def _():
        split_out(b_ref, acc, keep_ref, send_ref)


def weigh_call(bid, hs, act, up, grads):
    chunk, width = hs[0].shape
    rows, hidden = act.shape
    tile = 256
    tiles = width // tile
    whole = lambda t, b: (0, 0)
    total = width + hidden
    half = jax.ShapeDtypeStruct((total // 2, width), BF)
    return pl.pallas_call(
        functools.partial(weigh_kernel, tiles),
        out_shape=(half, half, jax.ShapeDtypeStruct((1, hidden), F32)),
        grid_spec=pltpu.PrefetchScalarGridSpec(
            num_scalar_prefetch=1,
            grid=(2 * tiles,),
            in_specs=[pl.BlockSpec((chunk, tile), lambda t, b: (0, jnp.minimum(t, tiles - 1)))] * 4
            + [
                pl.BlockSpec((rows, tile), lambda t, b: (0, jnp.maximum(t - tiles, 0))),
                pl.BlockSpec((rows, hidden), whole),
            ]
            + [pl.BlockSpec((chunk, width), whole)] * 4,
            out_specs=[
                pl.BlockSpec(half.shape, whole),
                pl.BlockSpec(half.shape, whole),
                pl.BlockSpec((1, hidden), whole),
            ],
            scratch_shapes=[pltpu.VMEM((total, width), F32)],
        ),
        cost_estimate=cost(4 * rows * width * hidden, 12 * rows * width),
        name="weigh",
    )(bid, *hs, act, up, *grads)


def mix_kernel(m0, m1, m2, m3, p0, p1, p2, p3, x_ref, v_ref, resid_ref, h_ref):
    total = x_ref[...].astype(F32) + v_ref[2:3, :]
    for m, p in ((m0, p0), (m1, p1), (m2, p2), (m3, p3)):
        total = total + dot_nn(m[...], p[...])
    resid_ref[...] = total
    hat, _ = normalize(total)
    h_ref[...] = (hat * v_ref[3:4, :] + v_ref[4:5, :]).astype(BF)


def mix_call(parts, projs, x, vectors):
    rows, width = x.shape
    per = rows // BLK
    inner = parts[0].shape[1]
    low = pl.BlockSpec((BLK, inner), lambda t: (t, 0))
    whole = lambda t: (0, 0)
    return pl.pallas_call(
        mix_kernel,
        out_shape=(jax.ShapeDtypeStruct((rows, width), F32), jax.ShapeDtypeStruct((rows, width), BF)),
        grid=(per,),
        in_specs=[low] * 4
        + [pl.BlockSpec(projs[0].shape, whole)] * 4
        + [pl.BlockSpec((BLK, width), lambda t: (t, 0)), pl.BlockSpec(vectors.shape, whole)],
        out_specs=[pl.BlockSpec((BLK, width), lambda t: (t, 0))] * 2,
        cost_estimate=cost(8 * rows * width * inner, 12 * rows * width),
        name="mix",
    )(*parts, *projs, x, vectors)


def turn_kernel(n_ref, s_ref, f_ref, resid_ref, cot_ref, v_ref, p0, p1, p2, p3, gr_ref, ga_ref, g0, g1, g2, g3, sum_ref):
    grad = n_ref[...].astype(F32) + s_ref[...].astype(F32) + f_ref[...].astype(F32)
    hat, rstd = normalize(resid_ref[...])
    cot = cot_ref[...].astype(F32)
    e = grad * v_ref[3:4, :]
    back = e - jnp.mean(e, axis=-1, keepdims=True) - hat * jnp.mean(e * hat, axis=-1, keepdims=True)
    grad_resid = cot + rstd * back
    gr_ref[...] = grad_resid
    att = grad_resid.astype(BF)
    ga_ref[...] = att
    for g, p in ((g0, p0), (g1, p1), (g2, p2), (g3, p3)):
        g[...] = dot_nt(att, p[...]).astype(BF)

    @pl.when(pl.program_id(0) == 0)
    def _():
        sum_ref[...] = jnp.zeros_like(sum_ref)

    for k, v in enumerate((grad_resid, grad * hat, grad, cot)):
        sum_ref[k + 4 : k + 5, :] += jnp.sum(v, axis=0, keepdims=True)


def turn_call(near, swapped, far, resid, cot, vectors, projs):
    rows, width = resid.shape
    per = rows // BLK
    inner = projs[0].shape[0]
    low = pl.BlockSpec((BLK, width), lambda t: (t, 0))
    whole = lambda t: (0, 0)
    return pl.pallas_call(
        turn_kernel,
        out_shape=(
            jax.ShapeDtypeStruct((rows, width), F32),
            jax.ShapeDtypeStruct((rows, width), BF),
        )
        + (jax.ShapeDtypeStruct((rows, inner), BF),) * 4
        + (jax.ShapeDtypeStruct((8, width), F32),),
        grid=(per,),
        in_specs=[low] * 5
        + [pl.BlockSpec(vectors.shape, whole)]
        + [pl.BlockSpec(projs[0].shape, whole)] * 4,
        out_specs=[low, low]
        + [pl.BlockSpec((BLK, inner), lambda t: (t, 0))] * 4
        + [pl.BlockSpec((8, width), whole)],
        cost_estimate=cost(rows, width),
        name="turn",
    )(near, swapped, far, resid, cot, vectors, *projs)


def tally_kernel(steps, b_ref, gp_ref, hat_ref, w_ref, v_ref, pw_ref, up_ref, s_ref, keep_ref, send_ref, acc, col):
    t = pl.program_id(0)
    gp = gp_ref[...]
    cols = gp.shape[1]
    half = acc.shape[0] // 2

    @pl.when(t == 0)
    def _():
        acc[:cols, :] = jnp.zeros((cols, acc.shape[1]), F32)
        acc[cols:, :] = pw_ref[...]
        col[...] = jnp.zeros_like(col)

    acc[:cols, :] += dot_tn(gp, hat_ref[...])
    col[...] += dot_tn(gp, jnp.ones((gp.shape[0], 128), BF))

    @pl.when(t == steps - 1)
    def _():
        total = col[:, 0:1]
        moment = acc[:cols, :]
        w = w_ref[...].astype(F32)
        small = s_ref[...]
        row = lax.broadcasted_iota(jnp.int32, small.shape, 0)
        small = jnp.where(row == 0, jnp.sum(w * moment, axis=0, keepdims=True), small)
        small = jnp.where(row == 1, jnp.sum(w * total, axis=0, keepdims=True), small)
        bias = jnp.concatenate((col[...].T[0:1, :], jnp.zeros((1, small.shape[1] - cols), F32)), axis=1)
        small = jnp.where(row == 2, bias, small)
        small = jnp.where(row == 3, up_ref[...], small).astype(BF)
        acc[:cols, :] = moment * v_ref[0:1, :] + total * v_ref[1:2, :]
        split_out(b_ref, acc, keep_ref, send_ref)
        keep_ref[half:, :] = small
        send_ref[half:, :] = small


def tally_call(bid, gp, hat, w, vectors, proj_grad, up_grad, sums):
    rows, width = hat.shape
    cols = gp.shape[1]
    total = cols + proj_grad.shape[0]
    block = 2 * BLK
    steps = rows // block
    whole = lambda t, b: (0, 0)
    half = jax.ShapeDtypeStruct((total // 2 + sums.shape[0], width), BF)
    return pl.pallas_call(
        functools.partial(tally_kernel, steps),
        out_shape=(half, half),
        grid_spec=pltpu.PrefetchScalarGridSpec(
            num_scalar_prefetch=1,
            grid=(steps,),
            in_specs=[
                pl.BlockSpec((block, cols), lambda t, b: (t, 0)),
                pl.BlockSpec((block, width), lambda t, b: (t, 0)),
            ]
            + [pl.BlockSpec(v.shape, whole) for v in (w, vectors, proj_grad, up_grad, sums)],
            out_specs=[pl.BlockSpec(half.shape, whole)] * 2,
            scratch_shapes=[pltpu.VMEM((total, width), F32), pltpu.VMEM((cols, 128), F32)],
        ),
        cost_estimate=cost(cols, width),
        name="tally",
    )(bid, gp, hat, w, vectors, proj_grad, up_grad, sums)


def spread_kernel(gp_ref, w_ref, *outs):
    e = dot_nn(gp_ref[...], w_ref[...]).astype(BF)
    for k, out in enumerate(outs):

        @pl.when(pl.program_id(0) == k)
        def _(out=out):
            out[...] = e


def spread_call(gp, w, chunk):
    cols, width = w.shape
    whole = lambda t: (0, 0)
    return pl.pallas_call(
        spread_kernel,
        out_shape=(jax.ShapeDtypeStruct((chunk, width), BF),) * 4,
        grid=(4,),
        in_specs=[pl.BlockSpec((chunk, cols), lambda t: (t, 0)), pl.BlockSpec(w.shape, whole)],
        out_specs=[pl.BlockSpec((chunk, width), whole)] * 4,
        cost_estimate=cost(cols, width),
        name="spread",
    )(gp, w)


def unpack_kernel(counts, places, b_ref, *rest):
    acc = rest[-1]
    piece = acc.shape[0] // 8
    for (part, at), block in zip(places, spots(b_ref, 8), strict=True):
        value = rest[part][at : at + piece, :].astype(F32)
        acc[pl.ds(pl.multiple_of(block * piece, 8), piece), :] = value
    start = 0
    for out, count in zip(rest[-1 - len(counts) : -1], counts, strict=True):
        out[...] = acc[start : start + count, :]
        start += count


def unpack_call(bid, parts, places, counts):
    total = sum(counts)
    width = parts[0].shape[1]
    vm = pl.BlockSpec(memory_space=pltpu.VMEM)
    return pl.pallas_call(
        functools.partial(unpack_kernel, counts, places),
        out_shape=tuple(jax.ShapeDtypeStruct((n, width), F32) for n in counts),
        in_specs=[pl.BlockSpec(memory_space=pltpu.SMEM)] + [vm] * len(parts),
        out_specs=[vm] * len(counts),
        scratch_shapes=[pltpu.VMEM((total, width), F32)],
        cost_estimate=cost(total, width),
        name="unpack",
    )(bid, *parts)


def tie(x, *needed):
    return lax.optimization_barrier((x,) + needed)[0]


def across(pieces):
    return [swap(piece, "batch", 2 * d) for d, piece in enumerate(pieces, 1)]


def sum_rest(x):
    for level in range(3, lax.axis_size("batch").bit_length() - 1):
        x = (x.astype(F32) + swap(x, "batch", 1 << level).astype(F32)).astype(x.dtype)
    return x


def fold(kept, got):
    piece = kept.shape[0] // 4
    total = kept[:piece].astype(F32)
    for g in got:
        total = total + g[:piece].astype(F32)
    return sum_rest(total.astype(BF))


def quarters(x):
    piece = x.shape[0] // 4
    return [x[d * piece : (d + 1) * piece] for d in range(1, 4)]


def sum_group(x):
    x = x + swap(x, "head", 1)
    return x + swap(x, "head", 2)


def per_device(
    inputs,
    lengths,
    cotangent,
    gain_attn,
    shift_attn,
    weight_qkv,
    bias_qkv,
    weight_proj,
    bias_proj,
    gain_mlp,
    shift_mlp,
    weight_up,
    bias_up,
    weight_down,
    bias_down,
):
    chunk, width = inputs.shape
    group_rows = chunk * lax.axis_size("head")
    heads, triple = weight_qkv.shape[1:]
    cols = heads * triple
    inner = cols // 3
    own = lax.axis_index("head")
    hid = own.astype(jnp.int32).reshape(1)
    bid = (lax.axis_index("batch") % 8).astype(jnp.int32).reshape(1)
    lens = lengths[0]
    live_rows = jnp.sum(lens[:-1])
    places = own * chunk + jnp.arange(chunk, dtype=jnp.int32)
    live = (places < live_rows)[:, None]
    qkv_t = weight_qkv.transpose(1, 2, 0).reshape(cols, width)
    proj = weight_proj.reshape(inner, width)
    zero = jnp.zeros((width,), F32)
    vectors = jnp.stack(
        (gain_attn, shift_attn, bias_proj, gain_mlp, shift_mlp, bias_up, bias_down, zero)
    )

    x_far = swap(inputs, "head", 2)
    x_near = swap(inputs, "head", 1)
    begun = qkv_call(hid, inputs, x_near, vectors, qkv_t, bias_qkv, 0, group_rows, ())
    x_far = tie(x_far, begun[0])
    x_last = swap(x_far, "head", 1)
    queries, keys, values, values_t, hats = qkv_call(
        hid, x_far, x_last, vectors, qkv_t, bias_qkv, 2, group_rows, begun
    )
    grad_own = jnp.where(live, cotangent, jnp.zeros_like(cotangent))
    proj_far = swap(tie(proj, x_far), "head", 2)
    grad_far = swap(tie(grad_own, x_last), "head", 2)

    out_far, out_last, level_far, level_last = attend_call(
        lens, hid, queries, keys, values_t, 2, chunk
    )
    from_last = swap(out_last, "head", 2)
    from_far = swap(out_far, "head", 2)
    out_own, out_mate, level_own, level_mate = attend_call(
        lens, hid, tie(queries, out_far), keys, values_t, 0, chunk
    )
    grads = (grad_own, swap(tie(grad_own, out_far), "head", 1), grad_far, swap(grad_far, "head", 1))
    from_last = swap(tie(from_last, out_own, from_far), "head", 1)
    parts = (out_own, swap(out_mate, "head", 1), from_far, from_last)
    proj_last = swap(tie(proj_far, out_own), "head", 1)
    projs = (proj, swap(tie(proj, out_far), "head", 1), proj_far, proj_last)
    resid, h_own = mix_call(parts, projs, tie(inputs, grad_far), vectors)
    h_far = swap(h_own, "head", 2)
    h_near = swap(h_own, "head", 1)

    near = feed_call(h_own, h_near, grads[0], grads[1], weight_up, vectors, weight_down, 0, group_rows, ())
    h_far = tie(h_far, near[0])
    h_last = swap(h_far, "head", 1)
    act, grad_up, norm_far, norm_last, down_far, down_last = feed_call(
        h_far, h_last, grads[2], grads[3], weight_up, vectors, weight_down, 2, group_rows, near[:2]
    )
    far_sum = (norm_far.astype(F32) + swap(norm_last, "head", 1).astype(F32)).astype(BF)
    grad_far_sum = swap(far_sum, "head", 2)
    near_swapped = swap(near[3], "head", 1)
    down_swapped = swap(tie(down_last, far_sum), "head", 1)
    near_down = swap(tie(near[5], far_sum), "head", 1)

    keep_feed, send_feed, grad_bup = weigh_call(
        bid, (h_own, h_near, h_far, h_last), tie(act, far_sum), grad_up, grads
    )
    other_feed = swap(send_feed, "batch", 1)
    grad_resid, grad_att, grad_near, grad_mate, grad_cross, grad_last, sums = turn_call(
        near[2],
        near_swapped,
        tie(grad_far_sum, grad_bup, down_swapped, near_down),
        resid,
        grad_own,
        vectors,
        projs,
    )
    got_last = swap(grad_last, "head", 2)
    got = swap(grad_cross, "head", 2)
    grad_mate = swap(grad_mate, "head", 1)
    grad_att = tie(grad_att, grad_mate)
    grad_proj = [dot_tn(p, grad_att) for p in parts]
    near_sent, far_sent = grad_proj[1].astype(BF), grad_proj[3].astype(BF)
    down_far = tie(down_far, grad_att)
    down_sum = (down_far.astype(F32) + down_swapped.astype(F32)).astype(BF)
    got_last = tie(got_last, near_sent, far_sent, down_sum)
    merged_grads = (grad_near, grad_mate, got, swap(got_last, "head", 1))
    grad_near_proj = grad_proj[0] + swap(near_sent, "head", 1).astype(F32)
    far_proj = (grad_proj[2] + swap(far_sent, "head", 1).astype(F32)).astype(BF)
    far_proj = swap(far_proj, "head", 2)

    kept_feed = (keep_feed.astype(F32) + tie(other_feed, got).astype(F32)).astype(BF)
    got_feed = across(quarters(kept_feed))
    down_other = swap(tie(down_sum, kept_feed), "head", 2)

    grad_packed = attend_back_call(
        lens,
        hid,
        tie(queries, kept_feed, grad_near_proj),
        keys,
        values,
        merged_grads,
        (out_own, out_mate, out_far, out_last),
        (level_own, level_mate, level_far, level_last),
        chunk,
    )
    got_feed = [tie(g, grad_packed) for g in got_feed]
    grad_wproj = grad_near_proj + tie(far_proj, grad_packed).astype(F32)
    total_feed = fold(kept_feed, got_feed)
    gathered_feed = across([total_feed] * 3)
    keep, send = tally_call(
        bid, tie(grad_packed, total_feed, down_other), hats, qkv_t, vectors, grad_wproj, grad_bup, sums
    )
    other = swap(send, "batch", 1)
    spread = spread_call(tie(grad_packed, keep), qkv_t, chunk)
    gathered_feed, spread = lax.optimization_barrier((gathered_feed, spread))
    e_own, e_near, e_far, e_last = spread

    feed_first = jnp.concatenate((total_feed, gathered_feed[0]), axis=0)
    feed_second = jnp.concatenate(gathered_feed[1:], axis=0)
    feed_got = swap(feed_first, "batch", 1)
    summed = (keep.astype(F32) + tie(other, feed_first, feed_second).astype(F32)).astype(BF)
    kept, small = summed[:-8], summed[-8:]
    pieces = [jnp.concatenate((q, small), axis=0) for q in quarters(kept)]
    e_swapped = swap(tie(e_last, *pieces), "head", 1)
    e_sum = (e_far.astype(F32) + e_swapped.astype(F32)).astype(BF)
    output = resid + near[4].astype(F32) + near_down.astype(F32) + tie(down_other, e_sum).astype(F32)
    output = (output + bias_down).astype(BF)
    got_attn = [tie(g, feed_got, output) for g in across(pieces)]

    tiny = [small.astype(F32)] + [g[-8:].astype(F32) for g in got_attn]
    small = sum_rest((tiny[0] + tiny[1]) + (tiny[2] + tiny[3]))
    total_attn = fold(kept, got_attn)
    gathered_attn = across([total_attn] * 3)
    second_got = swap(tie(feed_second, total_attn), "batch", 1)
    e_other = swap(tie(e_sum, total_attn), "head", 2)
    half = jnp.concatenate([total_attn] + [tie(g, second_got) for g in gathered_attn], axis=0)
    e_mate = swap(tie(e_near, half), "head", 1)
    last = swap(half, "batch", 1)
    biases = small[2:4]
    small = sum_group(tie(small, half))
    e_own = e_own.astype(F32) + e_mate.astype(F32) + tie(e_other, half).astype(F32)

    x_hat, x_rstd = normalize(tie(inputs, half).astype(F32))
    e_own = e_own * gain_attn
    grad_inputs = (
        grad_resid
        + x_rstd
        * (
            e_own
            - jnp.mean(e_own, axis=-1, keepdims=True)
            - x_hat * jnp.mean(e_own * x_hat, axis=-1, keepdims=True)
        )
    ).astype(BF)
    pair = tuple(k * total_feed.shape[0] for k in range(2))
    places = tuple((k, at) for k in range(4) for at in pair)
    parts = (feed_first, feed_second, feed_got, tie(second_got, half))
    sum_wup, sum_wdown = unpack_call(bid, parts, places, (width, width))
    places = tuple((k, at * total_attn.shape[0]) for k in range(2) for at in range(4))
    parts = (half, tie(last, sum_wup, grad_inputs))
    sum_wqkv, sum_wproj = unpack_call(bid, parts, places, (cols, inner))
    return (
        output,
        grad_inputs,
        small[0],
        small[1],
        sum_wqkv.reshape(heads, triple, width).transpose(2, 0, 1),
        biases[0, :cols].reshape(heads, triple),
        sum_wproj.reshape(heads, inner // heads, width),
        small[4],
        small[5],
        small[6],
        sum_wup,
        biases[1],
        sum_wdown,
        small[7],
    )


def solution(mesh):
    rows = P(("batch", "head"), None)
    in_specs = (
        rows,
        P("batch", None),
        rows,
        P(),
        P(),
        P(None, "head", None),
        P("head", None),
        P("head", None, None),
        P(),
        P(),
        P(),
        P(None, "head"),
        P("head"),
        P("head", None),
        P(),
    )
    out_specs = (
        rows,
        rows,
        P(),
        P(),
        P(None, "head", None),
        P("head", None),
        P("head", None, None),
        P(),
        P(),
        P(),
        P(None, "head"),
        P("head"),
        P("head", None),
        P(),
    )
    return jax.shard_map(
        per_device, mesh=mesh, in_specs=in_specs, out_specs=out_specs, check_vma=False
    )
```

```python
import functools
import math

import jax
import jax.numpy as jnp
from jax import lax
from jax.experimental import pallas as pl
from jax.experimental.pallas import tpu as pltpu
from jax.sharding import PartitionSpec as P

F32 = jnp.float32
BF = jnp.bfloat16
BLK = 256
NEG = -1e30
EPS = 1e-05
GELU_C = math.sqrt(2.0 / math.pi)
GELU_A = 0.044715


def dot_nn(a, b):
    return lax.dot_general(a, b, (((1,), (0,)), ((), ())), preferred_element_type=F32)


def dot_nt(a, b):
    return lax.dot_general(a, b, (((1,), (1,)), ((), ())), preferred_element_type=F32)


def dot_tn(a, b):
    return lax.dot_general(a, b, (((0,), (0,)), ((), ())), preferred_element_type=F32)


def cost(flops, nbytes, trans=0):
    return pl.CostEstimate(flops=int(flops), bytes_accessed=int(nbytes), transcendentals=int(trans))


def swap(x, axis, bits):
    size = lax.axis_size(axis)
    return lax.ppermute(x, axis, [(i, i ^ bits) for i in range(size)])


def normalize(v):
    center = v - jnp.mean(v, axis=-1, keepdims=True)
    rstd = lax.rsqrt(jnp.mean(center * center, axis=-1, keepdims=True) + EPS)
    return center * rstd, rstd


def qkv_kernel(heads, hd, steps, h_ref, a_ref, b_ref, v_ref, w_ref, bias_ref, *rest):
    q_out, k_out, v_out, vt_out, hat_out = rest[-5:]
    t = pl.program_id(0)
    x = jnp.where(t < steps // 2, a_ref[...], b_ref[...]).astype(F32)
    xhat, _ = normalize(x)
    hat_out[...] = xhat.astype(BF)
    h1 = (xhat * v_ref[0:1, :] + v_ref[1:2, :]).astype(BF)
    bias = jnp.concatenate([bias_ref[h : h + 1, :] for h in range(heads)], axis=1)
    packed = (dot_nt(h1, w_ref[...]) + bias).astype(BF)
    for h in range(heads):
        o = 3 * hd * h
        q_out[h] = packed[:, o : o + hd]
        k_out[h] = packed[:, o + hd : o + 2 * hd]
        v = packed[:, o + 2 * hd : o + 3 * hd]
        v_out[h] = v
        vt_out[h] = v.T


def qkv_call(hid, a, b, vectors, w, bias, first, group_rows, before):
    rows, width = a.shape
    heads, triple = bias.shape
    hd = triple // 3
    per = rows // BLK
    steps = 2 * per
    place = lambda t, h: (h[0] ^ (first + t // per)) * per + t % per
    whole = lambda t, h: (0, 0)
    out_shape = tuple(
        jax.ShapeDtypeStruct(s, BF)
        for s in ((heads, group_rows, hd),) * 3 + ((heads, hd, group_rows), (group_rows, width))
    )
    in_specs = [
        pl.BlockSpec((BLK, width), lambda t, h: (jnp.minimum(t, per - 1), 0)),
        pl.BlockSpec((BLK, width), lambda t, h: (jnp.maximum(t - per, 0), 0)),
        pl.BlockSpec(vectors.shape, whole),
        pl.BlockSpec(w.shape, whole),
        pl.BlockSpec(bias.shape, whole),
    ] + [pl.BlockSpec(memory_space=pl.ANY)] * len(before)
    return pl.pallas_call(
        functools.partial(qkv_kernel, heads, hd, steps),
        out_shape=out_shape,
        grid_spec=pltpu.PrefetchScalarGridSpec(
            num_scalar_prefetch=1,
            grid=(steps,),
            in_specs=in_specs,
            out_specs=[pl.BlockSpec((heads, BLK, hd), lambda t, h: (0, place(t, h), 0))] * 3
            + [
                pl.BlockSpec((heads, hd, BLK), lambda t, h: (0, 0, place(t, h))),
                pl.BlockSpec((BLK, width), lambda t, h: (first * per + t, 0)),
            ],
        ),
        input_output_aliases={6 + i: i for i in range(len(before))},
        cost_estimate=cost(4 * rows * width * w.shape[0], 12 * rows * width),
        name="qkv",
    )(hid, a, b, vectors, w, bias, *before)


def row_segment(len_ref, row):
    low = row
    high = row + 1
    start = jnp.int32(0)
    for k in range(len_ref.shape[0] - 1):
        stop = start + len_ref[k]
        inside = (row >= start) & (row < stop)
        low = jnp.where(inside, start, low)
        high = jnp.where(inside, stop, high)
        start = stop
    return low, high


def lane_starts(len_ref, row, width):
    i = row + lax.broadcasted_iota(jnp.int32, (1, width), 1)
    start = jnp.zeros((1, width), jnp.int32)
    stop = jnp.int32(0)
    for k in range(len_ref.shape[0] - 1):
        stop = stop + len_ref[k]
        start = jnp.where(i >= stop, stop, start)
    return jnp.where(i >= stop, i, start), i


def attend_kernel(heads, first, per, scale, len_ref, h_ref, q_ref, k_ref, vt_ref, oa_ref, ob_ref, la_ref, lb_ref, s_s, m_s, z_s, acc_s):
    t = pl.program_id(0)
    row = ((h_ref[0] ^ (first + t // per)) * per + t % per) * BLK
    start, i = lane_starts(len_ref, row, BLK)
    low, _ = row_segment(len_ref, row)
    m_s[...] = jnp.zeros_like(m_s)
    z_s[...] = jnp.zeros_like(z_s)
    acc_s[...] = jnp.zeros_like(acc_s)
    qs = [q_ref[h] * jnp.asarray(scale, BF) for h in range(heads)]
    blocks = (low // BLK, row // BLK + 1)

    def measure(jb, carry):
        j0 = pl.multiple_of(jb * BLK, BLK)
        j = j0 + lax.broadcasted_iota(jnp.int32, (BLK, BLK), 0)
        mask = (j >= start) & (j <= i)
        scores = [dot_nt(k_ref[h, pl.ds(j0, BLK), :], qs[h]) for h in range(heads)]
        tops = [m_s[h : h + 1, :] for h in range(heads)]
        for h in range(heads):
            s = jnp.where(mask, scores[h], 0.0)
            s_s[h, pl.ds(j0, BLK), :] = s
            tops[h] = jnp.maximum(tops[h], jnp.max(jnp.abs(s), axis=0, keepdims=True))
        for h in range(heads):
            m_s[h : h + 1, :] = tops[h]
        return carry

    lax.fori_loop(*blocks, measure, 0)
    tops = [m_s[h : h + 1, :] for h in range(heads)]
    offsets = [jnp.exp(-top) for top in tops]

    def gather(jb, carry):
        j0 = pl.multiple_of(jb * BLK, BLK)
        sums, weights = [], []
        for h in range(heads):
            s = s_s[h, pl.ds(j0, BLK), :]
            u = jnp.exp(jnp.abs(s) - tops[h]) - offsets[h]
            sums.append(jnp.sum(u, axis=0, keepdims=True))
            weights.append(jnp.where(s < 0, -u, u).astype(BF))
        adds = [dot_nn(vt_ref[h, :, pl.ds(j0, BLK)], weights[h]) for h in range(heads)]
        for h in range(heads):
            z_s[h : h + 1, :] += sums[h]
            acc_s[h] += adds[h]
        return carry

    lax.fori_loop(*blocks, gather, 0)
    count = (i - start + 1).astype(F32)
    outs, levels = [], []
    for h in range(heads):
        z = z_s[h : h + 1, :] + count * offsets[h]
        outs.append((acc_s[h] / z).T)
        levels.append(tops[h] + jnp.log(z))
    out = jnp.concatenate(outs, axis=1).astype(BF)

    def store(o_ref, l_ref):
        o_ref[...] = out
        for h in range(heads):
            l_ref[h : h + 1, :] = levels[h]

    @pl.when(t < per)
    def _():
        store(oa_ref, la_ref)

    @pl.when(t >= per)
    def _():
        store(ob_ref, lb_ref)


def attend_call(lengths, hid, q, k, vt, first, chunk):
    heads, rows, hd = q.shape
    per = chunk // BLK
    steps = 2 * per
    place = lambda t, n, h: (0, (h[0] ^ (first + t // per)) * per + t % per, 0)
    whole = lambda t, n, h: (0, 0, 0)
    return pl.pallas_call(
        functools.partial(attend_kernel, heads, first, per, 1.0 / math.sqrt(hd)),
        out_shape=(jax.ShapeDtypeStruct((chunk, heads * hd), BF),) * 2
        + (jax.ShapeDtypeStruct((8, chunk), F32),) * 2,
        grid_spec=pltpu.PrefetchScalarGridSpec(
            num_scalar_prefetch=2,
            grid=(steps,),
            in_specs=[
                pl.BlockSpec((heads, BLK, hd), place),
                pl.BlockSpec((heads, rows, hd), whole),
                pl.BlockSpec((heads, hd, rows), whole),
            ],
            out_specs=[
                pl.BlockSpec((BLK, heads * hd), lambda t, n, h: (jnp.minimum(t, per - 1), 0)),
                pl.BlockSpec((BLK, heads * hd), lambda t, n, h: (jnp.maximum(t - per, 0), 0)),
                pl.BlockSpec((8, BLK), lambda t, n, h: (0, jnp.minimum(t, per - 1))),
                pl.BlockSpec((8, BLK), lambda t, n, h: (0, jnp.maximum(t - per, 0))),
            ],
            scratch_shapes=[
                pltpu.VMEM((heads, rows, BLK), F32),
                pltpu.VMEM((8, BLK), F32),
                pltpu.VMEM((8, BLK), F32),
                pltpu.VMEM((heads, hd, BLK), F32),
            ],
        ),
        cost_estimate=cost(rows, hd),
        name="attend",
    )(lengths, hid, q, k, vt)


def attend_back_kernel(chunk, scale, len_ref, h_ref, q_ref, k_ref, v_ref, *rest):
    g_refs, o_refs, l_refs = rest[0:4], rest[4:8], rest[8:12]
    gp_ref, q_s, g_s, kt_s, l_s, c_s, d_s, dq_s, dk_s, dv_s = rest[12:]
    heads, rows, hd = q_ref.shape
    blocks = rows // BLK
    per = chunk // BLK
    own = h_ref[0]
    for c in range(4):
        r0 = pl.multiple_of((own ^ c) * chunk, chunk)
        g = g_refs[c][...]
        o = o_refs[c][...]
        for h in range(heads):
            gh = g[:, h * hd : (h + 1) * hd]
            g_s[h, pl.ds(r0, chunk), :] = gh
            both = gh.astype(F32) * o[:, h * hd : (h + 1) * hd].astype(F32)
            d_s[h : h + 1, pl.ds(r0, chunk)] = jnp.sum(both.T, axis=0, keepdims=True)
        level = l_refs[c][...]
        l_s[:, pl.ds(r0, chunk)] = level
        c_s[:, pl.ds(r0, chunk)] = jnp.exp(-level)
    for h in range(heads):
        q_s[h] = q_ref[h] * jnp.asarray(scale, BF)
    dq_s[...] = jnp.zeros_like(dq_s)

    def out_row(block):
        return pl.multiple_of(((own ^ (block // per)) * per + block % per) * BLK, BLK)

    def outer(jb, carry):
        j0 = pl.multiple_of(jb * BLK, BLK)
        dk_s[...] = jnp.zeros_like(dk_s)
        dv_s[...] = jnp.zeros_like(dv_s)
        for h in range(heads):
            kt_s[h] = k_ref[h, pl.ds(j0, BLK), :].T
        _, stop = row_segment(len_ref, j0 + BLK - 1)
        j = j0 + lax.broadcasted_iota(jnp.int32, (BLK, BLK), 0)

        def inner(ib, carry):
            i0 = pl.multiple_of(ib * BLK, BLK)
            start, i = lane_starts(len_ref, i0, BLK)
            mask = (j >= start) & (j <= i)
            at = pl.ds(i0, BLK)
            qh = [q_s[h, at, :] for h in range(heads)]
            gh = [g_s[h, at, :] for h in range(heads)]
            scores = [dot_nt(k_ref[h, pl.ds(j0, BLK), :], qh[h]) for h in range(heads)]
            gws = [dot_nt(v_ref[h, pl.ds(j0, BLK), :], gh[h]) for h in range(heads)]
            ws, gss = [], []
            for h in range(heads):
                s, gw = scores[h], gws[h]
                level = l_s[h : h + 1, at]
                offset = c_s[h : h + 1, at]
                d = d_s[h : h + 1, at]
                p = jnp.exp(jnp.where(mask, jnp.abs(s), NEG) - level)
                u = p - jnp.where(mask, offset, 0.0)
                sign = jnp.clip(s * 1e38, -1.0, 1.0)
                w = (sign * u).astype(BF)
                gs = (p * (gw - sign * d)).astype(BF)
                ws.append(w)
                gss.append(gs)
            dvs = [dot_nn(ws[h], gh[h]) for h in range(heads)]
            dks = [dot_nn(gss[h], qh[h]) for h in range(heads)]
            dqs = [dot_nn(kt_s[h], gss[h]) for h in range(heads)]
            for h in range(heads):
                dv_s[h] += dvs[h]
                dk_s[h] += dks[h]
                dq_s[h, :, at] += dqs[h]
            return carry

        lax.fori_loop(jb, (stop - 1) // BLK + 1, inner, 0)
        for h in range(heads):
            at = pl.ds(out_row(jb), BLK)
            gp_ref[at, (3 * h + 1) * hd : (3 * h + 2) * hd] = dk_s[h].astype(BF)
            gp_ref[at, (3 * h + 2) * hd : (3 * h + 3) * hd] = dv_s[h].astype(BF)
        return carry

    lax.fori_loop(0, blocks, outer, 0)

    def finish(ib, carry):
        i0 = pl.multiple_of(ib * BLK, BLK)
        for h in range(heads):
            dq = (dq_s[h, :, pl.ds(i0, BLK)] * scale).T.astype(BF)
            gp_ref[pl.ds(out_row(ib), BLK), 3 * h * hd : (3 * h + 1) * hd] = dq
        return carry

    lax.fori_loop(0, blocks, finish, 0)


def attend_back_call(lengths, hid, q, k, v, grads, outs, levels, chunk):
    heads, rows, hd = q.shape
    vm = pl.BlockSpec(memory_space=pltpu.VMEM)
    sm = pl.BlockSpec(memory_space=pltpu.SMEM)
    return pl.pallas_call(
        functools.partial(attend_back_kernel, chunk, 1.0 / math.sqrt(hd)),
        out_shape=jax.ShapeDtypeStruct((rows, heads * 3 * hd), BF),
        in_specs=[sm, sm] + [vm] * 15,
        out_specs=vm,
        scratch_shapes=[
            pltpu.VMEM((heads, rows, hd), BF),
            pltpu.VMEM((heads, rows, hd), BF),
            pltpu.VMEM((heads, hd, BLK), BF),
            pltpu.VMEM((8, rows), F32),
            pltpu.VMEM((8, rows), F32),
            pltpu.VMEM((8, rows), F32),
            pltpu.VMEM((heads, hd, rows), F32),
            pltpu.VMEM((heads, BLK, hd), F32),
            pltpu.VMEM((heads, BLK, hd), F32),
        ],
        cost_estimate=cost(heads * rows * rows * hd * 20, 30 * rows * heads * hd, heads * rows * rows // 2),
        name="attend_back",
    )(lengths, hid, q, k, v, *grads, *outs, *levels)


def feed_kernel(steps, ha_ref, hb_ref, ga_ref, gb_ref, up_ref, v_ref, down_ref, *rest):
    act_ref, gup_ref, gna_ref, gnb_ref, outa_ref, outb_ref = rest[-6:]
    early = pl.program_id(0) < steps // 2
    h2 = jnp.where(early, ha_ref[...], hb_ref[...])
    grad = jnp.where(early, ga_ref[...], gb_ref[...])
    u = dot_nn(h2, up_ref[...]) + v_ref[5:6, :]
    square = u * u
    tanh = jnp.tanh(u * (GELU_C + (GELU_C * GELU_A) * square))
    half = 0.5 * (1.0 + tanh)
    act = (u * half).astype(BF)
    slope = half + (0.5 * u) * (1.0 - tanh * tanh) * (GELU_C + (3.0 * GELU_C * GELU_A) * square)
    gup = (dot_nt(grad, down_ref[...]) * slope).astype(BF)
    act_ref[...] = act
    gup_ref[...] = gup
    gn = dot_nt(gup, up_ref[...]).astype(BF)
    out = dot_nn(act, down_ref[...]).astype(BF)

    @pl.when(early)
    def _():
        gna_ref[...] = gn
        outa_ref[...] = out

    @pl.when(jnp.logical_not(early))
    def _():
        gnb_ref[...] = gn
        outb_ref[...] = out


def feed_call(ha, hb, ga, gb, up, vectors, down, first, group_rows, before):
    rows, width = ha.shape
    hidden = up.shape[1]
    per = rows // BLK
    steps = 2 * per
    whole = lambda t: (0, 0)
    early = pl.BlockSpec((BLK, width), lambda t: (jnp.minimum(t, per - 1), 0))
    late = pl.BlockSpec((BLK, width), lambda t: (jnp.maximum(t - per, 0), 0))
    return pl.pallas_call(
        functools.partial(feed_kernel, steps),
        out_shape=(
            jax.ShapeDtypeStruct((group_rows, hidden), BF),
            jax.ShapeDtypeStruct((group_rows, hidden), BF),
        )
        + (jax.ShapeDtypeStruct((rows, width), BF),) * 4,
        grid=(steps,),
        in_specs=[
            early,
            late,
            early,
            late,
            pl.BlockSpec(up.shape, whole),
            pl.BlockSpec(vectors.shape, whole),
            pl.BlockSpec(down.shape, whole),
        ]
        + [pl.BlockSpec(memory_space=pl.ANY)] * len(before),
        out_specs=[
            pl.BlockSpec((BLK, hidden), lambda t: (first * per + t, 0)),
            pl.BlockSpec((BLK, hidden), lambda t: (first * per + t, 0)),
            early,
            late,
            early,
            late,
        ],
        input_output_aliases={7 + i: i for i in range(len(before))},
        cost_estimate=cost(16 * rows * width * hidden, 16 * rows * width, 2 * rows * hidden),
        name="feed",
    )(ha, hb, ga, gb, up, vectors, down, *before)


def spots(b_ref, pieces):
    return [b_ref[0] ^ (2 * (spot % 4) + spot // 4) for spot in range(pieces)]


def split_out(b_ref, acc, keep_ref, send_ref):
    piece = acc.shape[0] // 8
    for spot, block in enumerate(spots(b_ref, 8)):
        out = keep_ref if spot < 4 else send_ref
        value = acc[pl.ds(pl.multiple_of(block * piece, 8), piece), :]
        out[(spot % 4) * piece : (spot % 4 + 1) * piece, :] = value.astype(BF)


def weigh_kernel(tiles, b_ref, h0, h1, h2, h3, act_ref, up_ref, g0, g1, g2, g3, keep_ref, send_ref, bias_ref, acc):
    t = pl.program_id(0)
    tile = acc.shape[0] // (2 * tiles)
    chunk = h0.shape[0]
    at = pl.ds(pl.multiple_of(t * tile, tile), tile)

    @pl.when(t == 0)
    def _():
        bias_ref[...] = jnp.sum(up_ref[...].astype(F32), axis=0, keepdims=True)

    @pl.when(t < tiles)
    def _():
        total = dot_tn(h0[...], up_ref[:chunk, :])
        for k, h in enumerate((h1, h2, h3)):
            total = total + dot_tn(h[...], up_ref[(k + 1) * chunk : (k + 2) * chunk, :])
        acc[at, :] = total

    @pl.when(t >= tiles)
    def _():
        total = dot_tn(act_ref[:chunk, :], g0[...])
        for k, g in enumerate((g1, g2, g3)):
            total = total + dot_tn(act_ref[(k + 1) * chunk : (k + 2) * chunk, :], g[...])
        acc[at, :] = total

    @pl.when(t == 2 * tiles - 1)
    def _():
        split_out(b_ref, acc, keep_ref, send_ref)


def weigh_call(bid, hs, act, up, grads):
    chunk, width = hs[0].shape
    rows, hidden = act.shape
    tile = 256
    tiles = width // tile
    whole = lambda t, b: (0, 0)
    total = width + hidden
    half = jax.ShapeDtypeStruct((total // 2, width), BF)
    return pl.pallas_call(
        functools.partial(weigh_kernel, tiles),
        out_shape=(half, half, jax.ShapeDtypeStruct((1, hidden), F32)),
        grid_spec=pltpu.PrefetchScalarGridSpec(
            num_scalar_prefetch=1,
            grid=(2 * tiles,),
            in_specs=[pl.BlockSpec((chunk, tile), lambda t, b: (0, jnp.minimum(t, tiles - 1)))] * 4
            + [
                pl.BlockSpec((rows, tile), lambda t, b: (0, jnp.maximum(t - tiles, 0))),
                pl.BlockSpec((rows, hidden), whole),
            ]
            + [pl.BlockSpec((chunk, width), whole)] * 4,
            out_specs=[
                pl.BlockSpec(half.shape, whole),
                pl.BlockSpec(half.shape, whole),
                pl.BlockSpec((1, hidden), whole),
            ],
            scratch_shapes=[pltpu.VMEM((total, width), F32)],
        ),
        cost_estimate=cost(4 * rows * width * hidden, 12 * rows * width),
        name="weigh",
    )(bid, *hs, act, up, *grads)


def mix_kernel(m0, m1, m2, m3, p0, p1, p2, p3, x_ref, v_ref, resid_ref, h_ref):
    total = x_ref[...].astype(F32) + v_ref[2:3, :]
    for m, p in ((m0, p0), (m1, p1), (m2, p2), (m3, p3)):
        total = total + dot_nn(m[...], p[...])
    resid_ref[...] = total
    hat, _ = normalize(total)
    h_ref[...] = (hat * v_ref[3:4, :] + v_ref[4:5, :]).astype(BF)


def mix_call(parts, projs, x, vectors):
    rows, width = x.shape
    per = rows // BLK
    inner = parts[0].shape[1]
    low = pl.BlockSpec((BLK, inner), lambda t: (t, 0))
    whole = lambda t: (0, 0)
    return pl.pallas_call(
        mix_kernel,
        out_shape=(jax.ShapeDtypeStruct((rows, width), F32), jax.ShapeDtypeStruct((rows, width), BF)),
        grid=(per,),
        in_specs=[low] * 4
        + [pl.BlockSpec(projs[0].shape, whole)] * 4
        + [pl.BlockSpec((BLK, width), lambda t: (t, 0)), pl.BlockSpec(vectors.shape, whole)],
        out_specs=[pl.BlockSpec((BLK, width), lambda t: (t, 0))] * 2,
        cost_estimate=cost(8 * rows * width * inner, 12 * rows * width),
        name="mix",
    )(*parts, *projs, x, vectors)


def turn_kernel(n_ref, s_ref, f_ref, resid_ref, cot_ref, v_ref, p0, p1, p2, p3, gr_ref, ga_ref, g0, g1, g2, g3, sum_ref):
    grad = n_ref[...].astype(F32) + s_ref[...].astype(F32) + f_ref[...].astype(F32)
    hat, rstd = normalize(resid_ref[...])
    cot = cot_ref[...].astype(F32)
    e = grad * v_ref[3:4, :]
    back = e - jnp.mean(e, axis=-1, keepdims=True) - hat * jnp.mean(e * hat, axis=-1, keepdims=True)
    grad_resid = cot + rstd * back
    gr_ref[...] = grad_resid
    att = grad_resid.astype(BF)
    ga_ref[...] = att
    for g, p in ((g0, p0), (g1, p1), (g2, p2), (g3, p3)):
        g[...] = dot_nt(att, p[...]).astype(BF)

    @pl.when(pl.program_id(0) == 0)
    def _():
        sum_ref[...] = jnp.zeros_like(sum_ref)

    for k, v in enumerate((grad_resid, grad * hat, grad, cot)):
        sum_ref[k + 4 : k + 5, :] += jnp.sum(v, axis=0, keepdims=True)


def turn_call(near, swapped, far, resid, cot, vectors, projs):
    rows, width = resid.shape
    per = rows // BLK
    inner = projs[0].shape[0]
    low = pl.BlockSpec((BLK, width), lambda t: (t, 0))
    whole = lambda t: (0, 0)
    return pl.pallas_call(
        turn_kernel,
        out_shape=(
            jax.ShapeDtypeStruct((rows, width), F32),
            jax.ShapeDtypeStruct((rows, width), BF),
        )
        + (jax.ShapeDtypeStruct((rows, inner), BF),) * 4
        + (jax.ShapeDtypeStruct((8, width), F32),),
        grid=(per,),
        in_specs=[low] * 5
        + [pl.BlockSpec(vectors.shape, whole)]
        + [pl.BlockSpec(projs[0].shape, whole)] * 4,
        out_specs=[low, low]
        + [pl.BlockSpec((BLK, inner), lambda t: (t, 0))] * 4
        + [pl.BlockSpec((8, width), whole)],
        cost_estimate=cost(rows, width),
        name="turn",
    )(near, swapped, far, resid, cot, vectors, *projs)


def outer_kernel(m0, m1, m2, m3, g_ref, k0, s1, k2, s3):
    g = g_ref[...]
    for m, out in ((m1, s1), (m3, s3), (m0, k0), (m2, k2)):
        out[...] = dot_tn(m[...], g).astype(out.dtype)


def outer_call(parts, grad):
    rows, width = grad.shape
    shape = (parts[0].shape[1], width)
    vm = pl.BlockSpec(memory_space=pltpu.VMEM)
    return pl.pallas_call(
        outer_kernel,
        out_shape=tuple(jax.ShapeDtypeStruct(shape, t) for t in (F32, BF, F32, BF)),
        in_specs=[vm] * 5,
        out_specs=[vm] * 4,
        cost_estimate=cost(8 * rows * width * shape[0] * 8, 8 * rows * width),
        name="outer",
    )(*parts, grad)


def tally_kernel(steps, b_ref, gp_ref, hat_ref, w_ref, v_ref, pw_ref, up_ref, s_ref, keep_ref, send_ref, acc, col):
    t = pl.program_id(0)
    gp = gp_ref[...]
    cols = gp.shape[1]
    half = acc.shape[0] // 2

    @pl.when(t == 0)
    def _():
        acc[:cols, :] = jnp.zeros((cols, acc.shape[1]), F32)
        acc[cols:, :] = pw_ref[...]
        col[...] = jnp.zeros_like(col)

    acc[:cols, :] += dot_tn(gp, hat_ref[...])
    col[...] += dot_tn(gp, jnp.ones((gp.shape[0], 128), BF))

    @pl.when(t == steps - 1)
    def _():
        total = col[:, 0:1]
        moment = acc[:cols, :]
        w = w_ref[...].astype(F32)
        small = s_ref[...]
        row = lax.broadcasted_iota(jnp.int32, small.shape, 0)
        small = jnp.where(row == 0, jnp.sum(w * moment, axis=0, keepdims=True), small)
        small = jnp.where(row == 1, jnp.sum(w * total, axis=0, keepdims=True), small)
        bias = jnp.concatenate((col[...].T[0:1, :], jnp.zeros((1, small.shape[1] - cols), F32)), axis=1)
        small = jnp.where(row == 2, bias, small)
        small = jnp.where(row == 3, up_ref[...], small).astype(BF)
        acc[:cols, :] = moment * v_ref[0:1, :] + total * v_ref[1:2, :]
        split_out(b_ref, acc, keep_ref, send_ref)
        keep_ref[half:, :] = small
        send_ref[half:, :] = small


def tally_call(bid, gp, hat, w, vectors, proj_grad, up_grad, sums):
    rows, width = hat.shape
    cols = gp.shape[1]
    total = cols + proj_grad.shape[0]
    block = 2 * BLK
    steps = rows // block
    whole = lambda t, b: (0, 0)
    half = jax.ShapeDtypeStruct((total // 2 + sums.shape[0], width), BF)
    return pl.pallas_call(
        functools.partial(tally_kernel, steps),
        out_shape=(half, half),
        grid_spec=pltpu.PrefetchScalarGridSpec(
            num_scalar_prefetch=1,
            grid=(steps,),
            in_specs=[
                pl.BlockSpec((block, cols), lambda t, b: (t, 0)),
                pl.BlockSpec((block, width), lambda t, b: (t, 0)),
            ]
            + [pl.BlockSpec(v.shape, whole) for v in (w, vectors, proj_grad, up_grad, sums)],
            out_specs=[pl.BlockSpec(half.shape, whole)] * 2,
            scratch_shapes=[pltpu.VMEM((total, width), F32), pltpu.VMEM((cols, 128), F32)],
        ),
        cost_estimate=cost(cols, width),
        name="tally",
    )(bid, gp, hat, w, vectors, proj_grad, up_grad, sums)


def spread_kernel(gp_ref, w_ref, *outs):
    e = dot_nn(gp_ref[...], w_ref[...]).astype(BF)
    for k, out in enumerate(outs):

        @pl.when(pl.program_id(0) == k)
        def _(out=out):
            out[...] = e


def spread_call(gp, w, chunk):
    cols, width = w.shape
    whole = lambda t: (0, 0)
    return pl.pallas_call(
        spread_kernel,
        out_shape=(jax.ShapeDtypeStruct((chunk, width), BF),) * 4,
        grid=(4,),
        in_specs=[pl.BlockSpec((chunk, cols), lambda t: (t, 0)), pl.BlockSpec(w.shape, whole)],
        out_specs=[pl.BlockSpec((chunk, width), whole)] * 4,
        cost_estimate=cost(cols, width),
        name="spread",
    )(gp, w)


def unpack_kernel(counts, places, b_ref, *rest):
    acc = rest[-1]
    piece = acc.shape[0] // 8
    for (part, at), block in zip(places, spots(b_ref, 8), strict=True):
        value = rest[part][at : at + piece, :].astype(F32)
        acc[pl.ds(pl.multiple_of(block * piece, 8), piece), :] = value
    start = 0
    for out, count in zip(rest[-1 - len(counts) : -1], counts, strict=True):
        out[...] = acc[start : start + count, :]
        start += count


def unpack_call(bid, parts, places, counts):
    total = sum(counts)
    width = parts[0].shape[1]
    vm = pl.BlockSpec(memory_space=pltpu.VMEM)
    return pl.pallas_call(
        functools.partial(unpack_kernel, counts, places),
        out_shape=tuple(jax.ShapeDtypeStruct((n, width), F32) for n in counts),
        in_specs=[pl.BlockSpec(memory_space=pltpu.SMEM)] + [vm] * len(parts),
        out_specs=[vm] * len(counts),
        scratch_shapes=[pltpu.VMEM((total, width), F32)],
        cost_estimate=cost(total, width),
        name="unpack",
    )(bid, *parts)


def tie(x, *needed):
    return lax.optimization_barrier((x,) + needed)[0]


def across(pieces):
    return [swap(piece, "batch", 2 * d) for d, piece in enumerate(pieces, 1)]


def sum_rest(x):
    for level in range(3, lax.axis_size("batch").bit_length() - 1):
        x = (x.astype(F32) + swap(x, "batch", 1 << level).astype(F32)).astype(x.dtype)
    return x


def fold(kept, got):
    piece = kept.shape[0] // 4
    total = kept[:piece].astype(F32)
    for g in got:
        total = total + g[:piece].astype(F32)
    return sum_rest(total.astype(BF))


def quarters(x):
    piece = x.shape[0] // 4
    return [x[d * piece : (d + 1) * piece] for d in range(1, 4)]


def sum_group(x):
    x = x + swap(x, "head", 1)
    return x + swap(x, "head", 2)


def per_device(
    inputs,
    lengths,
    cotangent,
    gain_attn,
    shift_attn,
    weight_qkv,
    bias_qkv,
    weight_proj,
    bias_proj,
    gain_mlp,
    shift_mlp,
    weight_up,
    bias_up,
    weight_down,
    bias_down,
):
    chunk, width = inputs.shape
    group_rows = chunk * lax.axis_size("head")
    heads, triple = weight_qkv.shape[1:]
    cols = heads * triple
    inner = cols // 3
    own = lax.axis_index("head")
    hid = own.astype(jnp.int32).reshape(1)
    bid = (lax.axis_index("batch") % 8).astype(jnp.int32).reshape(1)
    lens = lengths[0]
    live_rows = jnp.sum(lens[:-1])
    places = own * chunk + jnp.arange(chunk, dtype=jnp.int32)
    live = (places < live_rows)[:, None]
    qkv_t = weight_qkv.transpose(1, 2, 0).reshape(cols, width)
    proj = weight_proj.reshape(inner, width)
    zero = jnp.zeros((width,), F32)
    vectors = jnp.stack(
        (gain_attn, shift_attn, bias_proj, gain_mlp, shift_mlp, bias_up, bias_down, zero)
    )

    x_far = swap(inputs, "head", 2)
    x_near = swap(inputs, "head", 1)
    begun = qkv_call(hid, inputs, x_near, vectors, qkv_t, bias_qkv, 0, group_rows, ())
    x_far = tie(x_far, begun[0])
    x_last = swap(x_far, "head", 1)
    queries, keys, values, values_t, hats = qkv_call(
        hid, x_far, x_last, vectors, qkv_t, bias_qkv, 2, group_rows, begun
    )
    grad_own = jnp.where(live, cotangent, jnp.zeros_like(cotangent))
    proj_far = swap(tie(proj, x_far), "head", 2)
    grad_far = swap(tie(grad_own, x_last), "head", 2)

    out_far, out_last, level_far, level_last = attend_call(
        lens, hid, queries, keys, values_t, 2, chunk
    )
    from_last = swap(out_last, "head", 2)
    from_far = swap(out_far, "head", 2)
    out_own, out_mate, level_own, level_mate = attend_call(
        lens, hid, tie(queries, out_far), keys, values_t, 0, chunk
    )
    grads = (grad_own, swap(tie(grad_own, out_far), "head", 1), grad_far, swap(grad_far, "head", 1))
    from_last = swap(tie(from_last, out_own, from_far), "head", 1)
    parts = (out_own, swap(out_mate, "head", 1), from_far, from_last)
    proj_last = swap(tie(proj_far, out_own), "head", 1)
    projs = (proj, swap(tie(proj, out_far), "head", 1), proj_far, proj_last)
    resid, h_own = mix_call(parts, projs, tie(inputs, grad_far), vectors)
    h_far = swap(h_own, "head", 2)
    h_near = swap(h_own, "head", 1)

    near = feed_call(h_own, h_near, grads[0], grads[1], weight_up, vectors, weight_down, 0, group_rows, ())
    h_far = tie(h_far, near[0])
    h_last = swap(h_far, "head", 1)
    act, grad_up, norm_far, norm_last, down_far, down_last = feed_call(
        h_far, h_last, grads[2], grads[3], weight_up, vectors, weight_down, 2, group_rows, near[:2]
    )
    near_swapped = swap(near[3], "head", 1)
    near_down = swap(near[5], "head", 1)
    norm_far = tie(norm_far, near_swapped, near_down)
    far_sum = (norm_far.astype(F32) + swap(norm_last, "head", 1).astype(F32)).astype(BF)
    grad_far_sum = swap(far_sum, "head", 2)
    down_swapped = swap(tie(down_last, far_sum), "head", 1)

    keep_feed, send_feed, grad_bup = weigh_call(
        bid, (h_own, h_near, h_far, h_last), tie(act, far_sum), grad_up, grads
    )
    other_feed = swap(send_feed, "batch", 1)
    grad_resid, grad_att, grad_near, grad_mate, grad_cross, grad_last, sums = turn_call(
        near[2],
        near_swapped,
        tie(grad_far_sum, grad_bup, down_swapped),
        resid,
        grad_own,
        vectors,
        projs,
    )
    got_last = swap(grad_last, "head", 2)
    got = swap(grad_cross, "head", 2)
    grad_mate = swap(grad_mate, "head", 1)
    own_proj, near_sent, cross_proj, far_sent = outer_call(parts, grad_att)
    down_far = tie(down_far, grad_att)
    down_sum = (down_far.astype(F32) + down_swapped.astype(F32)).astype(BF)
    got_last, near_sent, far_sent, down_sum = lax.optimization_barrier(
        (got_last, near_sent, far_sent, down_sum)
    )
    merged_grads = (grad_near, grad_mate, got, swap(got_last, "head", 1))
    grad_near_proj = own_proj + swap(near_sent, "head", 1).astype(F32)
    pair_proj = (cross_proj + swap(far_sent, "head", 1).astype(F32)).astype(BF)
    far_proj = swap(pair_proj, "head", 2)

    kept_feed = (keep_feed.astype(F32) + tie(other_feed, got, got_last).astype(F32)).astype(BF)
    got_feed = across(quarters(kept_feed))
    down_other = swap(tie(down_sum, kept_feed), "head", 2)

    grad_packed = attend_back_call(
        lens,
        hid,
        tie(queries, kept_feed, grad_near_proj),
        keys,
        values,
        merged_grads,
        (out_own, out_mate, out_far, out_last),
        (level_own, level_mate, level_far, level_last),
        chunk,
    )
    got_feed = [tie(g, grad_packed) for g in got_feed]
    grad_wproj = grad_near_proj + tie(far_proj, grad_packed).astype(F32)
    total_feed = fold(kept_feed, got_feed)
    gathered_feed = across([total_feed] * 3)
    keep, send = tally_call(
        bid, tie(grad_packed, total_feed, down_other), hats, qkv_t, vectors, grad_wproj, grad_bup, sums
    )
    other = swap(send, "batch", 1)
    spread = spread_call(tie(grad_packed, keep), qkv_t, chunk)
    gathered_feed, spread = lax.optimization_barrier((gathered_feed, spread))
    e_own, e_near, e_far, e_last = spread

    feed_first = jnp.concatenate((total_feed, gathered_feed[0]), axis=0)
    feed_second = jnp.concatenate(gathered_feed[1:], axis=0)
    feed_got = swap(feed_first, "batch", 1)
    summed = (keep.astype(F32) + tie(other, feed_first, feed_second).astype(F32)).astype(BF)
    kept, small = summed[:-8], summed[-8:]
    pieces = [jnp.concatenate((q, small), axis=0) for q in quarters(kept)]
    e_swapped = swap(tie(e_last, *pieces), "head", 1)
    e_sum = (e_far.astype(F32) + e_swapped.astype(F32)).astype(BF)
    output = resid + near[4].astype(F32) + near_down.astype(F32) + tie(down_other, e_sum).astype(F32)
    output = (output + bias_down).astype(BF)
    got_attn = [tie(g, feed_got, output) for g in across(pieces)]

    tiny = [small.astype(F32)] + [g[-8:].astype(F32) for g in got_attn]
    small = sum_rest((tiny[0] + tiny[1]) + (tiny[2] + tiny[3]))
    total_attn = fold(kept, got_attn)
    gathered_attn = across([total_attn] * 3)
    second_got = swap(tie(feed_second, total_attn), "batch", 1)
    e_other = swap(tie(e_sum, total_attn), "head", 2)
    half = jnp.concatenate([total_attn] + [tie(g, second_got) for g in gathered_attn], axis=0)
    e_mate = swap(tie(e_near, half), "head", 1)
    last = swap(half, "batch", 1)
    biases = small[2:4]
    small = sum_group(tie(small, half))
    e_own = e_own.astype(F32) + e_mate.astype(F32) + tie(e_other, half).astype(F32)

    x_hat, x_rstd = normalize(tie(inputs, half).astype(F32))
    e_own = e_own * gain_attn
    grad_inputs = (
        grad_resid
        + x_rstd
        * (
            e_own
            - jnp.mean(e_own, axis=-1, keepdims=True)
            - x_hat * jnp.mean(e_own * x_hat, axis=-1, keepdims=True)
        )
    ).astype(BF)
    pair = tuple(k * total_feed.shape[0] for k in range(2))
    places = tuple((k, at) for k in range(4) for at in pair)
    parts = (feed_first, feed_second, feed_got, tie(second_got, half))
    sum_wup, sum_wdown = unpack_call(bid, parts, places, (width, width))
    places = tuple((k, at * total_attn.shape[0]) for k in range(2) for at in range(4))
    parts = (half, tie(last, sum_wup, grad_inputs))
    sum_wqkv, sum_wproj = unpack_call(bid, parts, places, (cols, inner))
    return (
        output,
        grad_inputs,
        small[0],
        small[1],
        sum_wqkv.reshape(heads, triple, width).transpose(2, 0, 1),
        biases[0, :cols].reshape(heads, triple),
        sum_wproj.reshape(heads, inner // heads, width),
        small[4],
        small[5],
        small[6],
        sum_wup,
        biases[1],
        sum_wdown,
        small[7],
    )


def solution(mesh):
    rows = P(("batch", "head"), None)
    in_specs = (
        rows,
        P("batch", None),
        rows,
        P(),
        P(),
        P(None, "head", None),
        P("head", None),
        P("head", None, None),
        P(),
        P(),
        P(),
        P(None, "head"),
        P("head"),
        P("head", None),
        P(),
    )
    out_specs = (
        rows,
        rows,
        P(),
        P(),
        P(None, "head", None),
        P("head", None),
        P("head", None, None),
        P(),
        P(),
        P(),
        P(None, "head"),
        P("head"),
        P("head", None),
        P(),
    )
    return jax.shard_map(
        per_device, mesh=mesh, in_specs=in_specs, out_specs=out_specs, check_vma=False
    )
```

```python
import functools
import math

import jax
import jax.numpy as jnp
from jax import lax
from jax.experimental import pallas as pl
from jax.experimental.pallas import tpu as pltpu
from jax.sharding import PartitionSpec as P

F32 = jnp.float32
BF = jnp.bfloat16
BLK = 256
NEG = -1e30
EPS = 1e-05
GELU_C = math.sqrt(2.0 / math.pi)
GELU_A = 0.044715


def dot_nn(a, b):
    return lax.dot_general(a, b, (((1,), (0,)), ((), ())), preferred_element_type=F32)


def dot_nt(a, b):
    return lax.dot_general(a, b, (((1,), (1,)), ((), ())), preferred_element_type=F32)


def dot_tn(a, b):
    return lax.dot_general(a, b, (((0,), (0,)), ((), ())), preferred_element_type=F32)


def cost(flops, nbytes, trans=0):
    return pl.CostEstimate(flops=int(flops), bytes_accessed=int(nbytes), transcendentals=int(trans))


def swap(x, axis, bits):
    size = lax.axis_size(axis)
    return lax.ppermute(x, axis, [(i, i ^ bits) for i in range(size)])


def normalize(v):
    center = v - jnp.mean(v, axis=-1, keepdims=True)
    rstd = lax.rsqrt(jnp.mean(center * center, axis=-1, keepdims=True) + EPS)
    return center * rstd, rstd


def qkv_kernel(heads, hd, steps, h_ref, a_ref, b_ref, v_ref, w_ref, bias_ref, *rest):
    q_out, k_out, v_out, vt_out, hat_out = rest[-5:]
    t = pl.program_id(0)
    x = jnp.where(t < steps // 2, a_ref[...], b_ref[...]).astype(F32)
    xhat, _ = normalize(x)
    hat_out[...] = xhat.astype(BF)
    h1 = (xhat * v_ref[0:1, :] + v_ref[1:2, :]).astype(BF)
    bias = jnp.concatenate([bias_ref[h : h + 1, :] for h in range(heads)], axis=1)
    packed = (dot_nt(h1, w_ref[...]) + bias).astype(BF)
    for h in range(heads):
        o = 3 * hd * h
        q_out[h] = packed[:, o : o + hd]
        k_out[h] = packed[:, o + hd : o + 2 * hd]
        v = packed[:, o + 2 * hd : o + 3 * hd]
        v_out[h] = v
        vt_out[h] = v.T


def qkv_call(hid, a, b, vectors, w, bias, first, group_rows, before):
    rows, width = a.shape
    heads, triple = bias.shape
    hd = triple // 3
    per = rows // BLK
    steps = 2 * per
    place = lambda t, h: (h[0] ^ (first + t // per)) * per + t % per
    whole = lambda t, h: (0, 0)
    out_shape = tuple(
        jax.ShapeDtypeStruct(s, BF)
        for s in ((heads, group_rows, hd),) * 3 + ((heads, hd, group_rows), (group_rows, width))
    )
    in_specs = [
        pl.BlockSpec((BLK, width), lambda t, h: (jnp.minimum(t, per - 1), 0)),
        pl.BlockSpec((BLK, width), lambda t, h: (jnp.maximum(t - per, 0), 0)),
        pl.BlockSpec(vectors.shape, whole),
        pl.BlockSpec(w.shape, whole),
        pl.BlockSpec(bias.shape, whole),
    ] + [pl.BlockSpec(memory_space=pl.ANY)] * len(before)
    return pl.pallas_call(
        functools.partial(qkv_kernel, heads, hd, steps),
        out_shape=out_shape,
        grid_spec=pltpu.PrefetchScalarGridSpec(
            num_scalar_prefetch=1,
            grid=(steps,),
            in_specs=in_specs,
            out_specs=[pl.BlockSpec((heads, BLK, hd), lambda t, h: (0, place(t, h), 0))] * 3
            + [
                pl.BlockSpec((heads, hd, BLK), lambda t, h: (0, 0, place(t, h))),
                pl.BlockSpec((BLK, width), lambda t, h: (first * per + t, 0)),
            ],
        ),
        input_output_aliases={6 + i: i for i in range(len(before))},
        cost_estimate=cost(4 * rows * width * w.shape[0], 12 * rows * width),
        name="qkv",
    )(hid, a, b, vectors, w, bias, *before)


def row_segment(len_ref, row):
    low = row
    high = row + 1
    start = jnp.int32(0)
    for k in range(len_ref.shape[0] - 1):
        stop = start + len_ref[k]
        inside = (row >= start) & (row < stop)
        low = jnp.where(inside, start, low)
        high = jnp.where(inside, stop, high)
        start = stop
    return low, high


def lane_starts(len_ref, row, width):
    i = row + lax.broadcasted_iota(jnp.int32, (1, width), 1)
    start = jnp.zeros((1, width), jnp.int32)
    stop = jnp.int32(0)
    for k in range(len_ref.shape[0] - 1):
        stop = stop + len_ref[k]
        start = jnp.where(i >= stop, stop, start)
    return jnp.where(i >= stop, i, start), i


def attend_kernel(heads, first, per, scale, len_ref, h_ref, q_ref, k_ref, vt_ref, oa_ref, ob_ref, la_ref, lb_ref, s_s, m_s, z_s, acc_s):
    t = pl.program_id(0)
    row = ((h_ref[0] ^ (first + t // per)) * per + t % per) * BLK
    start, i = lane_starts(len_ref, row, BLK)
    low, _ = row_segment(len_ref, row)
    m_s[...] = jnp.zeros_like(m_s)
    z_s[...] = jnp.zeros_like(z_s)
    acc_s[...] = jnp.zeros_like(acc_s)
    qs = [q_ref[h] * jnp.asarray(scale, BF) for h in range(heads)]
    blocks = (low // BLK, row // BLK + 1)

    def measure(jb, carry):
        j0 = pl.multiple_of(jb * BLK, BLK)
        j = j0 + lax.broadcasted_iota(jnp.int32, (BLK, BLK), 0)
        mask = (j >= start) & (j <= i)
        scores = [dot_nt(k_ref[h, pl.ds(j0, BLK), :], qs[h]) for h in range(heads)]
        tops = [m_s[h : h + 1, :] for h in range(heads)]
        for h in range(heads):
            s = jnp.where(mask, scores[h], 0.0)
            s_s[h, pl.ds(j0, BLK), :] = s
            tops[h] = jnp.maximum(tops[h], jnp.max(jnp.abs(s), axis=0, keepdims=True))
        for h in range(heads):
            m_s[h : h + 1, :] = tops[h]
        return carry

    lax.fori_loop(*blocks, measure, 0)
    tops = [m_s[h : h + 1, :] for h in range(heads)]
    offsets = [jnp.exp(-top) for top in tops]

    def gather(jb, carry):
        j0 = pl.multiple_of(jb * BLK, BLK)
        sums, weights = [], []
        for h in range(heads):
            s = s_s[h, pl.ds(j0, BLK), :]
            u = jnp.exp(jnp.abs(s) - tops[h]) - offsets[h]
            sums.append(jnp.sum(u, axis=0, keepdims=True))
            weights.append(jnp.where(s < 0, -u, u).astype(BF))
        adds = [dot_nn(vt_ref[h, :, pl.ds(j0, BLK)], weights[h]) for h in range(heads)]
        for h in range(heads):
            z_s[h : h + 1, :] += sums[h]
            acc_s[h] += adds[h]
        return carry

    lax.fori_loop(*blocks, gather, 0)
    count = (i - start + 1).astype(F32)
    outs, levels = [], []
    for h in range(heads):
        z = z_s[h : h + 1, :] + count * offsets[h]
        outs.append((acc_s[h] / z).T)
        levels.append(tops[h] + jnp.log(z))
    out = jnp.concatenate(outs, axis=1).astype(BF)

    def store(o_ref, l_ref):
        o_ref[...] = out
        for h in range(heads):
            l_ref[h : h + 1, :] = levels[h]

    @pl.when(t < per)
    def _():
        store(oa_ref, la_ref)

    @pl.when(t >= per)
    def _():
        store(ob_ref, lb_ref)


def attend_call(lengths, hid, q, k, vt, first, chunk):
    heads, rows, hd = q.shape
    per = chunk // BLK
    steps = 2 * per
    place = lambda t, n, h: (0, (h[0] ^ (first + t // per)) * per + t % per, 0)
    whole = lambda t, n, h: (0, 0, 0)
    return pl.pallas_call(
        functools.partial(attend_kernel, heads, first, per, 1.0 / math.sqrt(hd)),
        out_shape=(jax.ShapeDtypeStruct((chunk, heads * hd), BF),) * 2
        + (jax.ShapeDtypeStruct((8, chunk), F32),) * 2,
        grid_spec=pltpu.PrefetchScalarGridSpec(
            num_scalar_prefetch=2,
            grid=(steps,),
            in_specs=[
                pl.BlockSpec((heads, BLK, hd), place),
                pl.BlockSpec((heads, rows, hd), whole),
                pl.BlockSpec((heads, hd, rows), whole),
            ],
            out_specs=[
                pl.BlockSpec((BLK, heads * hd), lambda t, n, h: (jnp.minimum(t, per - 1), 0)),
                pl.BlockSpec((BLK, heads * hd), lambda t, n, h: (jnp.maximum(t - per, 0), 0)),
                pl.BlockSpec((8, BLK), lambda t, n, h: (0, jnp.minimum(t, per - 1))),
                pl.BlockSpec((8, BLK), lambda t, n, h: (0, jnp.maximum(t - per, 0))),
            ],
            scratch_shapes=[
                pltpu.VMEM((heads, rows, BLK), F32),
                pltpu.VMEM((8, BLK), F32),
                pltpu.VMEM((8, BLK), F32),
                pltpu.VMEM((heads, hd, BLK), F32),
            ],
        ),
        cost_estimate=cost(rows, hd),
        name="attend",
    )(lengths, hid, q, k, vt)


def attend_back_kernel(chunk, scale, len_ref, h_ref, q_ref, k_ref, v_ref, *rest):
    g_refs, o_refs, l_refs = rest[0:4], rest[4:8], rest[8:12]
    gp_ref, q_s, g_s, kt_s, l_s, c_s, d_s, dq_s, dk_s, dv_s = rest[12:]
    heads, rows, hd = q_ref.shape
    blocks = rows // BLK
    per = chunk // BLK
    own = h_ref[0]
    for c in range(4):
        r0 = pl.multiple_of((own ^ c) * chunk, chunk)
        g = g_refs[c][...]
        o = o_refs[c][...]
        for h in range(heads):
            gh = g[:, h * hd : (h + 1) * hd]
            g_s[h, pl.ds(r0, chunk), :] = gh
            both = gh.astype(F32) * o[:, h * hd : (h + 1) * hd].astype(F32)
            d_s[h : h + 1, pl.ds(r0, chunk)] = jnp.sum(both.T, axis=0, keepdims=True)
        level = l_refs[c][...]
        l_s[:, pl.ds(r0, chunk)] = level
        c_s[:, pl.ds(r0, chunk)] = jnp.exp(-level)
    for h in range(heads):
        q_s[h] = q_ref[h] * jnp.asarray(scale, BF)
    dq_s[...] = jnp.zeros_like(dq_s)

    def out_row(block):
        return pl.multiple_of(((own ^ (block // per)) * per + block % per) * BLK, BLK)

    def outer(jb, carry):
        j0 = pl.multiple_of(jb * BLK, BLK)
        dk_s[...] = jnp.zeros_like(dk_s)
        dv_s[...] = jnp.zeros_like(dv_s)
        for h in range(heads):
            kt_s[h] = k_ref[h, pl.ds(j0, BLK), :].T
        _, stop = row_segment(len_ref, j0 + BLK - 1)
        j = j0 + lax.broadcasted_iota(jnp.int32, (BLK, BLK), 0)

        def inner(ib, carry):
            i0 = pl.multiple_of(ib * BLK, BLK)
            start, i = lane_starts(len_ref, i0, BLK)
            mask = (j >= start) & (j <= i)
            at = pl.ds(i0, BLK)
            qh = [q_s[h, at, :] for h in range(heads)]
            gh = [g_s[h, at, :] for h in range(heads)]
            scores = [dot_nt(k_ref[h, pl.ds(j0, BLK), :], qh[h]) for h in range(heads)]
            gws = [dot_nt(v_ref[h, pl.ds(j0, BLK), :], gh[h]) for h in range(heads)]
            ws, gss = [], []
            for h in range(heads):
                s, gw = scores[h], gws[h]
                level = l_s[h : h + 1, at]
                offset = c_s[h : h + 1, at]
                d = d_s[h : h + 1, at]
                p = jnp.exp(jnp.where(mask, jnp.abs(s), NEG) - level)
                u = p - jnp.where(mask, offset, 0.0)
                sign = jnp.clip(s * 1e38, -1.0, 1.0)
                w = (sign * u).astype(BF)
                gs = (p * (gw - sign * d)).astype(BF)
                ws.append(w)
                gss.append(gs)
            dvs = [dot_nn(ws[h], gh[h]) for h in range(heads)]
            dks = [dot_nn(gss[h], qh[h]) for h in range(heads)]
            dqs = [dot_nn(kt_s[h], gss[h]) for h in range(heads)]
            for h in range(heads):
                dv_s[h] += dvs[h]
                dk_s[h] += dks[h]
                dq_s[h, :, at] += dqs[h]
            return carry

        lax.fori_loop(jb, (stop - 1) // BLK + 1, inner, 0)
        for h in range(heads):
            at = pl.ds(out_row(jb), BLK)
            gp_ref[at, (3 * h + 1) * hd : (3 * h + 2) * hd] = dk_s[h].astype(BF)
            gp_ref[at, (3 * h + 2) * hd : (3 * h + 3) * hd] = dv_s[h].astype(BF)
        return carry

    lax.fori_loop(0, blocks, outer, 0)

    def finish(ib, carry):
        i0 = pl.multiple_of(ib * BLK, BLK)
        for h in range(heads):
            dq = (dq_s[h, :, pl.ds(i0, BLK)] * scale).T.astype(BF)
            gp_ref[pl.ds(out_row(ib), BLK), 3 * h * hd : (3 * h + 1) * hd] = dq
        return carry

    lax.fori_loop(0, blocks, finish, 0)


def attend_back_call(lengths, hid, q, k, v, grads, outs, levels, chunk):
    heads, rows, hd = q.shape
    vm = pl.BlockSpec(memory_space=pltpu.VMEM)
    sm = pl.BlockSpec(memory_space=pltpu.SMEM)
    return pl.pallas_call(
        functools.partial(attend_back_kernel, chunk, 1.0 / math.sqrt(hd)),
        out_shape=jax.ShapeDtypeStruct((rows, heads * 3 * hd), BF),
        in_specs=[sm, sm] + [vm] * 15,
        out_specs=vm,
        scratch_shapes=[
            pltpu.VMEM((heads, rows, hd), BF),
            pltpu.VMEM((heads, rows, hd), BF),
            pltpu.VMEM((heads, hd, BLK), BF),
            pltpu.VMEM((8, rows), F32),
            pltpu.VMEM((8, rows), F32),
            pltpu.VMEM((8, rows), F32),
            pltpu.VMEM((heads, hd, rows), F32),
            pltpu.VMEM((heads, BLK, hd), F32),
            pltpu.VMEM((heads, BLK, hd), F32),
        ],
        cost_estimate=cost(heads * rows * rows * hd * 20, 30 * rows * heads * hd, heads * rows * rows // 2),
        name="attend_back",
    )(lengths, hid, q, k, v, *grads, *outs, *levels)


def feed_kernel(steps, ha_ref, hb_ref, ga_ref, gb_ref, up_ref, v_ref, down_ref, *rest):
    act_ref, gup_ref, gna_ref, gnb_ref, outa_ref, outb_ref = rest[-6:]
    early = pl.program_id(0) < steps // 2
    h2 = jnp.where(early, ha_ref[...], hb_ref[...])
    grad = jnp.where(early, ga_ref[...], gb_ref[...])
    u = dot_nn(h2, up_ref[...]) + v_ref[5:6, :]
    square = u * u
    tanh = jnp.tanh(u * (GELU_C + (GELU_C * GELU_A) * square))
    half = 0.5 * (1.0 + tanh)
    act = (u * half).astype(BF)
    slope = half + (0.5 * u) * (1.0 - tanh * tanh) * (GELU_C + (3.0 * GELU_C * GELU_A) * square)
    gup = (dot_nt(grad, down_ref[...]) * slope).astype(BF)
    act_ref[...] = act
    gup_ref[...] = gup
    gn = dot_nt(gup, up_ref[...]).astype(BF)
    out = dot_nn(act, down_ref[...]).astype(BF)

    @pl.when(early)
    def _():
        gna_ref[...] = gn
        outa_ref[...] = out

    @pl.when(jnp.logical_not(early))
    def _():
        gnb_ref[...] = gn
        outb_ref[...] = out


def feed_call(ha, hb, ga, gb, up, vectors, down, first, group_rows, before):
    rows, width = ha.shape
    hidden = up.shape[1]
    per = rows // BLK
    steps = 2 * per
    whole = lambda t: (0, 0)
    early = pl.BlockSpec((BLK, width), lambda t: (jnp.minimum(t, per - 1), 0))
    late = pl.BlockSpec((BLK, width), lambda t: (jnp.maximum(t - per, 0), 0))
    return pl.pallas_call(
        functools.partial(feed_kernel, steps),
        out_shape=(
            jax.ShapeDtypeStruct((group_rows, hidden), BF),
            jax.ShapeDtypeStruct((group_rows, hidden), BF),
        )
        + (jax.ShapeDtypeStruct((rows, width), BF),) * 4,
        grid=(steps,),
        in_specs=[
            early,
            late,
            early,
            late,
            pl.BlockSpec(up.shape, whole),
            pl.BlockSpec(vectors.shape, whole),
            pl.BlockSpec(down.shape, whole),
        ]
        + [pl.BlockSpec(memory_space=pl.ANY)] * len(before),
        out_specs=[
            pl.BlockSpec((BLK, hidden), lambda t: (first * per + t, 0)),
            pl.BlockSpec((BLK, hidden), lambda t: (first * per + t, 0)),
            early,
            late,
            early,
            late,
        ],
        input_output_aliases={7 + i: i for i in range(len(before))},
        cost_estimate=cost(16 * rows * width * hidden, 16 * rows * width, 2 * rows * hidden),
        name="feed",
    )(ha, hb, ga, gb, up, vectors, down, *before)


def spots(b_ref, pieces):
    return [b_ref[0] ^ (2 * (spot % 4) + spot // 4) for spot in range(pieces)]


def split_out(b_ref, acc, keep_ref, send_ref):
    piece = acc.shape[0] // 8
    for spot, block in enumerate(spots(b_ref, 8)):
        out = keep_ref if spot < 4 else send_ref
        value = acc[pl.ds(pl.multiple_of(block * piece, 8), piece), :]
        out[(spot % 4) * piece : (spot % 4 + 1) * piece, :] = value.astype(BF)


def weigh_kernel(tiles, b_ref, h0, h1, h2, h3, act_ref, up_ref, g0, g1, g2, g3, keep_ref, send_ref, bias_ref, acc):
    t = pl.program_id(0)
    tile = acc.shape[0] // (2 * tiles)
    chunk = h0.shape[0]
    at = pl.ds(pl.multiple_of(t * tile, tile), tile)

    @pl.when(t == 0)
    def _():
        bias_ref[...] = jnp.sum(up_ref[...].astype(F32), axis=0, keepdims=True)

    @pl.when(t < tiles)
    def _():
        total = dot_tn(h0[...], up_ref[:chunk, :])
        for k, h in enumerate((h1, h2, h3)):
            total = total + dot_tn(h[...], up_ref[(k + 1) * chunk : (k + 2) * chunk, :])
        acc[at, :] = total

    @pl.when(t >= tiles)
    def _():
        total = dot_tn(act_ref[:chunk, :], g0[...])
        for k, g in enumerate((g1, g2, g3)):
            total = total + dot_tn(act_ref[(k + 1) * chunk : (k + 2) * chunk, :], g[...])
        acc[at, :] = total

    @pl.when(t == 2 * tiles - 1)
    def _():
        split_out(b_ref, acc, keep_ref, send_ref)


def weigh_call(bid, hs, act, up, grads):
    chunk, width = hs[0].shape
    rows, hidden = act.shape
    tile = 256
    tiles = width // tile
    whole = lambda t, b: (0, 0)
    total = width + hidden
    half = jax.ShapeDtypeStruct((total // 2, width), BF)
    return pl.pallas_call(
        functools.partial(weigh_kernel, tiles),
        out_shape=(half, half, jax.ShapeDtypeStruct((1, hidden), F32)),
        grid_spec=pltpu.PrefetchScalarGridSpec(
            num_scalar_prefetch=1,
            grid=(2 * tiles,),
            in_specs=[pl.BlockSpec((chunk, tile), lambda t, b: (0, jnp.minimum(t, tiles - 1)))] * 4
            + [
                pl.BlockSpec((rows, tile), lambda t, b: (0, jnp.maximum(t - tiles, 0))),
                pl.BlockSpec((rows, hidden), whole),
            ]
            + [pl.BlockSpec((chunk, width), whole)] * 4,
            out_specs=[
                pl.BlockSpec(half.shape, whole),
                pl.BlockSpec(half.shape, whole),
                pl.BlockSpec((1, hidden), whole),
            ],
            scratch_shapes=[pltpu.VMEM((total, width), F32)],
        ),
        cost_estimate=cost(4 * rows * width * hidden, 12 * rows * width),
        name="weigh",
    )(bid, *hs, act, up, *grads)


def mix_kernel(m0, m1, m2, m3, p0, p1, p2, p3, x_ref, v_ref, resid_ref, h_ref):
    total = x_ref[...].astype(F32) + v_ref[2:3, :]
    for m, p in ((m0, p0), (m1, p1), (m2, p2), (m3, p3)):
        total = total + dot_nn(m[...], p[...])
    resid_ref[...] = total
    hat, _ = normalize(total)
    h_ref[...] = (hat * v_ref[3:4, :] + v_ref[4:5, :]).astype(BF)


def mix_call(parts, projs, x, vectors):
    rows, width = x.shape
    per = rows // BLK
    inner = parts[0].shape[1]
    low = pl.BlockSpec((BLK, inner), lambda t: (t, 0))
    whole = lambda t: (0, 0)
    return pl.pallas_call(
        mix_kernel,
        out_shape=(jax.ShapeDtypeStruct((rows, width), F32), jax.ShapeDtypeStruct((rows, width), BF)),
        grid=(per,),
        in_specs=[low] * 4
        + [pl.BlockSpec(projs[0].shape, whole)] * 4
        + [pl.BlockSpec((BLK, width), lambda t: (t, 0)), pl.BlockSpec(vectors.shape, whole)],
        out_specs=[pl.BlockSpec((BLK, width), lambda t: (t, 0))] * 2,
        cost_estimate=cost(8 * rows * width * inner, 12 * rows * width),
        name="mix",
    )(*parts, *projs, x, vectors)


def turn_kernel(n_ref, s_ref, f_ref, resid_ref, cot_ref, v_ref, p0, p1, p2, p3, gr_ref, ga_ref, g0, g1, g2, g3, sum_ref):
    grad = n_ref[...].astype(F32) + s_ref[...].astype(F32) + f_ref[...].astype(F32)
    hat, rstd = normalize(resid_ref[...])
    cot = cot_ref[...].astype(F32)
    e = grad * v_ref[3:4, :]
    back = e - jnp.mean(e, axis=-1, keepdims=True) - hat * jnp.mean(e * hat, axis=-1, keepdims=True)
    grad_resid = cot + rstd * back
    gr_ref[...] = grad_resid
    att = grad_resid.astype(BF)
    ga_ref[...] = att
    for g, p in ((g0, p0), (g1, p1), (g2, p2), (g3, p3)):
        g[...] = dot_nt(att, p[...]).astype(BF)

    @pl.when(pl.program_id(0) == 0)
    def _():
        sum_ref[...] = jnp.zeros_like(sum_ref)

    for k, v in enumerate((grad_resid, grad * hat, grad, cot)):
        sum_ref[k + 4 : k + 5, :] += jnp.sum(v, axis=0, keepdims=True)


def turn_call(near, swapped, far, resid, cot, vectors, projs):
    rows, width = resid.shape
    per = rows // BLK
    inner = projs[0].shape[0]
    low = pl.BlockSpec((BLK, width), lambda t: (t, 0))
    whole = lambda t: (0, 0)
    return pl.pallas_call(
        turn_kernel,
        out_shape=(
            jax.ShapeDtypeStruct((rows, width), F32),
            jax.ShapeDtypeStruct((rows, width), BF),
        )
        + (jax.ShapeDtypeStruct((rows, inner), BF),) * 4
        + (jax.ShapeDtypeStruct((8, width), F32),),
        grid=(per,),
        in_specs=[low] * 5
        + [pl.BlockSpec(vectors.shape, whole)]
        + [pl.BlockSpec(projs[0].shape, whole)] * 4,
        out_specs=[low, low]
        + [pl.BlockSpec((BLK, inner), lambda t: (t, 0))] * 4
        + [pl.BlockSpec((8, width), whole)],
        cost_estimate=cost(rows, width),
        name="turn",
    )(near, swapped, far, resid, cot, vectors, *projs)


def outer_kernel(m0, m1, m2, m3, g_ref, k0, s1, k2, s3):
    g = g_ref[...]
    for m, out in ((m1, s1), (m3, s3), (m0, k0), (m2, k2)):
        out[...] = dot_tn(m[...], g).astype(out.dtype)


def outer_call(parts, grad):
    rows, width = grad.shape
    shape = (parts[0].shape[1], width)
    vm = pl.BlockSpec(memory_space=pltpu.VMEM)
    return pl.pallas_call(
        outer_kernel,
        out_shape=tuple(jax.ShapeDtypeStruct(shape, t) for t in (F32, BF, F32, BF)),
        in_specs=[vm] * 5,
        out_specs=[vm] * 4,
        cost_estimate=cost(8 * rows * width * shape[0] * 8, 8 * rows * width),
        name="outer",
    )(*parts, grad)


def tally_kernel(steps, b_ref, gp_ref, hat_ref, w_ref, v_ref, pw_ref, up_ref, s_ref, keep_ref, send_ref, acc, col):
    t = pl.program_id(0)
    gp = gp_ref[...]
    cols = gp.shape[1]
    half = acc.shape[0] // 2

    @pl.when(t == 0)
    def _():
        acc[:cols, :] = jnp.zeros((cols, acc.shape[1]), F32)
        acc[cols:, :] = pw_ref[...]
        col[...] = jnp.zeros_like(col)

    acc[:cols, :] += dot_tn(gp, hat_ref[...])
    col[...] += dot_tn(gp, jnp.ones((gp.shape[0], 128), BF))

    @pl.when(t == steps - 1)
    def _():
        total = col[:, 0:1]
        moment = acc[:cols, :]
        w = w_ref[...].astype(F32)
        small = s_ref[...]
        row = lax.broadcasted_iota(jnp.int32, small.shape, 0)
        small = jnp.where(row == 0, jnp.sum(w * moment, axis=0, keepdims=True), small)
        small = jnp.where(row == 1, jnp.sum(w * total, axis=0, keepdims=True), small)
        bias = jnp.concatenate((col[...].T[0:1, :], jnp.zeros((1, small.shape[1] - cols), F32)), axis=1)
        small = jnp.where(row == 2, bias, small)
        small = jnp.where(row == 3, up_ref[...], small).astype(BF)
        acc[:cols, :] = moment * v_ref[0:1, :] + total * v_ref[1:2, :]
        split_out(b_ref, acc, keep_ref, send_ref)
        keep_ref[half:, :] = small
        send_ref[half:, :] = small


def tally_call(bid, gp, hat, w, vectors, proj_grad, up_grad, sums):
    rows, width = hat.shape
    cols = gp.shape[1]
    total = cols + proj_grad.shape[0]
    block = 4 * BLK
    steps = rows // block
    whole = lambda t, b: (0, 0)
    half = jax.ShapeDtypeStruct((total // 2 + sums.shape[0], width), BF)
    return pl.pallas_call(
        functools.partial(tally_kernel, steps),
        out_shape=(half, half),
        grid_spec=pltpu.PrefetchScalarGridSpec(
            num_scalar_prefetch=1,
            grid=(steps,),
            in_specs=[
                pl.BlockSpec((block, cols), lambda t, b: (t, 0)),
                pl.BlockSpec((block, width), lambda t, b: (t, 0)),
            ]
            + [pl.BlockSpec(v.shape, whole) for v in (w, vectors, proj_grad, up_grad, sums)],
            out_specs=[pl.BlockSpec(half.shape, whole)] * 2,
            scratch_shapes=[pltpu.VMEM((total, width), F32), pltpu.VMEM((cols, 128), F32)],
        ),
        cost_estimate=cost(cols, width),
        name="tally",
    )(bid, gp, hat, w, vectors, proj_grad, up_grad, sums)


def spread_kernel(gp_ref, w_ref, *outs):
    e = dot_nn(gp_ref[...], w_ref[...]).astype(BF)
    for k, out in enumerate(outs):

        @pl.when(pl.program_id(0) == k)
        def _(out=out):
            out[...] = e


def spread_call(gp, w, chunk):
    cols, width = w.shape
    whole = lambda t: (0, 0)
    return pl.pallas_call(
        spread_kernel,
        out_shape=(jax.ShapeDtypeStruct((chunk, width), BF),) * 4,
        grid=(4,),
        in_specs=[pl.BlockSpec((chunk, cols), lambda t: (t, 0)), pl.BlockSpec(w.shape, whole)],
        out_specs=[pl.BlockSpec((chunk, width), whole)] * 4,
        cost_estimate=cost(cols, width),
        name="spread",
    )(gp, w)


def unpack_kernel(counts, places, b_ref, *rest):
    acc = rest[-1]
    piece = acc.shape[0] // 8
    for (part, at), block in zip(places, spots(b_ref, 8), strict=True):
        value = rest[part][at : at + piece, :].astype(F32)
        acc[pl.ds(pl.multiple_of(block * piece, 8), piece), :] = value
    start = 0
    for out, count in zip(rest[-1 - len(counts) : -1], counts, strict=True):
        out[...] = acc[start : start + count, :]
        start += count


def unpack_call(bid, parts, places, counts):
    total = sum(counts)
    width = parts[0].shape[1]
    vm = pl.BlockSpec(memory_space=pltpu.VMEM)
    return pl.pallas_call(
        functools.partial(unpack_kernel, counts, places),
        out_shape=tuple(jax.ShapeDtypeStruct((n, width), F32) for n in counts),
        in_specs=[pl.BlockSpec(memory_space=pltpu.SMEM)] + [vm] * len(parts),
        out_specs=[vm] * len(counts),
        scratch_shapes=[pltpu.VMEM((total, width), F32)],
        cost_estimate=cost(total, width),
        name="unpack",
    )(bid, *parts)


def tie(x, *needed):
    return lax.optimization_barrier((x,) + needed)[0]


def across(pieces):
    return [swap(piece, "batch", 2 * d) for d, piece in enumerate(pieces, 1)]


def sum_rest(x):
    for level in range(3, lax.axis_size("batch").bit_length() - 1):
        x = (x.astype(F32) + swap(x, "batch", 1 << level).astype(F32)).astype(x.dtype)
    return x


def fold(kept, got):
    piece = kept.shape[0] // 4
    total = kept[:piece].astype(F32)
    for g in got:
        total = total + g[:piece].astype(F32)
    return sum_rest(total.astype(BF))


def quarters(x):
    piece = x.shape[0] // 4
    return [x[d * piece : (d + 1) * piece] for d in range(1, 4)]


def sum_group(x):
    x = x + swap(x, "head", 1)
    return x + swap(x, "head", 2)


def per_device(
    inputs,
    lengths,
    cotangent,
    gain_attn,
    shift_attn,
    weight_qkv,
    bias_qkv,
    weight_proj,
    bias_proj,
    gain_mlp,
    shift_mlp,
    weight_up,
    bias_up,
    weight_down,
    bias_down,
):
    chunk, width = inputs.shape
    group_rows = chunk * lax.axis_size("head")
    heads, triple = weight_qkv.shape[1:]
    cols = heads * triple
    inner = cols // 3
    own = lax.axis_index("head")
    hid = own.astype(jnp.int32).reshape(1)
    bid = (lax.axis_index("batch") % 8).astype(jnp.int32).reshape(1)
    lens = lengths[0]
    live_rows = jnp.sum(lens[:-1])
    places = own * chunk + jnp.arange(chunk, dtype=jnp.int32)
    live = (places < live_rows)[:, None]
    qkv_t = weight_qkv.transpose(1, 2, 0).reshape(cols, width)
    proj = weight_proj.reshape(inner, width)
    zero = jnp.zeros((width,), F32)
    vectors = jnp.stack(
        (gain_attn, shift_attn, bias_proj, gain_mlp, shift_mlp, bias_up, bias_down, zero)
    )

    x_far = swap(inputs, "head", 2)
    x_near = swap(inputs, "head", 1)
    begun = qkv_call(hid, inputs, x_near, vectors, qkv_t, bias_qkv, 0, group_rows, ())
    x_far = tie(x_far, begun[0])
    x_last = swap(x_far, "head", 1)
    queries, keys, values, values_t, hats = qkv_call(
        hid, x_far, x_last, vectors, qkv_t, bias_qkv, 2, group_rows, begun
    )
    grad_own = jnp.where(live, cotangent, jnp.zeros_like(cotangent))
    proj_far = swap(tie(proj, x_far), "head", 2)
    grad_far = swap(tie(grad_own, x_last), "head", 2)

    out_far, out_last, level_far, level_last = attend_call(
        lens, hid, queries, keys, values_t, 2, chunk
    )
    from_last = swap(out_last, "head", 2)
    from_far = swap(out_far, "head", 2)
    out_own, out_mate, level_own, level_mate = attend_call(
        lens, hid, tie(queries, out_far), keys, values_t, 0, chunk
    )
    grads = (grad_own, swap(tie(grad_own, out_far), "head", 1), grad_far, swap(grad_far, "head", 1))
    from_last = swap(tie(from_last, out_own, from_far), "head", 1)
    parts = (out_own, swap(out_mate, "head", 1), from_far, from_last)
    proj_last = swap(tie(proj_far, out_own), "head", 1)
    projs = (proj, swap(tie(proj, out_far), "head", 1), proj_far, proj_last)
    resid, h_own = mix_call(parts, projs, tie(inputs, grad_far), vectors)
    h_far = swap(h_own, "head", 2)
    h_near = swap(h_own, "head", 1)

    near = feed_call(h_own, h_near, grads[0], grads[1], weight_up, vectors, weight_down, 0, group_rows, ())
    h_far = tie(h_far, near[0])
    h_last = swap(h_far, "head", 1)
    act, grad_up, norm_far, norm_last, down_far, down_last = feed_call(
        h_far, h_last, grads[2], grads[3], weight_up, vectors, weight_down, 2, group_rows, near[:2]
    )
    near_swapped = swap(near[3], "head", 1)
    near_down = swap(near[5], "head", 1)
    norm_far = tie(norm_far, near_swapped, near_down)
    far_sum = (norm_far.astype(F32) + swap(norm_last, "head", 1).astype(F32)).astype(BF)
    grad_far_sum = swap(far_sum, "head", 2)
    down_swapped = swap(tie(down_last, far_sum), "head", 1)

    keep_feed, send_feed, grad_bup = weigh_call(
        bid, (h_own, h_near, h_far, h_last), tie(act, far_sum), grad_up, grads
    )
    other_feed = swap(send_feed, "batch", 1)
    grad_resid, grad_att, grad_near, grad_mate, grad_cross, grad_last, sums = turn_call(
        near[2],
        near_swapped,
        tie(grad_far_sum, grad_bup, down_swapped),
        resid,
        grad_own,
        vectors,
        projs,
    )
    got_last = swap(grad_last, "head", 2)
    got = swap(grad_cross, "head", 2)
    grad_mate = swap(grad_mate, "head", 1)
    own_proj, near_sent, cross_proj, far_sent = outer_call(parts, grad_att)
    down_far = tie(down_far, grad_att)
    down_sum = (down_far.astype(F32) + down_swapped.astype(F32)).astype(BF)
    got_last, near_sent, far_sent, down_sum = lax.optimization_barrier(
        (got_last, near_sent, far_sent, down_sum)
    )
    merged_grads = (grad_near, grad_mate, got, swap(got_last, "head", 1))
    grad_near_proj = own_proj + swap(near_sent, "head", 1).astype(F32)
    pair_proj = (cross_proj + swap(far_sent, "head", 1).astype(F32)).astype(BF)
    far_proj = swap(pair_proj, "head", 2)

    kept_feed = (keep_feed.astype(F32) + tie(other_feed, got, got_last).astype(F32)).astype(BF)
    got_feed = across(quarters(kept_feed))
    down_other = swap(tie(down_sum, kept_feed), "head", 2)

    grad_packed = attend_back_call(
        lens,
        hid,
        tie(queries, kept_feed, grad_near_proj),
        keys,
        values,
        merged_grads,
        (out_own, out_mate, out_far, out_last),
        (level_own, level_mate, level_far, level_last),
        chunk,
    )
    got_feed = [tie(g, grad_packed) for g in got_feed]
    grad_wproj = grad_near_proj + tie(far_proj, grad_packed).astype(F32)
    total_feed = fold(kept_feed, got_feed)
    gathered_feed = across([total_feed] * 3)
    keep, send = tally_call(
        bid, tie(grad_packed, total_feed, down_other), hats, qkv_t, vectors, grad_wproj, grad_bup, sums
    )
    other = swap(send, "batch", 1)
    spread = spread_call(tie(grad_packed, keep), qkv_t, chunk)
    gathered_feed, spread = lax.optimization_barrier((gathered_feed, spread))
    e_own, e_near, e_far, e_last = spread

    feed_first = jnp.concatenate((total_feed, gathered_feed[0]), axis=0)
    feed_second = jnp.concatenate(gathered_feed[1:], axis=0)
    feed_got = swap(feed_first, "batch", 1)
    summed = (keep.astype(F32) + tie(other, feed_first, feed_second).astype(F32)).astype(BF)
    kept, small = summed[:-8], summed[-8:]
    pieces = [jnp.concatenate((q, small), axis=0) for q in quarters(kept)]
    e_swapped = swap(tie(e_last, *pieces), "head", 1)
    e_sum = (e_far.astype(F32) + e_swapped.astype(F32)).astype(BF)
    output = resid + near[4].astype(F32) + near_down.astype(F32) + tie(down_other, e_sum).astype(F32)
    output = (output + bias_down).astype(BF)
    got_attn = [tie(g, feed_got, output) for g in across(pieces)]

    tiny = [small.astype(F32)] + [g[-8:].astype(F32) for g in got_attn]
    small = sum_rest((tiny[0] + tiny[1]) + (tiny[2] + tiny[3]))
    total_attn = fold(kept, got_attn)
    gathered_attn = across([total_attn] * 3)
    second_got = swap(tie(feed_second, total_attn), "batch", 1)
    e_other = swap(tie(e_sum, total_attn), "head", 2)
    half = jnp.concatenate([total_attn] + [tie(g, second_got) for g in gathered_attn], axis=0)
    e_mate = swap(tie(e_near, half), "head", 1)
    last = swap(half, "batch", 1)
    biases = small[2:4]
    small = sum_group(tie(small, half))
    e_own = e_own.astype(F32) + e_mate.astype(F32) + tie(e_other, half).astype(F32)

    x_hat, x_rstd = normalize(tie(inputs, half).astype(F32))
    e_own = e_own * gain_attn
    grad_inputs = (
        grad_resid
        + x_rstd
        * (
            e_own
            - jnp.mean(e_own, axis=-1, keepdims=True)
            - x_hat * jnp.mean(e_own * x_hat, axis=-1, keepdims=True)
        )
    ).astype(BF)
    pair = tuple(k * total_feed.shape[0] for k in range(2))
    places = tuple((k, at) for k in range(4) for at in pair)
    parts = (feed_first, feed_second, feed_got, tie(second_got, half))
    sum_wup, sum_wdown = unpack_call(bid, parts, places, (width, width))
    places = tuple((k, at * total_attn.shape[0]) for k in range(2) for at in range(4))
    parts = (half, tie(last, sum_wup, grad_inputs))
    sum_wqkv, sum_wproj = unpack_call(bid, parts, places, (cols, inner))
    return (
        output,
        grad_inputs,
        small[0],
        small[1],
        sum_wqkv.reshape(heads, triple, width).transpose(2, 0, 1),
        biases[0, :cols].reshape(heads, triple),
        sum_wproj.reshape(heads, inner // heads, width),
        small[4],
        small[5],
        small[6],
        sum_wup,
        biases[1],
        sum_wdown,
        small[7],
    )


def solution(mesh):
    rows = P(("batch", "head"), None)
    in_specs = (
        rows,
        P("batch", None),
        rows,
        P(),
        P(),
        P(None, "head", None),
        P("head", None),
        P("head", None, None),
        P(),
        P(),
        P(),
        P(None, "head"),
        P("head"),
        P("head", None),
        P(),
    )
    out_specs = (
        rows,
        rows,
        P(),
        P(),
        P(None, "head", None),
        P("head", None),
        P("head", None, None),
        P(),
        P(),
        P(),
        P(None, "head"),
        P("head"),
        P("head", None),
        P(),
    )
    return jax.shard_map(
        per_device, mesh=mesh, in_specs=in_specs, out_specs=out_specs, check_vma=False
    )
```
